128 devices in a mesh: ctx: 16 (over z, y_lo, core), head: 8 (over x, y_hi).
Axes of the slice: x: 4, y: 4 (y_hi: 2, y_lo: 2; y = y_hi * 2 + y_lo), z: 4, core: 2. Of those that a mesh axis runs over, the one named last changes fastest.
Arguments:
- hidden: bfloat16 [8192, 4096], P('ctx'), may hold values from -6 to 6
- base_ids: int32 [8192], P('ctx'), may hold values from 0 to 4
- norm_gain: float32 [4096], replicated, may hold values from 0.1 to 1.9
- w_gate: bfloat16 [4096, 4096], P(None, 'head'), may hold values from -0.09375 to 0.09375
- w_value: bfloat16 [4096, 4096], P(None, 'head'), may hold values from -0.09375 to 0.09375
- w_bc: bfloat16 [4096, 256], replicated, may hold values from -0.09375 to 0.09375
- w_step: bfloat16 [4096, 64], P(None, 'head'), may hold values from -0.09375 to 0.09375
- conv_value: float32 [4, 4096], P(None, 'head'), may hold values from -3 to 3
- conv_bc: float32 [4, 256], replicated, may hold values from -3 to 3
- step_bias: float32 [64], P('head'), may hold values from -5.5 to -3.5
- decay_rate: float32 [64], P('head'), as said below
- skip_gain: float32 [64], P('head'), may hold values from 0.5 to 1.5
- out_gain: float32 [4096], P('head'), may hold values from 0.1 to 1.9
- w_out: bfloat16 [4096, 4096], P('head'), may hold values from -0.09375 to 0.09375
Outputs:
- mixed_out: bfloat16 [8192, 4096], P('ctx', 'head')
The draws below stay inside these ranges and needn't reach their ends.
Inputs may be any that keep to these rules, and one draw needn't show every extreme that they name: `base_ids`: 4 marks an unknown base N, 0 to 3 are A, C, G, T. `decay_rate`: positive rates.
All inputs are finite; a program needn't handle non-finite values.
Results may differ from the reference program's by a relative error of at most 0.0059.
Values may be sent and summed in bfloat16 or wider, within the bound.
No kernel may reach another device: no remote copies, remote signals or barrier semaphores. Data moves between devices by JAX's collectives and lax.ppermute only.
A program may use at most 192 MiB of HBM per device.

```python
import jax
import jax.numpy as jnp
from jax import lax

D = 4096
HEADS = 64
HEAD_DIM = 64
STATE = 128
CONV_WIDTH = 4
BLOCK = 256
INNER = 4096
TOKENS = 8192


def draw_decay_rate(key, part):
    uniform_draw = jax.random.uniform(key, (HEADS,), jnp.float32)
    lowest = jnp.log(1.0 / TOKENS)
    highest = jnp.log(8.0)
    return jnp.exp(lowest + uniform_draw * (highest - lowest)).astype(jnp.float32)


def plant(array, own_key, smallest, high):
    dims = array.shape
    index_at = [jax.random.randint(jax.random.fold_in(own_key, axis), (), 0, dims[axis]) for axis in range(len(dims))]
    array = array.at[tuple(index_at)].set(smallest)
    longest = dims.index(max(dims))
    index_at[longest] = (index_at[longest] + 1) % dims[longest]
    return array.at[tuple(index_at)].set(high)


def levels(key, dims, cuts, smallest, largest):
    factor_of = 1.0
    for dim, shards_of in cuts:
        heights = jax.random.uniform(jax.random.fold_in(jax.random.fold_in(key, 6), dim), (shards_of,), jnp.float32, smallest / len(cuts), largest / len(cuts))
        factor_of = factor_of * jnp.repeat(jnp.exp(heights), dims[dim] // shards_of).reshape((-1,) + (1,) * (len(dims) - 1 - dim))
    return factor_of


def normal_values(rng, extent, spread, limit, cuts=(), held_as=jnp.bfloat16):
    loudness = levels(rng, extent, cuts, -0.22, 0.18) if cuts else 1.0
    drawn = jax.random.normal(rng, extent, jnp.float32) * spread * loudness
    return jnp.minimum(jnp.maximum(drawn, -limit), limit).astype(held_as)


def setup_inputs(seed: int = 0) -> dict:
    key_list = jax.random.split(jax.random.key(seed), 15)
    hidden = normal_values(key_list[0], (TOKENS, D), 1.0, 6.0, ((0, 16),))
    base_ids = plant(jax.random.randint(key_list[1], (TOKENS,), 0, 5), jax.random.fold_in(key_list[1], 1), 0, 4).astype(jnp.int32)
    norm_gain = jnp.clip(1.0 + 0.18 * jax.random.normal(key_list[2], (D,), jnp.float32), 0.1, 1.9)
    w_gate = normal_values(key_list[3], (D, INNER), D ** -0.5, 0.09375, ((1, 8),))
    w_value = normal_values(key_list[4], (D, INNER), D ** -0.5, 0.09375, ((1, 8),))
    w_bc = normal_values(key_list[5], (D, 2 * STATE), D ** -0.5, 0.09375)
    w_step = normal_values(key_list[6], (D, HEADS), D ** -0.5, 0.09375, ((1, 8),))
    conv_value = normal_values(key_list[7], (CONV_WIDTH, INNER), CONV_WIDTH ** -0.5, 3.0, ((1, 8),), jnp.float32)
    conv_bc = normal_values(key_list[8], (CONV_WIDTH, 2 * STATE), CONV_WIDTH ** -0.5, 3.0, (), jnp.float32)
    step_bias = jnp.clip(-5.5 + 2.0 * jax.random.uniform(key_list[9], (HEADS,), jnp.float32) ** levels(key_list[9], (HEADS,), ((0, 8),), -0.2, 0.2), -5.5, -3.5)
    decay_rate = draw_decay_rate(jax.random.fold_in(key_list[14], 71), 0)
    skip_gain = jnp.clip(0.5 + 1.0 * jax.random.uniform(key_list[11], (HEADS,), jnp.float32) ** levels(key_list[11], (HEADS,), ((0, 8),), -0.2, 0.2), 0.5, 1.5)
    out_gain = jnp.clip(1.0 + 0.18 * jax.random.normal(key_list[12], (INNER,), jnp.float32), 0.1, 1.9)
    w_out = normal_values(key_list[13], (INNER, D), INNER ** -0.5, 0.09375, ((0, 8),))
    return {"hidden": hidden, "base_ids": base_ids, "norm_gain": norm_gain, "w_gate": w_gate, "w_value": w_value, "w_bc": w_bc, "w_step": w_step, "conv_value": conv_value, "conv_bc": conv_bc, "step_bias": step_bias, "decay_rate": decay_rate, "skip_gain": skip_gain, "out_gain": out_gain, "w_out": w_out}


EPSILON = 1e-05
PRECISE = lax.Precision.HIGHEST

def convolve(padded, kernel, kernel_len):
    length = padded.shape[0] - 2 * (kernel_len - 1)
    reach = 2 * (kernel_len - 1)
    forward_sum = kernel[0] * padded[0:length]
    backward_sum = kernel[0] * padded[reach:reach + length]
    for offset in range(1, kernel_len):
        forward_sum = forward_sum + kernel[offset] * padded[offset:offset + length]
        backward_sum = backward_sum + kernel[offset] * padded[reach - offset:reach - offset + length]
    return (forward_sum, backward_sum)

def scan_blocks(values, inputs_b, inputs_c, steps, log_decay):
    block_total = TOKENS // BLOCK

    def blocked(source_array):
        return source_array.reshape((block_total, BLOCK) + source_array.shape[1:])
    causal = jnp.arange(BLOCK)[:, None] >= jnp.arange(BLOCK)[None, :]

    def advance(state_carry, block_item):
        value_rows, b_rows, c_rows, step_rows, decay_rows = block_item
        cumulative = jnp.cumsum(decay_rows, axis=0)
        scores = jnp.dot(c_rows, b_rows.T, precision=PRECISE)
        gaps = cumulative[:, None, :] - cumulative[None, :, :]
        weights = jnp.exp(jnp.where(causal[:, :, None], gaps, -jnp.inf)) * scores[:, :, None] * step_rows[None, :, :]
        within = jnp.einsum('tsh,shp->thp', weights, value_rows, precision=PRECISE)
        across = jnp.exp(cumulative)[:, :, None] * jnp.einsum('tn,hpn->thp', c_rows, state_carry, precision=PRECISE)
        tail_weight = jnp.exp(cumulative[-1:] - cumulative) * step_rows
        new_state = jnp.exp(cumulative[-1])[:, None, None] * state_carry + jnp.einsum('sh,sn,shp->hpn', tail_weight, b_rows, value_rows, precision=PRECISE)
        return (new_state, within + across)
    start_state = jnp.zeros((HEADS, HEAD_DIM, STATE), jnp.float32)
    final_state, outputs = lax.scan(advance, start_state, (blocked(values), blocked(inputs_b), blocked(inputs_c), blocked(steps), blocked(log_decay)))
    return outputs.reshape(TOKENS, HEADS, HEAD_DIM)

def mixer(hidden_rows, keep_mask, norm_gain, w_gate, w_value, w_bc, w_step, conv_value, conv_bc, step_bias, decay_rate, skip_gain, out_gain, w_out):
    inv_rms = lax.rsqrt(lax.optimization_barrier(jnp.mean(jnp.square(hidden_rows.astype(jnp.float32)), axis=-1)) + EPSILON)
    scaled = (hidden_rows * norm_gain).astype(jnp.bfloat16)

    def project(weight):
        return jnp.dot(scaled, weight, preferred_element_type=jnp.float32) * inv_rms[:, None]
    gate_in = project(w_gate)
    value_in = project(w_value)
    bc_in = project(w_bc)
    step_in = project(w_step)
    mixed_in = jnp.concatenate([value_in, bc_in], axis=-1)
    kernel = jnp.concatenate([conv_value, conv_bc], axis=-1)
    padded = jnp.pad(mixed_in, ((CONV_WIDTH - 1, CONV_WIDTH - 1), (0, 0)))
    forward_mix, backward_mix = convolve(padded, kernel, CONV_WIDTH)
    forward_mix = jax.nn.silu(forward_mix)
    backward_mix = jax.nn.silu(backward_mix)
    steps = jax.nn.softplus(step_in + step_bias)
    log_decay = -decay_rate * steps

    def split_lane(mixed_lane):
        values = (mixed_lane[:, :INNER] * keep_mask[:, None]).reshape(TOKENS, HEADS, HEAD_DIM)
        return (values, mixed_lane[:, INNER:INNER + STATE], mixed_lane[:, INNER + STATE:])
    fwd_values, fwd_b, fwd_c = split_lane(forward_mix)
    bwd_values, bwd_b, bwd_c = split_lane(backward_mix)
    forward_out = scan_blocks(fwd_values, fwd_b, fwd_c, steps, log_decay) + skip_gain[:, None] * fwd_values
    backward_out = scan_blocks(bwd_values[::-1], bwd_b[::-1], bwd_c[::-1], steps[::-1], log_decay[::-1])[::-1] + skip_gain[:, None] * bwd_values
    summed = forward_out + backward_out
    gated = summed * jax.nn.silu(gate_in).reshape(TOKENS, HEADS, HEAD_DIM)
    normed = (gated * lax.rsqrt(lax.optimization_barrier(jnp.mean(jnp.square(gated), axis=-1, keepdims=True)) + EPSILON) * out_gain.reshape(HEADS, HEAD_DIM)).astype(jnp.bfloat16)
    return jnp.dot(normed.reshape(TOKENS, INNER), w_out, preferred_element_type=jnp.float32)

def reference(hidden, base_ids, norm_gain, w_gate, w_value, w_bc, w_step, conv_value, conv_bc, step_bias, decay_rate, skip_gain, out_gain, w_out):
    keep_mask = (base_ids != 4).astype(jnp.float32)
    weights = (norm_gain, w_gate, w_value, w_bc, w_step, conv_value, conv_bc, step_bias, decay_rate, skip_gain, out_gain, w_out)
    branch_own = mixer(hidden, keep_mask, *weights)
    branch_other = mixer(hidden[::-1, ::-1], keep_mask[::-1], *weights)
    return (branch_own + branch_other[::-1, ::-1]).astype(jnp.bfloat16)
```

```python
import functools

import jax
import jax.numpy as jnp
from jax import lax
from jax.experimental import pallas as pl
from jax.experimental.pallas import tpu as pltpu
from jax.sharding import PartitionSpec as P

EPSILON = 1e-05
HALO = 8
CHUNK = 128
TILE = 128
FLIP = 256
ROWS = 64
BF16 = jnp.bfloat16
F32 = jnp.float32
NT = (((1,), (1,)), ((), ()))
TN = (((0,), (0,)), ((), ()))


def params(megabytes, dims=1):
    return pltpu.CompilerParams(
        dimension_semantics=("arbitrary",) * dims, vmem_limit_bytes=megabytes << 20
    )


def iota(shape, dim):
    return lax.broadcasted_iota(jnp.int32, shape, dim)


def dot(a, b):
    return jnp.dot(a, b, preferred_element_type=F32)


def reversal(width):
    where = iota((width, width), 0) + iota((width, width), 1) == width - 1
    return jnp.where(where, 1.0, 0.0).astype(BF16)


def spreader(heads, width):
    shape = (heads, heads * width)
    return jnp.where(iota(shape, 1) // width == iota(shape, 0), 1.0, 0.0).astype(BF16)


def spread(columns, matrix):
    high = columns.astype(BF16)
    low = (columns - high.astype(F32)).astype(BF16)
    return dot(high, matrix) + dot(low, matrix)


def silu(x):
    return x / (1.0 + jnp.exp(-x))


def scale_rows(source, begin, gain, xs, squares):
    depth = source.shape[1]
    step = min(source.shape[0], TILE)
    for r in range(0, source.shape[0], step):
        x = source[r : r + step, :].astype(F32)
        xs[begin + r : begin + r + step, :] = (x * gain).astype(BF16)
        square = x * x
        partial = square[:, :TILE]
        for c in range(TILE, depth, TILE):
            partial = partial + square[:, c : c + TILE]
        squares[begin + r : begin + r + step, :] += partial


def scale_mirrored(source, begin, gain, xs):
    size, depth = source.shape
    flip = reversal(FLIP)
    for i in range(depth // FLIP):
        at = depth - (i + 1) * FLIP
        lanes = slice(i * FLIP, (i + 1) * FLIP)
        x = dot(source[:, at : at + FLIP], flip)
        xs[begin : begin + size, lanes] = (x * gain[:, lanes]).astype(BF16)


def multiply(xs, accs, weights, splits):
    part = xs.shape[0] // splits

    def body(i, carry):
        at = pl.ds(pl.multiple_of(i * part, 16), part)
        x = xs[at, :]
        for acc, weight in zip(accs, weights):
            if weight.shape[1] == x.shape[1]:
                acc[at, :] += lax.dot_general(x, weight[...], NT, preferred_element_type=F32)
            else:
                acc[at, :] += dot(x, weight[...])
        return carry

    lax.fori_loop(0, splits, body, 0)


def finish_rms(squares, width):
    mean = jnp.sum(squares[...], axis=1, keepdims=True) * (1.0 / width)
    squares[...] = jnp.broadcast_to(lax.rsqrt(mean + EPSILON), squares.shape)


def mix_kernel(
    hid_ref, mir_ref, halo_ref, halo_mir_ref, gain_ref, wv_ref, wbc_ref, wst_ref,
    mix_ref, step_ref, acc_v, acc_b, acc_s, xs, squares,
):
    k = pl.program_id(0)
    tokens, depth = hid_ref.shape
    rows = tokens + 2 * HALO
    inner = wv_ref.shape[1]

    @pl.when(k == 0)
    def _():
        for acc in (acc_v, acc_b, acc_s, squares):
            acc[...] = jnp.zeros_like(acc)

    gain = gain_ref[...]
    scale_rows(hid_ref, 0, gain, xs, squares)
    scale_rows(halo_ref, tokens, gain, xs, squares)
    scale_mirrored(mir_ref, rows, gain, xs)
    scale_mirrored(halo_mir_ref, rows + tokens, gain, xs)
    multiply(xs, (acc_v, acc_b, acc_s), (wv_ref, wbc_ref, wst_ref), 3)

    @pl.when(k == pl.num_programs(0) - 1)
    def _():
        finish_rms(squares, depth * pl.num_programs(0))
        spans = [(r, r + HALO, TILE) for r in range(0, tokens, TILE)]
        for b in range(2):
            for r, out, size in spans:
                here = slice(b * rows + r, b * rows + r + size)
                step_ref[b, r : r + size, :] = (
                    acc_s[here, :] * squares[r : r + size, : step_ref.shape[2]]
                )
            for r, out, size in spans + [(tokens, 0, HALO), (tokens + HALO, tokens + HALO, HALO)]:
                here = slice(b * rows + r, b * rows + r + size)
                scale = squares[r : r + size, :]
                for c in range(0, inner, TILE):
                    mix_ref[b, out : out + size, c : c + TILE] = acc_v[here, c : c + TILE] * scale
                for c in range(0, acc_b.shape[1], TILE):
                    mix_ref[b, out : out + size, inner + c : inner + c + TILE] = (
                        acc_b[here, c : c + TILE] * scale
                    )


def gate_kernel(hid_ref, mir_ref, gain_ref, wg_ref, gate_ref, acc_g, xs, squares):
    k = pl.program_id(0)
    tokens, depth = hid_ref.shape

    @pl.when(k == 0)
    def _():
        for acc in (acc_g, squares):
            acc[...] = jnp.zeros_like(acc)

    gain = gain_ref[...]
    scale_rows(hid_ref, 0, gain, xs, squares)
    scale_mirrored(mir_ref, tokens, gain, xs)
    multiply(xs, (acc_g,), (wg_ref,), 2)

    @pl.when(k == pl.num_programs(0) - 1)
    def _():
        finish_rms(squares, depth * pl.num_programs(0))
        for b in range(2):
            for r in range(0, tokens, TILE):
                scale = squares[r : r + TILE, :]
                for c in range(0, wg_ref.shape[1], TILE):
                    gate_ref[b, r : r + TILE, c : c + TILE] = silu(
                        acc_g[b * tokens + r : b * tokens + r + TILE, c : c + TILE] * scale
                    )


DEPTH = 1024


def project_mix(hidden, halo, norm_gain, w_value, w_bc, w_step):
    tokens, width = hidden.shape
    count = width // DEPTH
    inner, maps, heads = w_value.shape[1], w_bc.shape[1], w_step.shape[1]
    rows = tokens + 2 * HALO
    ahead = lambda k: (0, k)
    back = lambda k: (0, count - 1 - k)
    down = lambda k: (k, 0)
    whole = lambda k: (0, 0, 0)
    return pl.pallas_call(
        mix_kernel,
        grid=(count,),
        in_specs=[
            pl.BlockSpec((tokens, DEPTH), ahead),
            pl.BlockSpec((tokens, DEPTH), back),
            pl.BlockSpec((2 * HALO, DEPTH), ahead),
            pl.BlockSpec((2 * HALO, DEPTH), back),
            pl.BlockSpec((1, DEPTH), ahead),
            pl.BlockSpec((DEPTH, inner), down),
            pl.BlockSpec((DEPTH, maps), down),
            pl.BlockSpec((heads, DEPTH), ahead),
        ],
        out_specs=[
            pl.BlockSpec((2, rows, inner + maps), whole),
            pl.BlockSpec((2, tokens, heads), whole),
        ],
        out_shape=[
            jax.ShapeDtypeStruct((2, rows, inner + maps), F32),
            jax.ShapeDtypeStruct((2, tokens, heads), F32),
        ],
        scratch_shapes=[
            pltpu.VMEM((2 * rows, inner), F32),
            pltpu.VMEM((2 * rows, maps), F32),
            pltpu.VMEM((2 * rows, heads), F32),
            pltpu.VMEM((2 * rows, DEPTH), BF16),
            pltpu.VMEM((rows, TILE), F32),
        ],
        compiler_params=params(40),
        cost_estimate=pl.CostEstimate(
            flops=4 * rows * width * (inner + maps + FLIP), transcendentals=0, bytes_accessed=20 << 20
        ),
        name="project_mix",
    )(hidden, hidden, halo, halo, norm_gain[None], w_value, w_bc, w_step.T)


def project_gate(hidden, norm_gain, w_gate):
    tokens, width = hidden.shape
    count = width // DEPTH
    inner = w_gate.shape[1]
    ahead = lambda k: (0, k)
    back = lambda k: (0, count - 1 - k)
    return pl.pallas_call(
        gate_kernel,
        grid=(count,),
        in_specs=[
            pl.BlockSpec((tokens, DEPTH), ahead),
            pl.BlockSpec((tokens, DEPTH), back),
            pl.BlockSpec((1, DEPTH), ahead),
            pl.BlockSpec((DEPTH, inner), lambda k: (k, 0)),
        ],
        out_specs=pl.BlockSpec((2, tokens, inner), lambda k: (0, 0, 0)),
        out_shape=jax.ShapeDtypeStruct((2, tokens, inner), F32),
        scratch_shapes=[
            pltpu.VMEM((2 * tokens, inner), F32),
            pltpu.VMEM((2 * tokens, DEPTH), BF16),
            pltpu.VMEM((tokens, TILE), F32),
        ],
        compiler_params=params(32),
        cost_estimate=pl.CostEstimate(
            flops=4 * tokens * width * (inner + FLIP),
            transcendentals=2 * tokens * inner,
            bytes_accessed=14 << 20,
        ),
        name="project_gate",
    )(hidden, hidden, norm_gain[None], w_gate)


def conv_kernel(
    mix_ref, step_ref, keep_ref, taps_ref, bias_ref, rate_ref, skip_ref,
    direct_ref, xf_ref, xb_ref, maps_ref, cols_ref, rows_ref, prefix_ref, enter_ref, final_ref,
    dt_sc, wf_sc, wb_sc, vf_sc, vb_sc,
):
    tokens, heads = step_ref.shape[1:]
    inner = direct_ref.shape[2]
    width = inner // heads
    state = maps_ref.shape[3]
    chunks = tokens // CHUNK
    matrix = spreader(heads, width)

    raw = step_ref[0] + bias_ref[...]
    dt = jnp.maximum(raw, 0.0) + jnp.log1p(jnp.exp(-jnp.abs(raw)))
    log_decay = -rate_ref[...] * dt
    square = (CHUNK, CHUNK)
    lower = jnp.where(iota(square, 0) >= iota(square, 1), 1.0, 0.0)
    upper = jnp.where(iota(square, 0) <= iota(square, 1), 1.0, 0.0)
    eye = jnp.where(iota(square, 0) == iota(square, 1), 1.0, 0.0)
    dt_sc[...] = spread(dt, matrix)
    totals = []
    for c in range(chunks):
        at = slice(c * CHUNK, (c + 1) * CHUNK)
        part = log_decay[at]
        inclusive = jnp.dot(lower, part, precision=lax.Precision.HIGHEST, preferred_element_type=F32)
        exclusive = inclusive - part
        last = inclusive[CHUNK - 1 : CHUNK]
        totals.append(last)
        cols_ref[0, 0, at] = inclusive
        cols_ref[0, 1, at] = exclusive
        cols_ref[0, 2, at] = jnp.exp(inclusive)
        cols_ref[0, 3, at] = jnp.exp(last - exclusive)
        for i, array in ((0, inclusive), (1, exclusive)):
            rows_ref[0, i, :, at] = lax.dot_general(
                array, eye, TN, precision=lax.Precision.HIGHEST, preferred_element_type=F32
            )
        wf_sc[at] = spread(jnp.exp(last - inclusive), matrix)
        wb_sc[at] = spread(jnp.exp(exclusive), matrix)
    zero = jnp.zeros_like(totals[0])
    before, after = [zero], [zero]
    for c in range(chunks - 1):
        before.append(before[-1] + totals[c])
        after.append(after[-1] + totals[chunks - 1 - c])
    after = after[::-1]
    everything = before[-1] + totals[-1]
    stack = jnp.concatenate(before + after + totals + [everything] * 4, axis=0)
    spread_rows = spread(jnp.exp(stack), matrix)
    prefix_ref[0] = spread_rows
    lane_totals = jnp.dot(
        jnp.broadcast_to(everything, (8, heads)),
        matrix.astype(F32),
        precision=lax.Precision.HIGHEST,
        preferred_element_type=F32,
    )

    half = CONV - 1

    def block(i, carry):
        r = pl.multiple_of(i * ROWS, ROWS)
        keep = keep_ref[pl.ds(r, ROWS), :]
        here = pl.ds(r, ROWS)
        for c in range(0, inner + 2 * state, TILE):
            lanes = slice(c, c + TILE)
            window = mix_ref[0, pl.ds(r, ROWS + 2 * HALO), lanes]
            moved = [window[HALO + j : HALO + j + ROWS] for j in range(-half, half + 1)]
            forward = taps_ref[0:1, lanes] * moved[0]
            backward = taps_ref[0:1, lanes] * moved[2 * half]
            for o in range(1, CONV):
                forward = forward + taps_ref[o : o + 1, lanes] * moved[o]
                backward = backward + taps_ref[o : o + 1, lanes] * moved[2 * half - o]
            forward = silu(forward)
            backward = silu(backward)
            if c < inner:
                forward = forward * keep
                backward = backward * keep
                direct_ref[0, here, lanes] = skip_ref[:, lanes] * (forward + backward)
                dt_lanes = dt_sc[here, lanes]
                forward = forward * dt_lanes
                backward = backward * dt_lanes
                xf_ref[0, here, lanes] = forward.astype(BF16)
                xb_ref[0, here, lanes] = backward.astype(BF16)
                vf_sc[here, lanes] = (forward * wf_sc[here, lanes]).astype(BF16)
                vb_sc[here, lanes] = (backward * wb_sc[here, lanes]).astype(BF16)
            else:
                which = (c - inner) // TILE
                maps_ref[0, which, here, :] = forward.astype(BF16)
                maps_ref[0, 2 + which, here, :] = backward.astype(BF16)
        return carry

    lax.fori_loop(0, tokens // ROWS, block, 0)

    for direction, moved, order in ((0, vf_sc, range(chunks)), (1, vb_sc, range(chunks - 1, -1, -1))):
        for j in range(0, inner, TILE):
            lanes = slice(j, j + TILE)
            carry = jnp.zeros((state, TILE), F32)
            for c in order:
                at = slice(c * CHUNK, (c + 1) * CHUNK)
                enter_ref[0, direction, c, :, lanes] = carry.astype(BF16)
                gained = lax.dot_general(
                    maps_ref[0, 2 * direction, at, :], moved[at, lanes], TN, preferred_element_type=F32
                )
                carry = carry * prefix_ref[0, 2 * chunks + c : 2 * chunks + c + 1, lanes] + gained
            final_ref[direction, 0, j // TILE, :state] = carry
            final_ref[direction, 0, j // TILE, state:] = lane_totals[:, lanes]


CONV = 4


def convolve(mix, steps, keep, taps, step_bias, decay_rate, skip):
    rows, channels = mix.shape[1:]
    tokens, heads = steps.shape[1:]
    inner = skip.shape[1]
    state = (channels - inner) // 2
    chunks = tokens // CHUNK
    one = lambda b: (b, 0, 0)
    flat = lambda b: (0, 0)
    four = lambda b: (b, 0, 0, 0)
    five = lambda b: (b, 0, 0, 0, 0)
    return pl.pallas_call(
        conv_kernel,
        grid=(2,),
        in_specs=[
            pl.BlockSpec((1, rows, channels), one),
            pl.BlockSpec((1, tokens, heads), one),
            pl.BlockSpec((tokens, 1), flat),
            pl.BlockSpec((CONV, channels), flat),
            pl.BlockSpec((1, heads), flat),
            pl.BlockSpec((1, heads), flat),
            pl.BlockSpec((1, inner), flat),
        ],
        out_specs=[
            pl.BlockSpec((1, tokens, inner), one),
            pl.BlockSpec((1, tokens, inner), one),
            pl.BlockSpec((1, tokens, inner), one),
            pl.BlockSpec((1, 4, tokens, state), four),
            pl.BlockSpec((1, 4, tokens, heads), four),
            pl.BlockSpec((1, 2, heads, tokens), four),
            pl.BlockSpec((1, 4 * chunks, inner), one),
            pl.BlockSpec((1, 2, chunks, state, inner), five),
            pl.BlockSpec((2, 1, inner // TILE, state + 8, TILE), lambda b: (0, b, 0, 0, 0)),
        ],
        out_shape=[
            jax.ShapeDtypeStruct((2, tokens, inner), F32),
            jax.ShapeDtypeStruct((2, tokens, inner), BF16),
            jax.ShapeDtypeStruct((2, tokens, inner), BF16),
            jax.ShapeDtypeStruct((2, 4, tokens, state), BF16),
            jax.ShapeDtypeStruct((2, 4, tokens, heads), F32),
            jax.ShapeDtypeStruct((2, 2, heads, tokens), F32),
            jax.ShapeDtypeStruct((2, 4 * chunks, inner), F32),
            jax.ShapeDtypeStruct((2, 2, chunks, state, inner), BF16),
            jax.ShapeDtypeStruct((2, 2, inner // TILE, state + 8, TILE), F32),
        ],
        scratch_shapes=[
            pltpu.VMEM((tokens, inner), F32),
            pltpu.VMEM((tokens, inner), F32),
            pltpu.VMEM((tokens, inner), F32),
            pltpu.VMEM((tokens, inner), BF16),
            pltpu.VMEM((tokens, inner), BF16),
        ],
        compiler_params=params(40),
        cost_estimate=pl.CostEstimate(flops=1 << 30, transcendentals=1 << 22, bytes_accessed=20 << 20),
        name="convolve",
    )(mix, steps, keep, taps, step_bias[None], decay_rate[None], skip)


def within_kernel(
    direct_ref, xf_ref, xb_ref, maps_ref, cols_ref, rows_ref, wout_ref, local_ref, mirror_ref,
):
    heads = cols_ref.shape[3]
    inner = direct_ref.shape[2]
    width = inner // heads
    square = (CHUNK, CHUNK)
    below = iota(square, 0) >= iota(square, 1)
    above = iota(square, 0) <= iota(square, 1)
    scores_f = lax.dot_general(maps_ref[0, 1], maps_ref[0, 0], NT, preferred_element_type=F32)
    scores_b = lax.dot_general(maps_ref[0, 3], maps_ref[0, 2], NT, preferred_element_type=F32)
    scores_f = jnp.where(below, scores_f, 0.0)
    scores_b = jnp.where(above, scores_b, 0.0)
    left = iota((CHUNK, TILE), 1) < width
    for j in range(0, inner, TILE):
        lanes = slice(j, j + TILE)
        values = jnp.concatenate([xf_ref[0, :, lanes], xb_ref[0, :, lanes]], axis=0)
        parts = []
        for h in range(j // width, (j + TILE) // width):
            gap = jnp.where(
                below,
                cols_ref[0, 0, :, h : h + 1] - rows_ref[0, 0, h : h + 1, :],
                rows_ref[0, 1, h : h + 1, :] - cols_ref[0, 1, :, h : h + 1],
            )
            decay = jnp.exp(gap)
            weights = jnp.concatenate(
                [(decay * scores_f).astype(BF16), (decay * scores_b).astype(BF16)], axis=1
            )
            parts.append(dot(weights, values))
        local_ref[0, :, lanes] = direct_ref[0, :, lanes] + jnp.where(left, parts[0], parts[1])
    flip = reversal(FLIP)
    blocks = wout_ref.shape[1] // FLIP
    for i in range(blocks):
        at = (blocks - 1 - i) * FLIP
        mirror_ref[:, i * FLIP : (i + 1) * FLIP] = dot(wout_ref[:, at : at + FLIP], flip).astype(BF16)


def within(direct, xf, xb, maps, cols, rows, w_out):
    tokens, inner = direct.shape[1:]
    state = maps.shape[3]
    heads = cols.shape[3]
    chunks = tokens // CHUNK
    count = 2 * chunks
    slab = w_out.shape[1] // count
    token = lambda i: (i // chunks, i % chunks, 0)
    inside = lambda i: (i // chunks, 0, i % chunks, 0)
    return pl.pallas_call(
        within_kernel,
        grid=(count,),
        in_specs=[
            pl.BlockSpec((1, CHUNK, inner), token),
            pl.BlockSpec((1, CHUNK, inner), token),
            pl.BlockSpec((1, CHUNK, inner), token),
            pl.BlockSpec((1, 4, CHUNK, state), inside),
            pl.BlockSpec((1, 4, CHUNK, heads), inside),
            pl.BlockSpec((1, 2, heads, CHUNK), lambda i: (i // chunks, 0, 0, i % chunks)),
            pl.BlockSpec((inner, slab), lambda i: (0, count - 1 - i)),
        ],
        out_specs=[
            pl.BlockSpec((1, CHUNK, inner), token),
            pl.BlockSpec((inner, slab), lambda i: (0, i)),
        ],
        out_shape=[
            jax.ShapeDtypeStruct((2, tokens, inner), F32),
            jax.ShapeDtypeStruct(w_out.shape, BF16),
        ],
        compiler_params=params(32),
        cost_estimate=pl.CostEstimate(flops=4 << 30, transcendentals=1 << 22, bytes_accessed=24 << 20),
        name="within",
    )(direct, xf, xb, maps, cols, rows, w_out)


def chain_kernel(states_ref, incoming_ref):
    count = states_ref.shape[0]
    state = incoming_ref.shape[1]
    backward = lax.axis_index("ctx") >= count // 2
    carry = jnp.zeros(incoming_ref.shape[1:], F32)
    for n in range(count):
        at = jnp.where(backward, count - 1 - n, n)
        incoming_ref[at] = carry.astype(incoming_ref.dtype)
        carry = carry * jnp.exp(states_ref[at, state : state + 1, :]) + states_ref[at, :state, :]


def chain(states):
    count, rows, tile = states.shape
    return pl.pallas_call(
        chain_kernel,
        out_shape=jax.ShapeDtypeStruct((count, rows - 8, tile), BF16),
        compiler_params=pltpu.CompilerParams(vmem_limit_bytes=16 << 20),
        cost_estimate=pl.CostEstimate(flops=1 << 20, transcendentals=0, bytes_accessed=2 << 20),
        name="chain",
    )(states)


def output_kernel(
    local_ref, silu_ref, maps_ref, cols_ref, prefix_ref, enter_ref, incoming_ref, gain_ref,
    wout_ref, mirror_ref, out_ref, normed,
):
    i = pl.program_id(0)
    chunks = normed.shape[1] // CHUNK
    heads = cols_ref.shape[3]
    inner = local_ref.shape[2]
    width = inner // heads

    @pl.when(i < 2 * chunks)
    def _():
        chunk = i % chunks
        branch = i // chunks
        matrix = spreader(heads, width)
        scale_f = spread(cols_ref[0, 2], matrix)
        scale_b = spread(cols_ref[0, 3], matrix)
        shape = (FLIP, FLIP)
        group = jnp.where(iota(shape, 0) // width == iota(shape, 1) // width, 1.0, 0.0).astype(BF16)
        ahead = prefix_ref[0, pl.ds(chunk, 1), :]
        behind = prefix_ref[0, pl.ds(chunks + chunk, 1), :]
        for j in range(0, inner, FLIP):
            lanes = slice(j, j + FLIP)
            tiles = range(j // TILE, (j + FLIP) // TILE)
            into_f = jnp.concatenate([incoming_ref[0, 0, t].astype(F32) for t in tiles], axis=1)
            into_b = jnp.concatenate([incoming_ref[1, 0, t].astype(F32) for t in tiles], axis=1)
            into_f = enter_ref[0, 0, 0, :, lanes].astype(F32) + ahead[:, lanes] * into_f
            into_b = enter_ref[0, 1, 0, :, lanes].astype(F32) + behind[:, lanes] * into_b
            y = local_ref[0, :, lanes]
            y = y + scale_f[:, lanes] * dot(maps_ref[0, 1], into_f.astype(BF16))
            y = y + scale_b[:, lanes] * dot(maps_ref[0, 3], into_b.astype(BF16))
            y = y * silu_ref[0, :, lanes]
            square = y * y
            high = square.astype(BF16)
            low = (square - high.astype(F32)).astype(BF16)
            mean = (dot(high, group) + dot(low, group)) * (1.0 / width)
            y = y * lax.rsqrt(mean + EPSILON) * gain_ref[:, lanes]
            at = pl.ds(pl.multiple_of(chunk * CHUNK, CHUNK), CHUNK)
            normed[branch, at, lanes] = y.astype(BF16)

    @pl.when(i >= 2 * chunks)
    def _():
        out_ref[0] = (dot(normed[0], wout_ref[...]) + dot(normed[1], mirror_ref[...])).astype(
            out_ref.dtype
        )


def output(local, gate, maps, cols, prefix, enter, incoming, gain, w_out, mirror, parts):
    tokens, inner = local.shape[1:]
    state = maps.shape[3]
    heads = cols.shape[3]
    chunks = tokens // CHUNK
    pre = 2 * chunks
    slab = w_out.shape[1] // parts
    held = lambda i: jnp.minimum(i, pre - 1)
    token = lambda i: (held(i) // chunks, held(i) % chunks, 0)
    inside = lambda i: (held(i) // chunks, 0, held(i) % chunks, 0)
    column = lambda i: (0, jnp.maximum(i - pre, 0))
    return pl.pallas_call(
        output_kernel,
        grid=(pre + parts,),
        in_specs=[
            pl.BlockSpec((1, CHUNK, inner), token),
            pl.BlockSpec((1, CHUNK, inner), token),
            pl.BlockSpec((1, 4, CHUNK, state), inside),
            pl.BlockSpec((1, 4, CHUNK, heads), inside),
            pl.BlockSpec((1, 4 * chunks, inner), lambda i: (held(i) // chunks, 0, 0)),
            pl.BlockSpec(
                (1, 2, 1, state, inner), lambda i: (held(i) // chunks, 0, held(i) % chunks, 0, 0)
            ),
            pl.BlockSpec(
                (2, 1, inner // TILE, state, TILE), lambda i: (0, held(i) // chunks, 0, 0, 0)
            ),
            pl.BlockSpec((1, inner), lambda i: (0, 0)),
            pl.BlockSpec((inner, slab), column),
            pl.BlockSpec((inner, slab), column),
        ],
        out_specs=pl.BlockSpec((1, tokens, slab), lambda i: (jnp.maximum(i - pre, 0), 0, 0)),
        out_shape=jax.ShapeDtypeStruct((parts, tokens, slab), BF16),
        scratch_shapes=[pltpu.VMEM((2, tokens, inner), BF16)],
        compiler_params=params(32),
        name="output",
    )(local, gate, maps, cols, prefix, enter, incoming, gain, w_out, mirror)


def shards(
    hidden,
    base_ids,
    norm_gain,
    w_gate,
    w_value,
    w_bc,
    w_step,
    conv_value,
    conv_bc,
    step_bias,
    decay_rate,
    skip_gain,
    out_gain,
    w_out,
):
    count = lax.axis_size("ctx")
    up = [(i, i + 1) for i in range(count - 1)]
    down = [(j, i) for i, j in up]
    halo = jnp.concatenate(
        [
            lax.ppermute(hidden[-HALO:], "ctx", up),
            lax.ppermute(hidden[:HALO], "ctx", down),
        ],
        axis=0,
    )
    keep = (base_ids != 4).astype(F32)[:, None]
    mix, steps = project_mix(hidden, halo, norm_gain, w_value, w_bc, w_step)
    inner = w_gate.shape[1]
    heads = w_step.shape[1]
    taps = jnp.concatenate([conv_value, conv_bc], axis=1)
    skip = jnp.repeat(skip_gain, inner // heads)[None]
    direct, xf, xb, maps, cols, rows, prefix, enter, final = convolve(
        mix, steps, keep, taps, step_bias, decay_rate, skip
    )
    state, tile = final.shape[3:]
    sent = lax.all_to_all(final.reshape(count, state, tile), "ctx", 0, 0)
    incoming = lax.all_to_all(chain(sent), "ctx", 0, 0)
    incoming = incoming.reshape(final.shape[:3] + incoming.shape[1:])
    gate = project_gate(hidden, norm_gain, w_gate)
    local, mirror = within(direct, xf, xb, maps, cols, rows, w_out)
    parts = lax.axis_size("head")
    term = output(local, gate, maps, cols, prefix, enter, incoming, out_gain[None], w_out, mirror, parts)
    pieces = lax.all_to_all(term, "head", 0, 0)
    return jnp.sum(pieces.astype(F32), axis=0).astype(BF16)


def solution(mesh):
    return jax.shard_map(
        shards,
        mesh=mesh,
        in_specs=(
            P("ctx", None),
            P("ctx"),
            P(),
            P(None, "head"),
            P(None, "head"),
            P(),
            P(None, "head"),
            P(None, "head"),
            P(),
            P("head"),
            P("head"),
            P("head"),
            P("head"),
            P("head", None),
        ),
        out_specs=P("ctx", "head"),
        check_vma=False,
    )
```

```python
import functools

import jax
import jax.numpy as jnp
from jax import lax
from jax.experimental import pallas as pl
from jax.experimental.pallas import tpu as pltpu
from jax.sharding import PartitionSpec as P

EPSILON = 1e-05
HALO = 8
CHUNK = 128
TILE = 128
FLIP = 256
ROWS = 64
GRANT = 56
BF16 = jnp.bfloat16
F32 = jnp.float32
NT = (((1,), (1,)), ((), ()))
TN = (((0,), (0,)), ((), ()))


def params(megabytes, dims=1):
    return pltpu.CompilerParams(
        dimension_semantics=("arbitrary",) * dims, vmem_limit_bytes=megabytes << 20
    )


def iota(shape, dim):
    return lax.broadcasted_iota(jnp.int32, shape, dim)


def dot(a, b):
    return jnp.dot(a, b, preferred_element_type=F32)


def reversal(width):
    where = iota((width, width), 0) + iota((width, width), 1) == width - 1
    return jnp.where(where, 1.0, 0.0).astype(BF16)


def spreader(heads, width):
    shape = (heads, heads * width)
    return jnp.where(iota(shape, 1) // width == iota(shape, 0), 1.0, 0.0).astype(BF16)


def spread(columns, matrix):
    high = columns.astype(BF16)
    low = (columns - high.astype(F32)).astype(BF16)
    return dot(high, matrix) + dot(low, matrix)


def silu(x):
    half = 0.5 * x
    return half + half * jnp.tanh(half)


def scale_rows(source, begin, gain, xs, squares):
    depth = source.shape[1]
    step = min(source.shape[0], TILE)
    for r in range(0, source.shape[0], step):
        x = source[r : r + step, :].astype(F32)
        xs[begin + r : begin + r + step, :] = (x * gain).astype(BF16)
        square = x * x
        partial = square[:, :TILE]
        for c in range(TILE, depth, TILE):
            partial = partial + square[:, c : c + TILE]
        squares[begin + r : begin + r + step, :] += partial


def scale_mirrored(source, begin, gain, xs):
    size, depth = source.shape
    flip = reversal(FLIP)
    for i in range(depth // FLIP):
        at = depth - (i + 1) * FLIP
        lanes = slice(i * FLIP, (i + 1) * FLIP)
        x = dot(source[:, at : at + FLIP], flip)
        xs[begin : begin + size, lanes] = (x * gain[:, lanes]).astype(BF16)


def accumulate(xs, accs, weights, splits):
    part = xs.shape[0] // splits
    for i in range(splits):
        at = slice(i * part, (i + 1) * part)
        x = xs[at, :]
        for acc, weight in zip(accs, weights):
            acc[at, :] += dot(x, weight[...])


def finish_rms(squares, width):
    mean = jnp.sum(squares[...], axis=1, keepdims=True) * (1.0 / width)
    squares[...] = jnp.broadcast_to(lax.rsqrt(mean + EPSILON), squares.shape)


def scale_all(hid, mir, halo, halo_mir, gain, xs, squares):
    tokens, depth = hid.shape
    rows = tokens + 2 * HALO
    scale_rows(hid, 0, gain, xs, squares)
    scale_rows(halo, tokens, gain, xs, squares)
    scale_mirrored(mir, rows, gain, xs)
    scale_mirrored(halo_mir, rows + tokens, gain, xs)


def placed(tokens):
    spans = [(r, r + HALO, TILE) for r in range(0, tokens, TILE)]
    return spans + [(tokens, 0, HALO), (tokens + HALO, tokens + HALO, HALO)]


def mix_kernel(
    hid_ref, mir_ref, before_ref, after_ref, before_mir_ref, after_mir_ref, gain_ref,
    wv_ref, wb_ref, wst_ref, mix_ref, step_ref, acc_v, acc_b, xs, squares, weights,
):
    k = pl.program_id(0)
    tokens, depth = hid_ref.shape
    rows = tokens + 2 * HALO
    inner = wv_ref.shape[1]
    heads = wst_ref.shape[0]
    state = wb_ref.shape[1]

    @pl.when(k == 0)
    def _():
        for acc in (acc_v, acc_b, squares):
            acc[...] = jnp.zeros_like(acc)

    halo = jnp.concatenate([before_ref[...].astype(F32), after_ref[...].astype(F32)], axis=0)
    halo_mir = jnp.concatenate(
        [before_mir_ref[...].astype(F32), after_mir_ref[...].astype(F32)], axis=0
    ).astype(BF16)
    scale_all(hid_ref, mir_ref, halo, halo_mir, gain_ref[...], xs, squares)
    weights[:, :state] = wb_ref[...]
    turned = jnp.concatenate(
        [wst_ref[...].astype(F32), jnp.zeros((TILE - heads, depth), F32)], axis=0
    )
    for c in range(0, depth, TILE):
        weights[c : c + TILE, state:] = turned[:, c : c + TILE].T.astype(BF16)
    accumulate(xs, (acc_v, acc_b), (wv_ref, weights), 3)

    @pl.when(k == pl.num_programs(0) - 1)
    def _():
        finish_rms(squares, depth * pl.num_programs(0))
        for b in range(2):
            for r in range(0, tokens, CHUNK):
                at = r // CHUNK * heads
                step_ref[b, :, at : at + heads] = (
                    acc_b[b * rows + r : b * rows + r + CHUNK, state : state + heads]
                    * squares[r : r + CHUNK, :heads]
                )
            for r, out, size in placed(tokens):
                here = slice(b * rows + r, b * rows + r + size)
                scale = squares[r : r + size, :]
                for c in range(0, inner, TILE):
                    mix_ref[b, c // TILE, out : out + size, :] = acc_v[here, c : c + TILE] * scale
                mix_ref[b, inner // TILE, out : out + size, :] = acc_b[here, :state] * scale


def gate_kernel(
    hid_ref, mir_ref, before_ref, after_ref, before_mir_ref, after_mir_ref, gain_ref,
    wg_ref, wc_ref, taps_ref, gate_ref, maps_ref, acc_g, acc_c, xs, squares, padded,
):
    k = pl.program_id(0)
    tokens, depth = hid_ref.shape
    rows = tokens + 2 * HALO

    @pl.when(k == 0)
    def _():
        for acc in (acc_g, acc_c, squares):
            acc[...] = jnp.zeros_like(acc)

    halo = jnp.concatenate([before_ref[...].astype(F32), after_ref[...].astype(F32)], axis=0)
    halo_mir = jnp.concatenate(
        [before_mir_ref[...].astype(F32), after_mir_ref[...].astype(F32)], axis=0
    ).astype(BF16)
    scale_all(hid_ref, mir_ref, halo, halo_mir, gain_ref[...], xs, squares)
    accumulate(xs, (acc_g, acc_c), (wg_ref, wc_ref), 3)

    @pl.when(k == pl.num_programs(0) - 1)
    def _():
        finish_rms(squares, depth * pl.num_programs(0))
        for b in range(2):
            for r in range(0, tokens, TILE):
                scale = squares[r : r + TILE, :]
                for c in range(0, wg_ref.shape[1], TILE):
                    gate_ref[b, r : r + TILE, c : c + TILE] = silu(
                        acc_g[b * rows + r : b * rows + r + TILE, c : c + TILE] * scale
                    )
            for r, out, size in placed(tokens):
                padded[out : out + size, :] = (
                    acc_c[b * rows + r : b * rows + r + size, :] * squares[r : r + size, :]
                )
            for r in range(0, tokens, ROWS):
                forward, backward = convolved(padded, r, taps_ref[...])
                maps_ref[b, 0, r : r + ROWS, :] = forward.astype(BF16)
                maps_ref[b, 1, r : r + ROWS, :] = backward.astype(BF16)


def convolved(source, row, taps):
    half = CONV - 1
    moved = [source[pl.ds(row + HALO + j, ROWS), :] for j in range(-half, half + 1)]
    forward = taps[0:1] * moved[0]
    backward = taps[0:1] * moved[2 * half]
    for o in range(1, CONV):
        forward = forward + taps[o : o + 1] * moved[o]
        backward = backward + taps[o : o + 1] * moved[2 * half - o]
    return silu(forward), silu(backward)


CONV = 4
DEPTH = 1024


def token_specs(tokens, count):
    ahead = lambda k: (0, k)
    back = lambda k: (0, count - 1 - k)
    return [
        pl.BlockSpec((tokens, DEPTH), ahead),
        pl.BlockSpec((tokens, DEPTH), back),
        pl.BlockSpec((HALO, DEPTH), ahead),
        pl.BlockSpec((HALO, DEPTH), ahead),
        pl.BlockSpec((HALO, DEPTH), back),
        pl.BlockSpec((HALO, DEPTH), back),
        pl.BlockSpec((1, DEPTH), ahead),
    ]


def project_mix(hidden, before, after, norm_gain, w_value, w_bc, w_step):
    tokens, width = hidden.shape
    count = width // DEPTH
    inner, state, heads = w_value.shape[1], w_bc.shape[1] // 2, w_step.shape[1]
    rows = tokens + 2 * HALO
    planes = (inner + state) // TILE
    return pl.pallas_call(
        mix_kernel,
        grid=(count,),
        in_specs=token_specs(tokens, count)
        + [
            pl.BlockSpec((DEPTH, inner), lambda k: (k, 0)),
            pl.BlockSpec((DEPTH, state), lambda k: (k, 0)),
            pl.BlockSpec((heads, DEPTH), lambda k: (0, k)),
        ],
        out_specs=[
            pl.BlockSpec((2, planes, rows, TILE), lambda k: (0, 0, 0, 0)),
            pl.BlockSpec((2, CHUNK, heads * tokens // CHUNK), lambda k: (0, 0, 0)),
        ],
        out_shape=[
            jax.ShapeDtypeStruct((2, planes, rows, TILE), F32),
            jax.ShapeDtypeStruct((2, CHUNK, heads * tokens // CHUNK), F32),
        ],
        scratch_shapes=[
            pltpu.VMEM((2 * rows, inner), F32),
            pltpu.VMEM((2 * rows, state + TILE), F32),
            pltpu.VMEM((2 * rows, DEPTH), BF16),
            pltpu.VMEM((rows, TILE), F32),
            pltpu.VMEM((DEPTH, state + TILE), BF16),
        ],
        compiler_params=params(GRANT),
        cost_estimate=pl.CostEstimate(
            flops=4 * rows * width * (inner + 2 * state + FLIP), transcendentals=0, bytes_accessed=20 << 20
        ),
        name="project_mix",
    )(
        hidden, hidden, before, after, before, after, norm_gain[None], w_value, w_bc, w_step.T
    )


def project_gate(hidden, before, after, norm_gain, w_gate, w_bc, taps):
    tokens, width = hidden.shape
    count = width // DEPTH
    inner, state = w_gate.shape[1], w_bc.shape[1] // 2
    rows = tokens + 2 * HALO
    return pl.pallas_call(
        gate_kernel,
        grid=(count,),
        in_specs=token_specs(tokens, count)
        + [
            pl.BlockSpec((DEPTH, inner), lambda k: (k, 0)),
            pl.BlockSpec((DEPTH, state), lambda k: (k, 1)),
            pl.BlockSpec((CONV, state), lambda k: (0, 1)),
        ],
        out_specs=[
            pl.BlockSpec((2, tokens, inner), lambda k: (0, 0, 0)),
            pl.BlockSpec((2, 2, tokens, state), lambda k: (0, 0, 0, 0)),
        ],
        out_shape=[
            jax.ShapeDtypeStruct((2, tokens, inner), F32),
            jax.ShapeDtypeStruct((2, 2, tokens, state), BF16),
        ],
        scratch_shapes=[
            pltpu.VMEM((2 * rows, inner), F32),
            pltpu.VMEM((2 * rows, state), F32),
            pltpu.VMEM((2 * rows, DEPTH), BF16),
            pltpu.VMEM((rows, TILE), F32),
            pltpu.VMEM((rows, TILE), F32),
        ],
        compiler_params=params(GRANT),
        cost_estimate=pl.CostEstimate(
            flops=4 * rows * width * (inner + state + FLIP),
            transcendentals=2 * tokens * inner,
            bytes_accessed=14 << 20,
        ),
        name="project_gate",
    )(hidden, hidden, before, after, before, after, norm_gain[None], w_gate, w_bc, taps)


def thirds(x):
    high = x.astype(BF16)
    rest = x - high.astype(F32)
    middle = rest.astype(BF16)
    return high, middle, (rest - middle.astype(F32)).astype(BF16)


def exact(matrix, x):
    high, middle, low = thirds(x)
    return dot(matrix, high) + dot(matrix, middle) + dot(matrix, low)


def conv_kernel(
    mix_ref, step_ref, base_ref, tapv_ref, tapb_ref, bias_ref, rate_ref, skip_ref,
    direct_ref, xf_ref, xb_ref, maps_ref, cols_ref, rows_ref, prefix_ref, enter_ref, final_ref,
    dt_sc, wf_sc, wb_sc, keep_sc, vf_sc, vb_sc, carry_sc,
):
    tokens, inner = direct_ref.shape[1:]
    heads = bias_ref.shape[1]
    width = inner // heads
    state = maps_ref.shape[3]
    chunks = tokens // CHUNK
    matrix = spreader(heads, width)

    def lanes_of(x):
        return jnp.concatenate([x] * chunks, axis=1)

    raw = step_ref[0] + lanes_of(bias_ref[...])
    dt = jnp.maximum(raw, 0.0) + jnp.log1p(jnp.exp(-jnp.abs(raw)))
    log_decay = -lanes_of(rate_ref[...]) * dt
    square = (CHUNK, CHUNK)
    lower = jnp.where(iota(square, 0) >= iota(square, 1), 1.0, 0.0).astype(BF16)
    inclusive = exact(lower, log_decay)
    exclusive = inclusive - log_decay
    last = inclusive[CHUNK - 1 : CHUNK]
    columns = (inclusive, exclusive, jnp.exp(inclusive), jnp.exp(last - exclusive))
    pad = jnp.zeros((CHUNK, TILE - chunks * heads), F32)
    turned = [jnp.concatenate([x, pad], axis=1).T for x in (inclusive, exclusive)]
    shape = (chunks * heads, inner)
    for c in range(chunks):
        mine = slice(c * heads, (c + 1) * heads)
        for q, x in enumerate(columns):
            cols_ref[0, c, q] = x[:, mine]
        for q, x in enumerate(turned):
            rows_ref[0, c, q] = x[mine, :]
        select = jnp.where(iota(shape, 1) // width + c * heads == iota(shape, 0), 1.0, 0.0)
        select = select.astype(BF16)
        at = slice(c * CHUNK, (c + 1) * CHUNK)
        dt_sc[at] = spread(dt, select)
        wf_sc[at] = spread(jnp.exp(last - inclusive), select)
        wb_sc[at] = spread(jnp.exp(exclusive), select)
    totals = [last[:, c * heads : (c + 1) * heads] for c in range(chunks)]
    zero = jnp.zeros_like(totals[0])
    before, after = [zero], [zero]
    for c in range(chunks - 1):
        before.append(before[-1] + totals[c])
        after.append(after[-1] + totals[chunks - 1 - c])
    after = after[::-1]
    everything = before[-1] + totals[-1]
    stack = jnp.concatenate(before + after + totals + [everything] * chunks, axis=0)
    prefix_ref[0] = spread(jnp.exp(stack), matrix)
    sent_totals = jnp.concatenate(
        [dot(x, matrix) for x in thirds(everything)] + [jnp.zeros((16 - 3, inner), F32)], axis=0
    ).astype(BF16)

    keep = jnp.where(base_ref[...] != 4, 1.0, 0.0)
    keep = jnp.concatenate([keep, jnp.zeros((CHUNK - chunks, CHUNK), F32)], axis=0).T
    for c in range(chunks):
        keep_sc[c * CHUNK : (c + 1) * CHUNK] = jnp.broadcast_to(keep[:, c : c + 1], square)
    skip = spread(skip_ref[...], matrix)

    def block(i, carry):
        r = pl.multiple_of(i * ROWS, ROWS)
        here = pl.ds(r, ROWS)
        kept = keep_sc[here, :]
        for c in range(0, inner, TILE):
            lanes = slice(c, c + TILE)
            forward, backward = convolved(mix_ref.at[0, c // TILE], r, tapv_ref[:, lanes])
            forward = forward * kept
            backward = backward * kept
            direct_ref[0, here, lanes] = skip[:, lanes] * (forward + backward)
            dt_lanes = dt_sc[here, lanes]
            forward = forward * dt_lanes
            backward = backward * dt_lanes
            xf_ref[0, here, lanes] = forward.astype(BF16)
            xb_ref[0, here, lanes] = backward.astype(BF16)
            vf_sc[here, lanes] = (forward * wf_sc[here, lanes]).astype(BF16)
            vb_sc[here, lanes] = (backward * wb_sc[here, lanes]).astype(BF16)
        forward, backward = convolved(mix_ref.at[0, inner // TILE], r, tapb_ref[...])
        maps_ref[0, 0, here, :] = forward.astype(BF16)
        maps_ref[0, 1, here, :] = backward.astype(BF16)
        return carry

    lax.fori_loop(0, tokens // ROWS, block, 0)

    for direction, moved, order in ((0, vf_sc, range(chunks)), (1, vb_sc, range(chunks - 1, -1, -1))):
        for n, c in enumerate(order):
            at = slice(c * CHUNK, (c + 1) * CHUNK)
            gained = lax.dot_general(
                maps_ref[0, direction, at, :], moved[at, :], TN, preferred_element_type=F32
            )
            if n == 0:
                enter_ref[0, direction, c] = jnp.zeros(enter_ref.shape[3:], BF16)
                carry_sc[...] = gained
            else:
                enter_ref[0, direction, c] = carry_sc[...].astype(BF16)
                total = prefix_ref[0, 2 * chunks + c : 2 * chunks + c + 1, :]
                carry_sc[...] = carry_sc[...] * total + gained
        for j in range(0, inner, TILE):
            final_ref[direction, 0, j // TILE, :state] = carry_sc[:, j : j + TILE].astype(BF16)
            final_ref[direction, 0, j // TILE, state:] = sent_totals[:, j : j + TILE]


def convolve(mix, steps, base_ids, conv_value, conv_bc, step_bias, decay_rate, skip_gain):
    planes, rows = mix.shape[1:3]
    tokens = rows - 2 * HALO
    inner = conv_value.shape[1]
    heads = step_bias.shape[1]
    state = conv_bc.shape[1] // 2
    chunks = tokens // CHUNK
    one = lambda b: (b, 0, 0)
    flat = lambda b: (0, 0)
    four = lambda b: (b, 0, 0, 0)
    five = lambda b: (b, 0, 0, 0, 0)
    return pl.pallas_call(
        conv_kernel,
        grid=(2,),
        in_specs=[
            pl.BlockSpec((1, planes, rows, TILE), four),
            pl.BlockSpec((1, CHUNK, heads * chunks), one),
            pl.BlockSpec((chunks, CHUNK), flat),
            pl.BlockSpec((CONV, inner), flat),
            pl.BlockSpec((CONV, state), flat),
            pl.BlockSpec((1, heads), flat),
            pl.BlockSpec((1, heads), flat),
            pl.BlockSpec((1, heads), flat),
        ],
        out_specs=[
            pl.BlockSpec((1, tokens, inner), one),
            pl.BlockSpec((1, tokens, inner), one),
            pl.BlockSpec((1, tokens, inner), one),
            pl.BlockSpec((1, 2, tokens, state), four),
            pl.BlockSpec((1, chunks, 4, CHUNK, heads), five),
            pl.BlockSpec((1, chunks, 2, heads, CHUNK), five),
            pl.BlockSpec((1, 4 * chunks, inner), one),
            pl.BlockSpec((1, 2, chunks, state, inner), five),
            pl.BlockSpec((2, 1, inner // TILE, state + 16, TILE), lambda b: (0, b, 0, 0, 0)),
        ],
        out_shape=[
            jax.ShapeDtypeStruct((2, tokens, inner), F32),
            jax.ShapeDtypeStruct((2, tokens, inner), BF16),
            jax.ShapeDtypeStruct((2, tokens, inner), BF16),
            jax.ShapeDtypeStruct((2, 2, tokens, state), BF16),
            jax.ShapeDtypeStruct((2, chunks, 4, CHUNK, heads), F32),
            jax.ShapeDtypeStruct((2, chunks, 2, heads, CHUNK), F32),
            jax.ShapeDtypeStruct((2, 4 * chunks, inner), F32),
            jax.ShapeDtypeStruct((2, 2, chunks, state, inner), BF16),
            jax.ShapeDtypeStruct((2, 2, inner // TILE, state + 16, TILE), BF16),
        ],
        scratch_shapes=[
            pltpu.VMEM((tokens, inner), F32),
            pltpu.VMEM((tokens, inner), F32),
            pltpu.VMEM((tokens, inner), F32),
            pltpu.VMEM((tokens, TILE), F32),
            pltpu.VMEM((tokens, inner), BF16),
            pltpu.VMEM((tokens, inner), BF16),
            pltpu.VMEM((state, inner), F32),
        ],
        compiler_params=params(GRANT),
        cost_estimate=pl.CostEstimate(flops=1 << 30, transcendentals=1 << 22, bytes_accessed=20 << 20),
        name="convolve",
    )(mix, steps, base_ids, conv_value, conv_bc, step_bias, decay_rate, skip_gain)


def within_kernel(
    direct_ref, xf_ref, xb_ref, b_ref, c_ref, cols_ref, rows_ref, wout_ref, local_ref, mirror_ref
):
    heads = cols_ref.shape[4]
    inner = direct_ref.shape[2]
    width = inner // heads
    square = (CHUNK, CHUNK)
    below = iota(square, 0) >= iota(square, 1)
    above = iota(square, 0) <= iota(square, 1)
    scores_f = lax.dot_general(c_ref[0, 0], b_ref[0, 0], NT, preferred_element_type=F32)
    scores_b = lax.dot_general(c_ref[0, 1], b_ref[0, 1], NT, preferred_element_type=F32)
    scores_f = jnp.where(below, scores_f, 0.0)
    scores_b = jnp.where(above, scores_b, 0.0)
    left = iota((CHUNK, TILE), 1) < width
    for j in range(0, inner, TILE):
        lanes = slice(j, j + TILE)
        values = jnp.concatenate([xf_ref[0, :, lanes], xb_ref[0, :, lanes]], axis=0)
        parts = []
        for h in range(j // width, (j + TILE) // width):
            gap = jnp.where(
                below,
                cols_ref[0, 0, 0, :, h : h + 1] - rows_ref[0, 0, 0, h : h + 1, :],
                rows_ref[0, 0, 1, h : h + 1, :] - cols_ref[0, 0, 1, :, h : h + 1],
            )
            decay = jnp.exp(gap)
            weights = jnp.concatenate(
                [(decay * scores_f).astype(BF16), (decay * scores_b).astype(BF16)], axis=1
            )
            parts.append(dot(weights, values))
        local_ref[0, :, lanes] = direct_ref[0, :, lanes] + jnp.where(left, parts[0], parts[1])
    flip = reversal(FLIP)
    blocks = wout_ref.shape[1] // FLIP
    for i in range(blocks):
        at = (blocks - 1 - i) * FLIP
        mirror_ref[:, i * FLIP : (i + 1) * FLIP] = dot(wout_ref[:, at : at + FLIP], flip).astype(BF16)


def within(direct, xf, xb, b_maps, c_maps, cols, rows, w_out):
    tokens, inner = direct.shape[1:]
    state = b_maps.shape[3]
    heads = cols.shape[4]
    chunks = tokens // CHUNK
    count = 2 * chunks
    slab = w_out.shape[1] // count
    token = lambda i: (i // chunks, i % chunks, 0)
    inside = lambda i: (i // chunks, 0, i % chunks, 0)
    five = lambda i: (i // chunks, i % chunks, 0, 0, 0)
    return pl.pallas_call(
        within_kernel,
        grid=(count,),
        in_specs=[
            pl.BlockSpec((1, CHUNK, inner), token),
            pl.BlockSpec((1, CHUNK, inner), token),
            pl.BlockSpec((1, CHUNK, inner), token),
            pl.BlockSpec((1, 2, CHUNK, state), inside),
            pl.BlockSpec((1, 2, CHUNK, state), inside),
            pl.BlockSpec((1, 1, 4, CHUNK, heads), five),
            pl.BlockSpec((1, 1, 2, heads, CHUNK), five),
            pl.BlockSpec((inner, slab), lambda i: (0, count - 1 - i)),
        ],
        out_specs=[
            pl.BlockSpec((1, CHUNK, inner), token),
            pl.BlockSpec((inner, slab), lambda i: (0, i)),
        ],
        out_shape=[
            jax.ShapeDtypeStruct((2, tokens, inner), F32),
            jax.ShapeDtypeStruct(w_out.shape, BF16),
        ],
        compiler_params=params(GRANT),
        cost_estimate=pl.CostEstimate(flops=4 << 30, transcendentals=1 << 22, bytes_accessed=24 << 20),
        name="within",
    )(direct, xf, xb, b_maps, c_maps, cols, rows, w_out)


def chain_kernel(states_ref, incoming_ref):
    count = states_ref.shape[0]
    state = incoming_ref.shape[1]
    backward = lax.axis_index("ctx") >= count // 2
    carry = jnp.zeros(incoming_ref.shape[1:], F32)
    for n in range(count):
        at = jnp.where(backward, count - 1 - n, n)
        incoming_ref[at] = carry.astype(incoming_ref.dtype)
        total = jnp.sum(states_ref[at, state:, :].astype(F32), axis=0, keepdims=True)
        carry = carry * jnp.exp(total) + states_ref[at, :state, :].astype(F32)


def chain(states):
    count, rows, tile = states.shape
    return pl.pallas_call(
        chain_kernel,
        out_shape=jax.ShapeDtypeStruct((count, rows - 16, tile), BF16),
        compiler_params=pltpu.CompilerParams(vmem_limit_bytes=16 << 20),
        cost_estimate=pl.CostEstimate(flops=1 << 20, transcendentals=0, bytes_accessed=2 << 20),
        name="chain",
    )(states)


def normalise(
    branch, chunk, local_ref, silu_ref, c_ref, cols_ref, prefix_ref, enter_ref, incoming_ref,
    gain_ref, normed,
):
    chunks = normed.shape[1] // CHUNK
    heads = cols_ref.shape[4]
    inner = local_ref.shape[2]
    width = inner // heads
    matrix = spreader(heads, width)
    scale_f = spread(cols_ref[0, 0, 2], matrix)
    scale_b = spread(cols_ref[0, 0, 3], matrix)
    shape = (FLIP, FLIP)
    group = jnp.where(iota(shape, 0) // width == iota(shape, 1) // width, 1.0, 0.0).astype(BF16)
    ahead = prefix_ref[0, pl.ds(chunk, 1), :]
    behind = prefix_ref[0, pl.ds(chunks + chunk, 1), :]
    for j in range(0, inner, FLIP):
        lanes = slice(j, j + FLIP)
        tiles = range(j // TILE, (j + FLIP) // TILE)
        into_f = jnp.concatenate([incoming_ref[0, 0, t].astype(F32) for t in tiles], axis=1)
        into_b = jnp.concatenate([incoming_ref[1, 0, t].astype(F32) for t in tiles], axis=1)
        into_f = enter_ref[0, 0, 0, :, lanes].astype(F32) + ahead[:, lanes] * into_f
        into_b = enter_ref[0, 1, 0, :, lanes].astype(F32) + behind[:, lanes] * into_b
        y = local_ref[0, :, lanes]
        y = y + scale_f[:, lanes] * dot(c_ref[0, 0], into_f.astype(BF16))
        y = y + scale_b[:, lanes] * dot(c_ref[0, 1], into_b.astype(BF16))
        y = y * silu_ref[0, :, lanes]
        square = y * y
        high = square.astype(BF16)
        low = (square - high.astype(F32)).astype(BF16)
        mean = (dot(high, group) + dot(low, group)) * (1.0 / width)
        y = y * lax.rsqrt(mean + EPSILON) * gain_ref[:, lanes]
        at = pl.ds(pl.multiple_of(chunk * CHUNK, CHUNK), CHUNK)
        normed[branch, at, lanes] = y.astype(BF16)


def multiply_out(n, row, normed, wout_ref, mirror_ref, send_ref, keep_ref):
    rows = send_ref.shape[1]
    half = 4

    def product():
        at = slice(row, row + rows)
        return (dot(normed[0, at], wout_ref[...]) + dot(normed[1, at], mirror_ref[...])).astype(BF16)

    @pl.when(n < half)
    def _():
        send_ref[0] = product()

    @pl.when(n >= half)
    def _():
        keep_ref[0] = product()


def first_kernel(
    blocks_ref, local_ref, silu_ref, c_ref, cols_ref, prefix_ref, enter_ref, incoming_ref, gain_ref,
    wout_ref, mirror_ref, send_ref, keep_ref, normed,
):
    i = pl.program_id(0)
    chunks = normed.shape[1] // CHUNK

    @pl.when(i < 2 * chunks)
    def _():
        normalise(
            i // chunks, i % chunks, local_ref, silu_ref, c_ref, cols_ref, prefix_ref, enter_ref,
            incoming_ref, gain_ref, normed,
        )

    @pl.when(i >= 2 * chunks)
    def _():
        multiply_out(i - 2 * chunks, 0, normed, wout_ref, mirror_ref, send_ref, keep_ref)


def first_output(blocks, local, gate, c_maps, cols, prefix, enter, incoming, gain, w_out, mirror, rows):
    tokens, inner = local.shape[1:]
    state = c_maps.shape[3]
    heads = cols.shape[4]
    chunks = tokens // CHUNK
    parts = 8
    pre = 2 * chunks
    slab = w_out.shape[1] // parts
    held = lambda i: jnp.minimum(i, pre - 1)
    token = lambda i, n: (held(i) // chunks, held(i) % chunks, 0)
    inside = lambda i, n: (held(i) // chunks, 0, held(i) % chunks, 0)
    column = lambda i, n: (0, n[jnp.maximum(i - pre, 0)])
    return pl.pallas_call(
        first_kernel,
        grid_spec=pltpu.PrefetchScalarGridSpec(
            num_scalar_prefetch=1,
            grid=(pre + parts,),
            in_specs=[
                pl.BlockSpec((1, CHUNK, inner), token),
                pl.BlockSpec((1, CHUNK, inner), token),
                pl.BlockSpec((1, 2, CHUNK, state), inside),
                pl.BlockSpec(
                    (1, 1, 4, CHUNK, heads), lambda i, n: (held(i) // chunks, held(i) % chunks, 0, 0, 0)
                ),
                pl.BlockSpec((1, 4 * chunks, inner), lambda i, n: (held(i) // chunks, 0, 0)),
                pl.BlockSpec(
                    (1, 2, 1, state, inner),
                    lambda i, n: (held(i) // chunks, 0, held(i) % chunks, 0, 0),
                ),
                pl.BlockSpec(
                    (2, 1, inner // TILE, state, TILE), lambda i, n: (0, held(i) // chunks, 0, 0, 0)
                ),
                pl.BlockSpec((1, inner), lambda i, n: (0, 0)),
                pl.BlockSpec((inner, slab), column),
                pl.BlockSpec((inner, slab), column),
            ],
            out_specs=[
                pl.BlockSpec((1, rows, slab), lambda i, n: (jnp.clip(i - pre, 0, 3), 0, 0)),
                pl.BlockSpec((1, rows, slab), lambda i, n: (jnp.maximum(i - pre - 4, 0), 0, 0)),
                pl.BlockSpec((2, tokens, inner), lambda i, n: (0, 0, 0)),
            ],
        ),
        out_shape=[
            jax.ShapeDtypeStruct((4, rows, slab), BF16),
            jax.ShapeDtypeStruct((4, rows, slab), BF16),
            jax.ShapeDtypeStruct((2, tokens, inner), BF16),
        ],
        compiler_params=params(GRANT),
        cost_estimate=pl.CostEstimate(flops=3 << 30, transcendentals=1 << 20, bytes_accessed=24 << 20),
        name="first_output",
    )(blocks, local, gate, c_maps, cols, prefix, enter, incoming, gain, w_out, mirror)


def next_output(blocks, normed, w_out, mirror, row, rows):
    tokens, inner = normed.shape[1:]
    parts = 8
    slab = w_out.shape[1] // parts
    column = lambda i, n: (0, n[i])

    def kernel(blocks_ref, normed_ref, wout_ref, mirror_ref, send_ref, keep_ref):
        multiply_out(pl.program_id(0), row, normed_ref, wout_ref, mirror_ref, send_ref, keep_ref)

    return pl.pallas_call(
        kernel,
        grid_spec=pltpu.PrefetchScalarGridSpec(
            num_scalar_prefetch=1,
            grid=(parts,),
            in_specs=[
                pl.BlockSpec((2, tokens, inner), lambda i, n: (0, 0, 0)),
                pl.BlockSpec((inner, slab), column),
                pl.BlockSpec((inner, slab), column),
            ],
            out_specs=[
                pl.BlockSpec((1, rows, slab), lambda i, n: (jnp.minimum(i, 3), 0, 0)),
                pl.BlockSpec((1, rows, slab), lambda i, n: (jnp.maximum(i - 4, 0), 0, 0)),
            ],
        ),
        out_shape=[jax.ShapeDtypeStruct((4, rows, slab), BF16)] * 2,
        compiler_params=params(GRANT),
        cost_estimate=pl.CostEstimate(flops=2 << 30, transcendentals=0, bytes_accessed=12 << 20),
        name="next_output",
    )(blocks, normed, w_out, mirror)


ORDERS = ((2, 6, 1), (6, 1, 2), (1, 2, 6))
GROUPS = ((0, 176), (176, 176), (352, 160))


def block_order(order):
    kept = [0]
    for partner in order[:0:-1]:
        kept = [k ^ partner for k in kept] + kept
    return [k ^ order[0] for k in kept] + kept


def reduced(send, keep, order):
    for partner in order:
        pairs = [(i, i ^ partner) for i in range(lax.axis_size("head"))]
        arrived = lax.ppermute(send, "head", pairs)
        half = keep.shape[0] // 2
        total = (keep.astype(F32) + arrived.astype(F32)).astype(BF16)
        send, keep = total[:half], total[half:]
    return total[0]


def shards(
    hidden,
    base_ids,
    norm_gain,
    w_gate,
    w_value,
    w_bc,
    w_step,
    conv_value,
    conv_bc,
    step_bias,
    decay_rate,
    skip_gain,
    out_gain,
    w_out,
):
    count = lax.axis_size("ctx")
    up = [(i, i + 1) for i in range(count - 1)]
    down = [(j, i) for i, j in up]
    before = lax.ppermute(hidden[-HALO:], "ctx", up)
    after = lax.ppermute(hidden[:HALO], "ctx", down)
    mix, steps = project_mix(hidden, before, after, norm_gain, w_value, w_bc, w_step)
    direct, xf, xb, b_maps, cols, rows, prefix, enter, final = convolve(
        mix,
        steps,
        base_ids.reshape(-1, CHUNK),
        conv_value,
        conv_bc,
        step_bias[None],
        decay_rate[None],
        skip_gain[None],
    )
    state, tile = final.shape[3:]
    sent = lax.all_to_all(final.reshape(count, state, tile), "ctx", 0, 0)
    gate, c_maps = project_gate(hidden, before, after, norm_gain, w_gate, w_bc, conv_bc)
    sent, gate, c_maps = lax.optimization_barrier((sent, gate, c_maps))
    incoming = lax.all_to_all(chain(sent), "ctx", 0, 0)
    incoming = incoming.reshape(final.shape[:3] + incoming.shape[1:])
    local, mirror = within(direct, xf, xb, b_maps, c_maps, cols, rows, w_out)
    blocks = jnp.array([block_order(o) for o in ORDERS], jnp.int32) ^ lax.axis_index("head")
    send, keep, normed = first_output(
        blocks[0], local, gate, c_maps, cols, prefix, enter, incoming, out_gain[None], w_out, mirror,
        GROUPS[0][1],
    )
    groups = [(send, keep)]
    for i in (1, 2):
        groups.append(next_output(blocks[i], normed, w_out, mirror, *GROUPS[i]))
    return jnp.concatenate([reduced(*g, o) for g, o in zip(groups, ORDERS)], axis=0)


def solution(mesh):
    return jax.shard_map(
        shards,
        mesh=mesh,
        in_specs=(
            P("ctx", None),
            P("ctx"),
            P(),
            P(None, "head"),
            P(None, "head"),
            P(),
            P(None, "head"),
            P(None, "head"),
            P(),
            P("head"),
            P("head"),
            P("head"),
            P("head"),
            P("head", None),
        ),
        out_specs=P("ctx", "head"),
        check_vma=False,
    )
```

```python
import functools

import jax
import jax.numpy as jnp
from jax import lax
from jax.experimental import pallas as pl
from jax.experimental.pallas import tpu as pltpu
from jax.sharding import PartitionSpec as P

EPSILON = 1e-05
HALO = 8
CHUNK = 128
TILE = 128
FLIP = 256
ROWS = 64
GRANT = 56
BF16 = jnp.bfloat16
F32 = jnp.float32
NT = (((1,), (1,)), ((), ()))
TN = (((0,), (0,)), ((), ()))


def params(megabytes, dims=1):
    return pltpu.CompilerParams(
        dimension_semantics=("arbitrary",) * dims, vmem_limit_bytes=megabytes << 20
    )


def iota(shape, dim):
    return lax.broadcasted_iota(jnp.int32, shape, dim)


def dot(a, b):
    return jnp.dot(a, b, preferred_element_type=F32)


def reversal(width):
    where = iota((width, width), 0) + iota((width, width), 1) == width - 1
    return jnp.where(where, 1.0, 0.0).astype(BF16)


def spreader(heads, width):
    shape = (heads, heads * width)
    return jnp.where(iota(shape, 1) // width == iota(shape, 0), 1.0, 0.0).astype(BF16)


def selector(group, heads, columns, inner):
    shape = (columns, inner)
    where = iota(shape, 1) // (inner // heads) + group * heads == iota(shape, 0)
    return jnp.where(where, 1.0, 0.0).astype(BF16)


def spread(columns, matrix):
    high = columns.astype(BF16)
    low = (columns - high.astype(F32)).astype(BF16)
    return dot(high, matrix) + dot(low, matrix)


def silu(x):
    half = 0.5 * x
    return half + half * jnp.tanh(half)


def scale_rows(source, begin, gain, xs, squares):
    depth = source.shape[1]
    step = min(source.shape[0], TILE)
    for r in range(0, source.shape[0], step):
        x = source[r : r + step, :].astype(F32)
        xs[begin + r : begin + r + step, :] = (x * gain).astype(BF16)
        square = x * x
        partial = square[:, :TILE]
        for c in range(TILE, depth, TILE):
            partial = partial + square[:, c : c + TILE]
        squares[begin + r : begin + r + step, :] += partial


def scale_mirrored(source, begin, gain, xs):
    size, depth = source.shape
    flip = reversal(FLIP)
    for i in range(depth // FLIP):
        at = depth - (i + 1) * FLIP
        lanes = slice(i * FLIP, (i + 1) * FLIP)
        x = dot(source[:, at : at + FLIP], flip)
        xs[begin : begin + size, lanes] = (x * gain[:, lanes]).astype(BF16)


def accumulate(xs, acc, weights, splits):
    part = xs.shape[0] // splits
    depth = weights[0].shape[0]
    for i in range(splits):
        at = slice(i * part, (i + 1) * part)
        total = dot(xs[at, :depth], weights[0][...])
        for j in range(1, len(weights)):
            total = total + dot(xs[at, j * depth : (j + 1) * depth], weights[j][...])
        acc[at, :] += total


def finish_rms(squares, width):
    mean = jnp.sum(squares[...], axis=1, keepdims=True) * (1.0 / width)
    squares[...] = jnp.broadcast_to(lax.rsqrt(mean + EPSILON), squares.shape)


def scale_all(hid, before, after, gain, xs, squares):
    tokens, depth = hid[0].shape
    rows = tokens + 2 * HALO
    for i in range(2):
        lanes = pl.ds(i * depth, depth)
        halo = jnp.concatenate([before[i][...].astype(F32), after[i][...].astype(F32)], axis=0)
        own, other = gain[i][...], gain[1 - i][...]
        scale_rows(hid[i], 0, own, xs.at[:, lanes], squares)
        scale_rows(halo, tokens, own, xs.at[:, lanes], squares)
        lanes = pl.ds((1 - i) * depth, depth)
        scale_mirrored(hid[i], rows, other, xs.at[:, lanes])
        scale_mirrored(halo.astype(BF16), rows + tokens, other, xs.at[:, lanes])


def placed(tokens):
    spans = [(r, r + HALO, TILE) for r in range(0, tokens, TILE)]
    return spans + [(tokens, 0, HALO), (tokens + HALO, tokens + HALO, HALO)]


def mix_step(hid, before, after, gain, wv, wb, wst, mix, steps, acc_v, acc_b, xs, squares, weights, last):
    tokens, depth = hid[0].shape
    rows = tokens + 2 * HALO
    inner = wv[0].shape[1]
    heads = wst[0].shape[0]
    state = wb[0].shape[1]
    scale_all(hid, before, after, gain, xs, squares)
    for i in range(2):
        weights[i * depth : (i + 1) * depth, :state] = wb[i][...]
        turned = jnp.concatenate(
            [wst[i][...].astype(F32), jnp.zeros((TILE - heads, depth), F32)], axis=0
        )
        for c in range(0, depth, TILE):
            weights[i * depth + c : i * depth + c + TILE, state:] = (
                turned[:, c : c + TILE].T.astype(BF16)
            )
    accumulate(xs, acc_v, wv, 3)
    accumulate(xs, acc_b, (weights,), 3)

    @pl.when(last)
    def _():
        finish_rms(squares, WIDTH)
        for b in range(2):
            for r in range(0, tokens, CHUNK):
                at = r // CHUNK * heads
                steps[b, :, at : at + heads] = (
                    acc_b[b * rows + r : b * rows + r + CHUNK, state : state + heads]
                    * squares[r : r + CHUNK, :heads]
                )
            for r, out, size in placed(tokens):
                here = slice(b * rows + r, b * rows + r + size)
                scale = squares[r : r + size, :]
                for c in range(0, inner, TILE):
                    mix[b, c // TILE, out : out + size, :] = acc_v[here, c : c + TILE] * scale
                mix[b, inner // TILE, out : out + size, :] = acc_b[here, :state] * scale


def gate_kernel(*refs):
    hid, before, after, gain, wg, wc = (refs[2 * i : 2 * i + 2] for i in range(6))
    taps_ref, gate_ref, maps_ref, acc_g, acc_c, xs, squares, padded = refs[12:]
    k = pl.program_id(0)
    tokens = hid[0].shape[0]
    rows = tokens + 2 * HALO

    @pl.when(k == 0)
    def _():
        for acc in (acc_g, acc_c, squares):
            acc[...] = jnp.zeros_like(acc)

    scale_all(hid, before, after, gain, xs, squares)
    accumulate(xs, acc_g, wg, 3)
    accumulate(xs, acc_c, wc, 3)

    @pl.when(k == pl.num_programs(0) - 1)
    def _():
        finish_rms(squares, WIDTH)
        for b in range(2):
            for r in range(0, tokens, TILE):
                scale = squares[r : r + TILE, :]
                for c in range(0, gate_ref.shape[2], TILE):
                    gate_ref[b, r : r + TILE, c : c + TILE] = silu(
                        acc_g[b * rows + r : b * rows + r + TILE, c : c + TILE] * scale
                    )
            for r, out, size in placed(tokens):
                padded[out : out + size, :] = (
                    acc_c[b * rows + r : b * rows + r + size, :] * squares[r : r + size, :]
                )
            for r in range(0, tokens, ROWS):
                forward, backward = convolved(padded, r, taps_ref[...])
                maps_ref[b, 0, r : r + ROWS, :] = forward.astype(BF16)
                maps_ref[b, 1, r : r + ROWS, :] = backward.astype(BF16)


def convolved(source, row, taps):
    half = CONV - 1
    moved = [source[pl.ds(row + HALO + j, ROWS), :] for j in range(-half, half + 1)]
    forward = taps[0:1] * moved[0]
    backward = taps[0:1] * moved[2 * half]
    for o in range(1, CONV):
        forward = forward + taps[o : o + 1] * moved[o]
        backward = backward + taps[o : o + 1] * moved[2 * half - o]
    return silu(forward), silu(backward)


CONV = 4
DEPTH = 512
WIDTH = 4096


PAIRS = 4


def paired(block, index):
    held = lambda k: jnp.minimum(k, PAIRS - 1)
    return [
        pl.BlockSpec(block, lambda k: index(held(k))),
        pl.BlockSpec(block, lambda k: index(2 * PAIRS - 1 - held(k))),
    ]


def token_specs(tokens):
    across = lambda k: (0, k)
    return (
        paired((tokens, DEPTH), across)
        + paired((HALO, DEPTH), across)
        + paired((HALO, DEPTH), across)
        + paired((1, DEPTH), across)
    )


def project_gate(hidden, before, after, norm_gain, w_gate, w_bc, taps):
    tokens, width = hidden.shape
    inner, state = w_gate.shape[1], w_bc.shape[1] // 2
    rows = tokens + 2 * HALO
    return pl.pallas_call(
        gate_kernel,
        grid=(PAIRS,),
        in_specs=token_specs(tokens)
        + paired((DEPTH, inner), lambda k: (k, 0))
        + paired((DEPTH, state), lambda k: (k, 1))
        + [pl.BlockSpec((CONV, state), lambda k: (0, 1))],
        out_specs=[
            pl.BlockSpec((2, tokens, inner), lambda k: (0, 0, 0)),
            pl.BlockSpec((2, 2, tokens, state), lambda k: (0, 0, 0, 0)),
        ],
        out_shape=[
            jax.ShapeDtypeStruct((2, tokens, inner), F32),
            jax.ShapeDtypeStruct((2, 2, tokens, state), BF16),
        ],
        scratch_shapes=[
            pltpu.VMEM((2 * rows, inner), F32),
            pltpu.VMEM((2 * rows, state), F32),
            pltpu.VMEM((2 * rows, 2 * DEPTH), BF16),
            pltpu.VMEM((rows, TILE), F32),
            pltpu.VMEM((rows, TILE), F32),
        ],
        compiler_params=params(GRANT),
        cost_estimate=pl.CostEstimate(
            flops=4 * rows * width * (inner + state + FLIP),
            transcendentals=2 * tokens * inner,
            bytes_accessed=14 << 20,
        ),
        name="project_gate",
    )(*twice(hidden, before, after, norm_gain[None], w_gate, w_bc), taps)


def twice(*arrays):
    return [x for x in arrays for _ in range(2)]


def thirds(x):
    high = x.astype(BF16)
    rest = x - high.astype(F32)
    middle = rest.astype(BF16)
    return high, middle, (rest - middle.astype(F32)).astype(BF16)


def exact(matrix, x):
    high, middle, low = thirds(x)
    return dot(matrix, high) + dot(matrix, middle) + dot(matrix, low)


def conv_step(
    mix, steps, base_ref, tapv_ref, tapb_ref, bias_ref, rate_ref, skip_ref,
    direct_ref, xf_ref, xb_ref, maps_ref, cols_ref, rows_ref, enter_ref, final_ref,
    dt_sc, wf_sc, wb_sc, keep_sc, vf_sc, vb_sc, carry_sc,
):
    tokens, inner = direct_ref.shape[1:]
    heads = bias_ref.shape[1]
    width = inner // heads
    state = maps_ref.shape[3]
    chunks = tokens // CHUNK
    matrix = spreader(heads, width)

    def lanes_of(x):
        return jnp.concatenate([x] * chunks, axis=1)

    raw = steps[...] + lanes_of(bias_ref[...])
    dt = jnp.maximum(raw, 0.0) + jnp.log1p(jnp.exp(-jnp.abs(raw)))
    log_decay = -lanes_of(rate_ref[...]) * dt
    square = (CHUNK, CHUNK)
    lower = jnp.where(iota(square, 0) >= iota(square, 1), 1.0, 0.0).astype(BF16)
    inclusive = exact(lower, log_decay)
    exclusive = inclusive - log_decay
    last = inclusive[CHUNK - 1 : CHUNK]
    pad = jnp.zeros((CHUNK, TILE - chunks * heads), F32)
    turned = [jnp.concatenate([x, pad], axis=1).T for x in (inclusive, exclusive)]
    for c in range(chunks):
        mine = slice(c * heads, (c + 1) * heads)
        for q, x in enumerate(turned):
            rows_ref[0, c, q] = x[mine, :]
        select = selector(c, heads, chunks * heads, inner)
        at = slice(c * CHUNK, (c + 1) * CHUNK)
        dt_sc[at] = spread(dt, select)
        wf_sc[at] = spread(jnp.exp(last - inclusive), select)
        wb_sc[at] = spread(jnp.exp(exclusive), select)
    totals = [last[:, c * heads : (c + 1) * heads] for c in range(chunks)]
    zero = jnp.zeros_like(totals[0])
    before, after = [zero], [zero]
    for c in range(chunks - 1):
        before.append(before[-1] + totals[c])
        after.append(after[-1] + totals[chunks - 1 - c])
    after = after[::-1]
    everything = before[-1] + totals[-1]
    leaving = last - exclusive
    columns = (
        inclusive,
        exclusive,
        jnp.exp(inclusive),
        jnp.exp(leaving),
        jnp.exp(inclusive + jnp.concatenate(before, axis=1)),
        jnp.exp(leaving + jnp.concatenate(after, axis=1)),
    )
    for c in range(chunks):
        mine = slice(c * heads, (c + 1) * heads)
        cols_ref[0, c] = jnp.concatenate([x[:, mine] for x in columns], axis=1)
    chunk_decay = spread(jnp.exp(jnp.concatenate(totals + [zero] * (8 - chunks), axis=0)), matrix)
    sent_totals = jnp.concatenate(
        [dot(x, matrix) for x in thirds(everything)] + [jnp.zeros((16 - 3, inner), F32)], axis=0
    ).astype(BF16)

    keep = jnp.where(base_ref[...] != 4, 1.0, 0.0)
    keep = jnp.concatenate([keep, jnp.zeros((CHUNK - chunks, CHUNK), F32)], axis=0).T
    for c in range(chunks):
        keep_sc[c * CHUNK : (c + 1) * CHUNK] = jnp.broadcast_to(keep[:, c : c + 1], square)
    skip = spread(skip_ref[...], matrix)

    def block(i, carry):
        r = pl.multiple_of(i * ROWS, ROWS)
        here = pl.ds(r, ROWS)
        kept = keep_sc[here, :]
        for c in range(0, inner, TILE):
            lanes = slice(c, c + TILE)
            forward, backward = convolved(mix.at[c // TILE], r, tapv_ref[:, lanes])
            forward = forward * kept
            backward = backward * kept
            direct_ref[0, here, lanes] = skip[:, lanes] * (forward + backward)
            dt_lanes = dt_sc[here, lanes]
            forward = forward * dt_lanes
            backward = backward * dt_lanes
            xf_ref[0, here, lanes] = forward.astype(BF16)
            xb_ref[0, here, lanes] = backward.astype(BF16)
            vf_sc[here, lanes] = (forward * wf_sc[here, lanes]).astype(BF16)
            vb_sc[here, lanes] = (backward * wb_sc[here, lanes]).astype(BF16)
        forward, backward = convolved(mix.at[inner // TILE], r, tapb_ref[...])
        maps_ref[0, 0, here, :] = forward.astype(BF16)
        maps_ref[0, 1, here, :] = backward.astype(BF16)
        return carry

    lax.fori_loop(0, tokens // ROWS, block, 0)

    for direction, moved, order in ((0, vf_sc, range(chunks)), (1, vb_sc, range(chunks - 1, -1, -1))):
        for n, c in enumerate(order):
            at = slice(c * CHUNK, (c + 1) * CHUNK)
            gained = lax.dot_general(
                maps_ref[0, direction, at, :], moved[at, :], TN, preferred_element_type=F32
            )
            if n == 0:
                enter_ref[0, direction, c] = jnp.zeros(enter_ref.shape[3:], BF16)
                carry_sc[...] = gained
            else:
                enter_ref[0, direction, c] = carry_sc[...].astype(BF16)
                carry_sc[...] = carry_sc[...] * chunk_decay[c : c + 1, :] + gained
        for j in range(0, inner, TILE):
            final_ref[direction, 0, j // TILE, :state] = carry_sc[:, j : j + TILE].astype(BF16)
            final_ref[direction, 0, j // TILE, state:] = sent_totals[:, j : j + TILE]


COLUMNS = 6


def front_kernel(*refs):
    hid, before, after, gain, wv, wb, wst = (refs[2 * i : 2 * i + 2] for i in range(7))
    small, outs, scratch = refs[14:20], refs[20:28], refs[28:]
    acc_v, acc_b, xs, squares, weights, mix, steps = scratch[:7]
    i = pl.program_id(0)

    @pl.when(i == 0)
    def _():
        for acc in (acc_v, acc_b, squares):
            acc[...] = jnp.zeros_like(acc)

    @pl.when(i < PAIRS)
    def _():
        mix_step(
            hid, before, after, gain, wv, wb, wst, mix, steps, acc_v, acc_b, xs, squares, weights,
            i == PAIRS - 1,
        )

    @pl.when(i >= PAIRS)
    def _():
        b = i - PAIRS
        conv_step(mix.at[b], steps.at[b], *small, *outs, *scratch[7:])


def front(
    hidden, before, after, norm_gain, w_value, w_bc, w_step,
    base_ids, conv_value, conv_bc, step_bias, decay_rate, skip_gain,
):
    tokens, width = hidden.shape
    inner, state, heads = w_value.shape[1], w_bc.shape[1] // 2, w_step.shape[1]
    rows = tokens + 2 * HALO
    chunks = tokens // CHUNK
    branch = lambda k: jnp.maximum(k - PAIRS, 0)
    one = lambda k: (branch(k), 0, 0)
    flat = lambda k: (0, 0)
    four = lambda k: (branch(k), 0, 0, 0)
    five = lambda k: (branch(k), 0, 0, 0, 0)
    return pl.pallas_call(
        front_kernel,
        grid=(PAIRS + 2,),
        in_specs=token_specs(tokens)
        + paired((DEPTH, inner), lambda k: (k, 0))
        + paired((DEPTH, state), lambda k: (k, 0))
        + paired((heads, DEPTH), lambda k: (0, k))
        + [
            pl.BlockSpec((chunks, CHUNK), flat),
            pl.BlockSpec((CONV, inner), flat),
            pl.BlockSpec((CONV, state), flat),
            pl.BlockSpec((1, heads), flat),
            pl.BlockSpec((1, heads), flat),
            pl.BlockSpec((1, heads), flat),
        ],
        out_specs=[
            pl.BlockSpec((1, tokens, inner), one),
            pl.BlockSpec((1, tokens, inner), one),
            pl.BlockSpec((1, tokens, inner), one),
            pl.BlockSpec((1, 2, tokens, state), four),
            pl.BlockSpec((1, chunks, CHUNK, COLUMNS * heads), four),
            pl.BlockSpec((1, chunks, 2, heads, CHUNK), five),
            pl.BlockSpec((1, 2, chunks, state, inner), five),
            pl.BlockSpec((2, 1, inner // TILE, state + 16, TILE), lambda k: (0, branch(k), 0, 0, 0)),
        ],
        out_shape=[
            jax.ShapeDtypeStruct((2, tokens, inner), F32),
            jax.ShapeDtypeStruct((2, tokens, inner), BF16),
            jax.ShapeDtypeStruct((2, tokens, inner), BF16),
            jax.ShapeDtypeStruct((2, 2, tokens, state), BF16),
            jax.ShapeDtypeStruct((2, chunks, CHUNK, COLUMNS * heads), F32),
            jax.ShapeDtypeStruct((2, chunks, 2, heads, CHUNK), F32),
            jax.ShapeDtypeStruct((2, 2, chunks, state, inner), BF16),
            jax.ShapeDtypeStruct((2, 2, inner // TILE, state + 16, TILE), BF16),
        ],
        scratch_shapes=[
            pltpu.VMEM((2 * rows, inner), F32),
            pltpu.VMEM((2 * rows, state + TILE), F32),
            pltpu.VMEM((2 * rows, 2 * DEPTH), BF16),
            pltpu.VMEM((rows, TILE), F32),
            pltpu.VMEM((2 * DEPTH, state + TILE), BF16),
            pltpu.VMEM((2, (inner + state) // TILE, rows, TILE), F32),
            pltpu.VMEM((2, CHUNK, heads * chunks), F32),
            pltpu.VMEM((tokens, inner), F32),
            pltpu.VMEM((tokens, inner), F32),
            pltpu.VMEM((tokens, inner), F32),
            pltpu.VMEM((tokens, TILE), F32),
            pltpu.VMEM((tokens, inner), BF16),
            pltpu.VMEM((tokens, inner), BF16),
            pltpu.VMEM((state, inner), F32),
        ],
        compiler_params=params(GRANT),
        cost_estimate=pl.CostEstimate(
            flops=4 * rows * width * (inner + 2 * state + FLIP),
            transcendentals=1 << 22,
            bytes_accessed=24 << 20,
        ),
        name="front",
    )(
        *twice(hidden, before, after, norm_gain[None], w_value, w_bc, w_step.T),
        base_ids, conv_value, conv_bc, step_bias, decay_rate, skip_gain,
    )


def within_kernel(direct_ref, xf_ref, xb_ref, b_ref, c_ref, cols_ref, rows_ref, enter_ref, local_ref):
    heads = rows_ref.shape[3]
    inner = direct_ref.shape[2]
    width = inner // heads
    square = (CHUNK, CHUNK)
    below = iota(square, 0) >= iota(square, 1)
    above = iota(square, 0) <= iota(square, 1)
    scores_f = lax.dot_general(c_ref[0, 0], b_ref[0, 0], NT, preferred_element_type=F32)
    scores_b = lax.dot_general(c_ref[0, 1], b_ref[0, 1], NT, preferred_element_type=F32)
    scores_f = jnp.where(below, scores_f, 0.0)
    scores_b = jnp.where(above, scores_b, 0.0)
    left = iota((CHUNK, TILE), 1) < width
    cols = cols_ref[0, 0]
    across_f = dot(c_ref[0, 0], enter_ref[0, 0, 0]) * spread(
        cols, selector(2, heads, cols.shape[1], inner)
    )
    across_b = dot(c_ref[0, 1], enter_ref[0, 1, 0]) * spread(
        cols, selector(3, heads, cols.shape[1], inner)
    )
    local_ref[0] = direct_ref[0] + across_f + across_b
    for j in range(0, inner, TILE):
        lanes = slice(j, j + TILE)
        values = jnp.concatenate([xf_ref[0, :, lanes], xb_ref[0, :, lanes]], axis=0)
        parts = []
        for h in range(j // width, (j + TILE) // width):
            gap = jnp.where(
                below,
                cols[:, h : h + 1] - rows_ref[0, 0, 0, h : h + 1, :],
                rows_ref[0, 0, 1, h : h + 1, :] - cols[:, heads + h : heads + h + 1],
            )
            decay = jnp.exp(gap)
            weights = jnp.concatenate(
                [(decay * scores_f).astype(BF16), (decay * scores_b).astype(BF16)], axis=1
            )
            parts.append(dot(weights, values))
        local_ref[0, :, lanes] += jnp.where(left, parts[0], parts[1])


def within(direct, xf, xb, b_maps, c_maps, cols, rows, enter):
    tokens, inner = direct.shape[1:]
    state = b_maps.shape[3]
    heads = rows.shape[3]
    chunks = tokens // CHUNK
    token = lambda i: (i // chunks, i % chunks, 0)
    inside = lambda i: (i // chunks, 0, i % chunks, 0)
    return pl.pallas_call(
        within_kernel,
        grid=(2 * chunks,),
        in_specs=[
            pl.BlockSpec((1, CHUNK, inner), token),
            pl.BlockSpec((1, CHUNK, inner), token),
            pl.BlockSpec((1, CHUNK, inner), token),
            pl.BlockSpec((1, 2, CHUNK, state), inside),
            pl.BlockSpec((1, 2, CHUNK, state), inside),
            pl.BlockSpec((1, 1, CHUNK, cols.shape[3]), lambda i: (i // chunks, i % chunks, 0, 0)),
            pl.BlockSpec((1, 1, 2, heads, CHUNK), lambda i: (i // chunks, i % chunks, 0, 0, 0)),
            pl.BlockSpec((1, 2, 1, state, inner), lambda i: (i // chunks, 0, i % chunks, 0, 0)),
        ],
        out_specs=pl.BlockSpec((1, CHUNK, inner), token),
        out_shape=jax.ShapeDtypeStruct((2, tokens, inner), F32),
        compiler_params=params(GRANT),
        cost_estimate=pl.CostEstimate(flops=4 << 30, transcendentals=1 << 22, bytes_accessed=16 << 20),
        name="within",
    )(direct, xf, xb, b_maps, c_maps, cols, rows, enter)


def chain_kernel(states_ref, incoming_ref):
    count = states_ref.shape[0]
    state = incoming_ref.shape[1]
    backward = lax.axis_index("ctx") >= count // 2
    carry = jnp.zeros(incoming_ref.shape[1:], F32)
    for n in range(count):
        at = jnp.where(backward, count - 1 - n, n)
        incoming_ref[at] = carry.astype(incoming_ref.dtype)
        total = jnp.sum(states_ref[at, state:, :].astype(F32), axis=0, keepdims=True)
        carry = carry * jnp.exp(total) + states_ref[at, :state, :].astype(F32)


def chain(states):
    count, rows, tile = states.shape
    return pl.pallas_call(
        chain_kernel,
        out_shape=jax.ShapeDtypeStruct((count, rows - 16, tile), BF16),
        compiler_params=pltpu.CompilerParams(vmem_limit_bytes=16 << 20),
        cost_estimate=pl.CostEstimate(flops=1 << 20, transcendentals=0, bytes_accessed=2 << 20),
        name="chain",
    )(states)


ORDERS = ((2, 6, 1), (6, 1, 2), (1, 2, 6))
GROUPS = ((0, 176), (176, 176), (352, 160))
STEPS = (2, 3, 0, 1)
PARTS = 8


def kept_blocks(order):
    kept = {0}
    for partner in order[1:]:
        kept |= {k ^ partner for k in kept}
    return kept


def slots(order):
    kept = kept_blocks(order)
    given = [r for s in STEPS for r in (s, PARTS - 1 - s)]
    return [r for r in given if r not in kept], [r for r in given if r in kept]


def normalise(row, b, local_ref, silu_ref, c_ref, cols_ref, incoming_ref, gain_ref, normed):
    size, inner = local_ref.shape[1:]
    columns = cols_ref.shape[3]
    heads = columns // COLUMNS
    width = inner // heads
    cols = cols_ref[0].reshape(size, columns)
    shape = (FLIP, FLIP)
    group = jnp.where(iota(shape, 0) // width == iota(shape, 1) // width, 1.0, 0.0).astype(BF16)
    scale_f = spread(cols, selector(4, heads, columns, inner))
    scale_b = spread(cols, selector(5, heads, columns, inner))
    for j in range(0, inner, FLIP):
        lanes = slice(j, j + FLIP)
        tiles = range(j // TILE, (j + FLIP) // TILE)
        into_f = jnp.concatenate([incoming_ref[0, 0, t] for t in tiles], axis=1)
        into_b = jnp.concatenate([incoming_ref[1, 0, t] for t in tiles], axis=1)
        y = local_ref[0, :, lanes]
        y = y + scale_f[:, lanes] * dot(c_ref[0, 0], into_f)
        y = y + scale_b[:, lanes] * dot(c_ref[0, 1], into_b)
        y = y * silu_ref[0, :, lanes]
        square = y * y
        high = square.astype(BF16)
        low = (square - high.astype(F32)).astype(BF16)
        mean = (dot(high, group) + dot(low, group)) * (1.0 / width)
        y = y * lax.rsqrt(mean + EPSILON) * gain_ref[:, lanes]
        normed[b, pl.ds(pl.multiple_of(row, size), size), lanes] = y.astype(BF16)


def output_kernel(
    place_ref, local_ref, silu_ref, c_ref, cols_ref, incoming_ref, gain_ref, wout_ref, wmir_ref, *rest
):
    outs, (normed, mirrored, product) = rest[:-3], rest[-3:]
    i = pl.program_id(0)
    size = local_ref.shape[1]
    halves = normed.shape[1] // size
    pre = 2 * halves
    slab = wout_ref.shape[1]

    @pl.when(i < pre)
    def _():
        normalise(
            (i % halves) * size, i // halves, local_ref, silu_ref, c_ref, cols_ref, incoming_ref,
            gain_ref, normed,
        )

    @pl.when(i >= pre)
    def _():
        flip = reversal(FLIP)
        straight = (wout_ref, wmir_ref)
        for n in range(2):
            source = straight[1 - n]
            for c in range(0, slab, FLIP):
                at = slab - FLIP - c
                mirrored[:, c : c + FLIP] = dot(source[:, at : at + FLIP], flip).astype(BF16)
            product[n] = dot(normed[0], straight[n][...]) + dot(normed[1], mirrored[...])

    for t, step in enumerate(STEPS):

        @pl.when(i == pre + t)
        def _():
            for g, (order, (row, rows)) in enumerate(zip(ORDERS, GROUPS)):
                sent, kept = slots(order)
                for n, block in enumerate((step, PARTS - 1 - step)):
                    ref, held = (outs[2 * g], sent) if block in sent else (outs[2 * g + 1], kept)
                    at = held.index(block) % ref.shape[0]
                    ref[at] = product[n, row : row + rows, :].astype(ref.dtype)


def output(local, gate, c_maps, cols, incoming, gain, w_out):
    tokens, inner = local.shape[1:]
    state = c_maps.shape[3]
    chunks = tokens // CHUNK
    size = 2 * CHUNK
    halves = tokens // size
    pre = 2 * halves
    slab = w_out.shape[1] // PARTS
    held = lambda i: jnp.minimum(i, pre - 1)
    token = lambda i, n: (held(i) // halves, held(i) % halves, 0)
    block = lambda i, n: n[0] ^ (jnp.maximum(i - pre, 0) ^ STEPS[0])
    late = lambda i: jnp.maximum(i - pre, 0)
    out_specs, out_shape = [], []
    for order, (_, rows) in zip(ORDERS, GROUPS):
        sent, _ = slots(order)
        if {STEPS[0], PARTS - 1 - STEPS[0]} <= set(sent):
            per, places = 2, (lambda i, n: (jnp.minimum(late(i), 1), 0, 0), lambda i, n: (jnp.maximum(late(i) - 2, 0), 0, 0))
        else:
            per, places = 1, (lambda i, n: (late(i), 0, 0),) * 2
        for place, dtype in zip(places, (BF16, F32)):
            out_specs.append(pl.BlockSpec((per, rows, slab), place))
            out_shape.append(jax.ShapeDtypeStruct((PARTS // 2, rows, slab), dtype))
    return pl.pallas_call(
        output_kernel,
        grid_spec=pltpu.PrefetchScalarGridSpec(
            num_scalar_prefetch=1,
            grid=(pre + len(STEPS),),
            in_specs=[
                pl.BlockSpec((1, size, inner), token),
                pl.BlockSpec((1, size, inner), token),
                pl.BlockSpec((1, 2, size, state), lambda i, n: (held(i) // halves, 0, held(i) % halves, 0)),
                pl.BlockSpec(
                    (1, size // CHUNK, CHUNK, cols.shape[3]),
                    lambda i, n: (held(i) // halves, held(i) % halves, 0, 0),
                ),
                pl.BlockSpec(
                    (2, 1, inner // TILE, state, TILE), lambda i, n: (0, held(i) // halves, 0, 0, 0)
                ),
                pl.BlockSpec((1, inner), lambda i, n: (0, 0)),
                pl.BlockSpec((inner, slab), lambda i, n: (0, block(i, n))),
                pl.BlockSpec((inner, slab), lambda i, n: (0, PARTS - 1 - block(i, n))),
            ],
            out_specs=out_specs,
            scratch_shapes=[
                pltpu.VMEM((2, tokens, inner), BF16),
                pltpu.VMEM((inner, slab), BF16),
                pltpu.VMEM((2, tokens, slab), F32),
            ],
        ),
        out_shape=out_shape,
        compiler_params=params(GRANT),
        cost_estimate=pl.CostEstimate(flops=6 << 30, transcendentals=1 << 20, bytes_accessed=20 << 20),
        name="output",
    )(lax.axis_index("head")[None], local, gate, c_maps, cols, incoming, gain, w_out, w_out)


def reduced(send, keep, order):
    sent, kept = slots(order)
    for n, partner in enumerate(order):
        pairs = [(i, i ^ partner) for i in range(PARTS)]
        arrived = lax.ppermute(send, "head", pairs)
        arrived_as = [r ^ partner for r in sent]

        def total(block):
            return keep[kept.index(block)] + arrived[arrived_as.index(block)].astype(F32)

        if n == len(order) - 1:
            return total(0).astype(BF16)
        following = order[n + 1]
        rest = {0}
        for other in order[n + 2 :]:
            rest |= {k ^ other for k in rest}
        new_kept = [r for r in kept if r in rest]
        new_sent = [r ^ following for r in new_kept]
        send = jnp.stack([total(r).astype(BF16) for r in new_sent])
        keep = jnp.stack([total(r) for r in new_kept])
        sent, kept = new_sent, new_kept


def shards(
    hidden,
    base_ids,
    norm_gain,
    w_gate,
    w_value,
    w_bc,
    w_step,
    conv_value,
    conv_bc,
    step_bias,
    decay_rate,
    skip_gain,
    out_gain,
    w_out,
):
    count = lax.axis_size("ctx")
    up = [(i, i + 1) for i in range(count - 1)]
    down = [(j, i) for i, j in up]
    before = lax.ppermute(hidden[-HALO:], "ctx", up)
    after = lax.ppermute(hidden[:HALO], "ctx", down)
    direct, xf, xb, b_maps, cols, rows, enter, final = front(
        hidden, before, after, norm_gain, w_value, w_bc, w_step,
        base_ids.reshape(-1, CHUNK),
        conv_value,
        conv_bc,
        step_bias[None],
        decay_rate[None],
        skip_gain[None],
    )
    state, tile = final.shape[3:]
    sent = lax.all_to_all(final.reshape(count, state, tile), "ctx", 0, 0)
    gate, c_maps = project_gate(hidden, before, after, norm_gain, w_gate, w_bc, conv_bc)
    sent, gate, c_maps = lax.optimization_barrier((sent, gate, c_maps))
    incoming = lax.all_to_all(chain(sent), "ctx", 0, 0)
    incoming = incoming.reshape(final.shape[:3] + incoming.shape[1:])
    local = within(direct, xf, xb, b_maps, c_maps, cols, rows, enter)
    outs = output(local, gate, c_maps, cols, incoming, out_gain[None], w_out)
    return jnp.concatenate(
        [reduced(outs[2 * g], outs[2 * g + 1], order) for g, order in enumerate(ORDERS)], axis=0
    )


def solution(mesh):
    return jax.shard_map(
        shards,
        mesh=mesh,
        in_specs=(
            P("ctx", None),
            P("ctx"),
            P(),
            P(None, "head"),
            P(None, "head"),
            P(),
            P(None, "head"),
            P(None, "head"),
            P(),
            P("head"),
            P("head"),
            P("head"),
            P("head"),
            P("head", None),
        ),
        out_specs=P("ctx", "head"),
        check_vma=False,
    )
```

```python
import functools

import jax
import jax.numpy as jnp
from jax import lax
from jax.experimental import pallas as pl
from jax.experimental.pallas import tpu as pltpu
from jax.sharding import PartitionSpec as P

EPSILON = 1e-05
HALO = 8
CHUNK = 128
TILE = 128
FLIP = 256
ROWS = 64
GRANT = 56
OUTPUT_GRANT = 28
BF16 = jnp.bfloat16
F32 = jnp.float32
NT = (((1,), (1,)), ((), ()))
TN = (((0,), (0,)), ((), ()))


def params(megabytes, dims=1):
    return pltpu.CompilerParams(
        dimension_semantics=("arbitrary",) * dims, vmem_limit_bytes=megabytes << 20
    )


def streamed(*arrays):
    return [pltpu.with_memory_space_constraint(x, pltpu.HBM) for x in arrays]


def iota(shape, dim):
    return lax.broadcasted_iota(jnp.int32, shape, dim)


def dot(a, b):
    return jnp.dot(a, b, preferred_element_type=F32)


def reversal(width):
    where = iota((width, width), 0) + iota((width, width), 1) == width - 1
    return jnp.where(where, 1.0, 0.0).astype(BF16)


def spreader(heads, width):
    shape = (heads, heads * width)
    return jnp.where(iota(shape, 1) // width == iota(shape, 0), 1.0, 0.0).astype(BF16)


def selector(group, heads, columns, inner):
    shape = (columns, inner)
    where = iota(shape, 1) // (inner // heads) + group * heads == iota(shape, 0)
    return jnp.where(where, 1.0, 0.0).astype(BF16)


def spread(columns, matrix):
    high = columns.astype(BF16)
    low = (columns - high.astype(F32)).astype(BF16)
    return dot(high, matrix) + dot(low, matrix)


def silu(x):
    half = 0.5 * x
    return half + half * jnp.tanh(half)


def scale_rows(source, begin, gain, xs, squares):
    depth = source.shape[1]
    step = min(source.shape[0], TILE)
    for r in range(0, source.shape[0], step):
        x = source[r : r + step, :].astype(F32)
        xs[begin + r : begin + r + step, :] = (x * gain).astype(BF16)
        square = x * x
        partial = square[:, :TILE]
        for c in range(TILE, depth, TILE):
            partial = partial + square[:, c : c + TILE]
        squares[begin + r : begin + r + step, :] += partial


def scale_mirrored(source, begin, gain, xs):
    size, depth = source.shape
    flip = reversal(FLIP)
    for i in range(depth // FLIP):
        at = depth - (i + 1) * FLIP
        lanes = slice(i * FLIP, (i + 1) * FLIP)
        x = dot(source[:, at : at + FLIP], flip)
        xs[begin : begin + size, lanes] = (x * gain[:, lanes]).astype(BF16)


def accumulate(xs, acc, weights, splits):
    part = xs.shape[0] // splits
    depth = weights[0].shape[0]
    for i in range(splits):
        at = slice(i * part, (i + 1) * part)
        total = dot(xs[at, :depth], weights[0][...])
        for j in range(1, len(weights)):
            total = total + dot(xs[at, j * depth : (j + 1) * depth], weights[j][...])
        acc[at, :] += total


def finish_rms(squares, width):
    mean = jnp.sum(squares[...], axis=1, keepdims=True) * (1.0 / width)
    squares[...] = jnp.broadcast_to(lax.rsqrt(mean + EPSILON), squares.shape)


def scale_all(hid, gain, xs, squares, halo=None):
    tokens, depth = hid[0].shape
    rows = xs.shape[0] // 2
    for i in range(2):
        lanes = pl.ds(i * depth, depth)
        mirrored = pl.ds((1 - i) * depth, depth)
        own, other = gain[i][...], gain[1 - i][...]
        scale_rows(hid[i], 0, own, xs.at[:, lanes], squares)
        scale_mirrored(hid[i], rows, other, xs.at[:, mirrored])
        if halo:
            beside = jnp.concatenate([half[i][...].astype(F32) for half in halo], axis=0)
            scale_rows(beside, tokens, own, xs.at[:, lanes], squares)
            scale_mirrored(beside.astype(BF16), rows + tokens, other, xs.at[:, mirrored])


def placed(tokens):
    spans = [(r, r + HALO, TILE) for r in range(0, tokens, TILE)]
    return spans + [(tokens, 0, HALO), (tokens + HALO, tokens + HALO, HALO)]


def mix_step(hid, before, after, gain, wv, wbc, wst, mix, steps, acc_v, acc_b, acc_s, xs, squares, last):
    tokens, depth = hid[0].shape
    rows = tokens + 2 * HALO
    inner, maps = acc_v.shape[1], acc_b.shape[1]
    heads = acc_s.shape[1]
    chunks = tokens // CHUNK
    scale_all(hid, gain, xs, squares, (before, after))
    accumulate(xs, acc_v, wv, 3)
    accumulate(xs, acc_b, wbc, 3)
    for b in range(2):
        at = slice(b * rows, b * rows + tokens)
        total = lax.dot_general(wst[0][...], xs[at, :depth], NT, preferred_element_type=F32)
        total = total + lax.dot_general(wst[1][...], xs[at, depth:], NT, preferred_element_type=F32)
        acc_s[b] += total

    @pl.when(last)
    def _():
        finish_rms(squares, WIDTH)
        spans = [slice(c * CHUNK, (c + 1) * CHUNK) for c in range(chunks)]
        scale = jnp.concatenate([squares[at, :heads] for at in spans], axis=1)
        for b in range(2):
            stack = [acc_s[b, :, at] for at in spans]
            stack.append(jnp.zeros((TILE - chunks * heads, CHUNK), F32))
            steps[b] = jnp.concatenate(stack, axis=0).T[:, : chunks * heads] * scale
            for r, out, size in placed(tokens):
                here = slice(b * rows + r, b * rows + r + size)
                scales = squares[r : r + size, :]
                for c in range(0, inner, TILE):
                    mix[b, c // TILE, out : out + size, :] = acc_v[here, c : c + TILE] * scales
                for c in range(0, maps, TILE):
                    mix[b, (inner + c) // TILE, out : out + size, :] = acc_b[here, c : c + TILE] * scales


def gate_kernel(*refs):
    hid, gain, wg = (refs[2 * i : 2 * i + 2] for i in range(3))
    gate_ref, acc_g, xs, squares = refs[6:]
    k = pl.program_id(0)
    tokens = hid[0].shape[0]

    @pl.when(k == 0)
    def _():
        for acc in (acc_g, squares):
            acc[...] = jnp.zeros_like(acc)

    scale_all(hid, gain, xs, squares)
    accumulate(xs, acc_g, wg, 2)

    @pl.when(k == pl.num_programs(0) - 1)
    def _():
        finish_rms(squares, WIDTH)
        for b in range(2):
            for r in range(0, tokens, TILE):
                scale = squares[r : r + TILE, :]
                for c in range(0, gate_ref.shape[2], TILE):
                    gate_ref[b, r : r + TILE, c : c + TILE] = silu(
                        acc_g[b * tokens + r : b * tokens + r + TILE, c : c + TILE] * scale
                    )


def convolved(source, row, taps):
    half = CONV - 1
    moved = [source[pl.ds(row + HALO + j, ROWS), :] for j in range(-half, half + 1)]
    forward = taps[0:1] * moved[0]
    backward = taps[0:1] * moved[2 * half]
    for o in range(1, CONV):
        forward = forward + taps[o : o + 1] * moved[o]
        backward = backward + taps[o : o + 1] * moved[2 * half - o]
    return silu(forward), silu(backward)


CONV = 4
DEPTH = 512
WIDTH = 4096


PAIRS = 4


def paired(block, index):
    held = lambda k: jnp.minimum(k, PAIRS - 1)
    return [
        pl.BlockSpec(block, lambda k: index(held(k))),
        pl.BlockSpec(block, lambda k: index(2 * PAIRS - 1 - held(k))),
    ]


def across(k):
    return (0, k)


def downward(k):
    return (k, 0)


def project_gate(hidden, norm_gain, w_gate):
    tokens, width = hidden.shape
    inner = w_gate.shape[1]
    return pl.pallas_call(
        gate_kernel,
        grid=(PAIRS,),
        in_specs=paired((tokens, DEPTH), across)
        + paired((1, DEPTH), across)
        + paired((DEPTH, inner), downward),
        out_specs=pl.BlockSpec((2, tokens, inner), lambda k: (0, 0, 0)),
        out_shape=jax.ShapeDtypeStruct((2, tokens, inner), F32),
        scratch_shapes=[
            pltpu.VMEM((2 * tokens, inner), F32),
            pltpu.VMEM((2 * tokens, 2 * DEPTH), BF16),
            pltpu.VMEM((tokens, TILE), F32),
        ],
        compiler_params=params(GRANT),
        cost_estimate=pl.CostEstimate(
            flops=4 * tokens * width * (inner + FLIP),
            transcendentals=2 * tokens * inner,
            bytes_accessed=12 << 20,
        ),
        name="project_gate",
    )(*twice(*streamed(hidden), norm_gain[None], *streamed(w_gate)))


def twice(*arrays):
    return [x for x in arrays for _ in range(2)]


def thirds(x):
    high = x.astype(BF16)
    rest = x - high.astype(F32)
    middle = rest.astype(BF16)
    return high, middle, (rest - middle.astype(F32)).astype(BF16)


def exact(matrix, x):
    high, middle, low = thirds(x)
    return dot(matrix, high) + dot(matrix, middle) + dot(matrix, low)


def conv_step(
    mix, steps, base_ref, tapv_ref, tapb_ref, bias_ref, rate_ref, skip_ref,
    direct_ref, xf_ref, xb_ref, maps_ref, cmaps_ref, cols_ref, rows_ref, enter_ref, final_ref,
    dt_sc, wf_sc, wb_sc, keep_sc, vf_sc, vb_sc, carry_sc,
):
    tokens, inner = direct_ref.shape[1:]
    heads = bias_ref.shape[1]
    width = inner // heads
    state = maps_ref.shape[3]
    chunks = tokens // CHUNK
    matrix = spreader(heads, width)

    def lanes_of(x):
        return jnp.concatenate([x] * chunks, axis=1)

    raw = steps[...] + lanes_of(bias_ref[...])
    dt = jnp.maximum(raw, 0.0) + jnp.log1p(jnp.exp(-jnp.abs(raw)))
    log_decay = -lanes_of(rate_ref[...]) * dt
    square = (CHUNK, CHUNK)
    lower = jnp.where(iota(square, 0) >= iota(square, 1), 1.0, 0.0).astype(BF16)
    inclusive = exact(lower, log_decay)
    exclusive = inclusive - log_decay
    last = inclusive[CHUNK - 1 : CHUNK]
    pad = jnp.zeros((CHUNK, TILE - chunks * heads), F32)
    turned = [jnp.concatenate([x, pad], axis=1).T for x in (inclusive, exclusive)]
    for c in range(chunks):
        mine = slice(c * heads, (c + 1) * heads)
        for q, x in enumerate(turned):
            rows_ref[0, c, q] = x[mine, :]
        select = selector(c, heads, chunks * heads, inner)
        at = slice(c * CHUNK, (c + 1) * CHUNK)
        dt_sc[at] = spread(dt, select)
        wf_sc[at] = spread(jnp.exp(last - inclusive), select)
        wb_sc[at] = spread(jnp.exp(exclusive), select)
    totals = [last[:, c * heads : (c + 1) * heads] for c in range(chunks)]
    zero = jnp.zeros_like(totals[0])
    before, after = [zero], [zero]
    for c in range(chunks - 1):
        before.append(before[-1] + totals[c])
        after.append(after[-1] + totals[chunks - 1 - c])
    after = after[::-1]
    everything = before[-1] + totals[-1]
    leaving = last - exclusive
    columns = (
        inclusive,
        exclusive,
        jnp.exp(inclusive),
        jnp.exp(leaving),
        jnp.exp(inclusive + jnp.concatenate(before, axis=1)),
        jnp.exp(leaving + jnp.concatenate(after, axis=1)),
    )
    for c in range(chunks):
        mine = slice(c * heads, (c + 1) * heads)
        cols_ref[0, c] = jnp.concatenate([x[:, mine] for x in columns], axis=1)
    chunk_decay = spread(jnp.exp(jnp.concatenate(totals + [zero] * (8 - chunks), axis=0)), matrix)
    sent_totals = jnp.concatenate(
        [dot(x, matrix) for x in thirds(everything)] + [jnp.zeros((16 - 3, inner), F32)], axis=0
    ).astype(BF16)

    keep = jnp.where(base_ref[...] != 4, 1.0, 0.0)
    keep = jnp.concatenate([keep, jnp.zeros((CHUNK - chunks, CHUNK), F32)], axis=0).T
    for c in range(chunks):
        keep_sc[c * CHUNK : (c + 1) * CHUNK] = jnp.broadcast_to(keep[:, c : c + 1], square)
    skip = spread(skip_ref[...], matrix)

    def block(i, carry):
        r = pl.multiple_of(i * ROWS, ROWS)
        here = pl.ds(r, ROWS)
        kept = keep_sc[here, :]
        for c in range(0, inner, TILE):
            lanes = slice(c, c + TILE)
            forward, backward = convolved(mix.at[c // TILE], r, tapv_ref[:, lanes])
            forward = forward * kept
            backward = backward * kept
            direct_ref[0, here, lanes] = skip[:, lanes] * (forward + backward)
            dt_lanes = dt_sc[here, lanes]
            forward = forward * dt_lanes
            backward = backward * dt_lanes
            xf_ref[0, here, lanes] = forward.astype(BF16)
            xb_ref[0, here, lanes] = backward.astype(BF16)
            vf_sc[here, lanes] = (forward * wf_sc[here, lanes]).astype(BF16)
            vb_sc[here, lanes] = (backward * wb_sc[here, lanes]).astype(BF16)
        for n, maps in enumerate((maps_ref, cmaps_ref)):
            taps = tapb_ref[:, n * state : (n + 1) * state]
            forward, backward = convolved(mix.at[inner // TILE + n], r, taps)
            maps[0, 0, here, :] = forward.astype(BF16)
            maps[0, 1, here, :] = backward.astype(BF16)
        return carry

    lax.fori_loop(0, tokens // ROWS, block, 0)

    for direction, moved, order in ((0, vf_sc, range(chunks)), (1, vb_sc, range(chunks - 1, -1, -1))):
        for n, c in enumerate(order):
            at = slice(c * CHUNK, (c + 1) * CHUNK)
            gained = lax.dot_general(
                maps_ref[0, direction, at, :], moved[at, :], TN, preferred_element_type=F32
            )
            if n == 0:
                enter_ref[0, direction, c] = jnp.zeros(enter_ref.shape[3:], BF16)
                carry_sc[...] = gained
            else:
                enter_ref[0, direction, c] = carry_sc[...].astype(BF16)
                carry_sc[...] = carry_sc[...] * chunk_decay[c : c + 1, :] + gained
        for j in range(0, inner, TILE):
            final_ref[direction, 0, j // TILE, :state] = carry_sc[:, j : j + TILE].astype(BF16)
            final_ref[direction, 0, j // TILE, state:] = sent_totals[:, j : j + TILE]


COLUMNS = 6


def front_kernel(*refs):
    hid, before, after, gain, wv, wbc, wst = (refs[2 * i : 2 * i + 2] for i in range(7))
    small, outs, scratch = refs[14:20], refs[20:29], refs[29:]
    acc_v, acc_b, acc_s, xs, squares, mix, steps = scratch[:7]
    i = pl.program_id(0)

    @pl.when(i == 0)
    def _():
        for acc in (acc_v, acc_b, acc_s, squares):
            acc[...] = jnp.zeros_like(acc)

    @pl.when(i < PAIRS)
    def _():
        mix_step(
            hid, before, after, gain, wv, wbc, wst, mix, steps, acc_v, acc_b, acc_s, xs, squares,
            i == PAIRS - 1,
        )

    @pl.when(i >= PAIRS)
    def _():
        b = i - PAIRS
        conv_step(mix.at[b], steps.at[b], *small, *outs, *scratch[7:])


def front(
    hidden, before, after, norm_gain, w_value, w_bc, w_step,
    base_ids, conv_value, conv_bc, step_bias, decay_rate, skip_gain,
):
    tokens, width = hidden.shape
    inner, state, heads = w_value.shape[1], w_bc.shape[1] // 2, w_step.shape[1]
    rows = tokens + 2 * HALO
    chunks = tokens // CHUNK
    branch = lambda k: jnp.maximum(k - PAIRS, 0)
    one = lambda k: (branch(k), 0, 0)
    flat = lambda k: (0, 0)
    four = lambda k: (branch(k), 0, 0, 0)
    five = lambda k: (branch(k), 0, 0, 0, 0)
    return pl.pallas_call(
        front_kernel,
        grid=(PAIRS + 2,),
        in_specs=paired((tokens, DEPTH), across)
        + paired((HALO, DEPTH), across)
        + paired((HALO, DEPTH), across)
        + paired((1, DEPTH), across)
        + paired((DEPTH, inner), downward)
        + paired((DEPTH, 2 * state), downward)
        + paired((heads, DEPTH), across)
        + [
            pl.BlockSpec((chunks, CHUNK), flat),
            pl.BlockSpec((CONV, inner), flat),
            pl.BlockSpec((CONV, 2 * state), flat),
            pl.BlockSpec((1, heads), flat),
            pl.BlockSpec((1, heads), flat),
            pl.BlockSpec((1, heads), flat),
        ],
        out_specs=[
            pl.BlockSpec((1, tokens, inner), one),
            pl.BlockSpec((1, tokens, inner), one),
            pl.BlockSpec((1, tokens, inner), one),
            pl.BlockSpec((1, 2, tokens, state), four),
            pl.BlockSpec((1, 2, tokens, state), four),
            pl.BlockSpec((1, chunks, CHUNK, COLUMNS * heads), four),
            pl.BlockSpec((1, chunks, 2, heads, CHUNK), five),
            pl.BlockSpec((1, 2, chunks, state, inner), five),
            pl.BlockSpec((2, 1, inner // TILE, state + 16, TILE), lambda k: (0, branch(k), 0, 0, 0)),
        ],
        out_shape=[
            jax.ShapeDtypeStruct((2, tokens, inner), F32),
            jax.ShapeDtypeStruct((2, tokens, inner), BF16),
            jax.ShapeDtypeStruct((2, tokens, inner), BF16),
            jax.ShapeDtypeStruct((2, 2, tokens, state), BF16),
            jax.ShapeDtypeStruct((2, 2, tokens, state), BF16),
            jax.ShapeDtypeStruct((2, chunks, CHUNK, COLUMNS * heads), F32),
            jax.ShapeDtypeStruct((2, chunks, 2, heads, CHUNK), F32),
            jax.ShapeDtypeStruct((2, 2, chunks, state, inner), BF16),
            jax.ShapeDtypeStruct((2, 2, inner // TILE, state + 16, TILE), BF16),
        ],
        scratch_shapes=[
            pltpu.VMEM((2 * rows, inner), F32),
            pltpu.VMEM((2 * rows, 2 * state), F32),
            pltpu.VMEM((2, heads, tokens), F32),
            pltpu.VMEM((2 * rows, 2 * DEPTH), BF16),
            pltpu.VMEM((rows, TILE), F32),
            pltpu.VMEM((2, (inner + 2 * state) // TILE, rows, TILE), F32),
            pltpu.VMEM((2, CHUNK, heads * chunks), F32),
            pltpu.VMEM((tokens, inner), F32),
            pltpu.VMEM((tokens, inner), F32),
            pltpu.VMEM((tokens, inner), F32),
            pltpu.VMEM((tokens, TILE), F32),
            pltpu.VMEM((tokens, inner), BF16),
            pltpu.VMEM((tokens, inner), BF16),
            pltpu.VMEM((state, inner), F32),
        ],
        compiler_params=params(GRANT),
        cost_estimate=pl.CostEstimate(
            flops=4 * rows * width * (inner + 2 * state + FLIP),
            transcendentals=1 << 22,
            bytes_accessed=24 << 20,
        ),
        name="front",
    )(
        *twice(*streamed(hidden), before, after, norm_gain[None], *streamed(w_value, w_bc, w_step.T)),
        base_ids, conv_value, conv_bc, step_bias, decay_rate, skip_gain,
    )


def within_kernel(direct_ref, xf_ref, xb_ref, b_ref, c_ref, cols_ref, rows_ref, enter_ref, local_ref):
    heads = rows_ref.shape[3]
    inner = direct_ref.shape[2]
    width = inner // heads
    square = (CHUNK, CHUNK)
    below = iota(square, 0) >= iota(square, 1)
    above = iota(square, 0) <= iota(square, 1)
    scores_f = lax.dot_general(c_ref[0, 0], b_ref[0, 0], NT, preferred_element_type=F32)
    scores_b = lax.dot_general(c_ref[0, 1], b_ref[0, 1], NT, preferred_element_type=F32)
    scores_f = jnp.where(below, scores_f, 0.0)
    scores_b = jnp.where(above, scores_b, 0.0)
    left = iota((CHUNK, TILE), 1) < width
    cols = cols_ref[0, 0]
    across_f = dot(c_ref[0, 0], enter_ref[0, 0, 0]) * spread(
        cols, selector(2, heads, cols.shape[1], inner)
    )
    across_b = dot(c_ref[0, 1], enter_ref[0, 1, 0]) * spread(
        cols, selector(3, heads, cols.shape[1], inner)
    )
    local_ref[0] = direct_ref[0] + across_f + across_b
    for j in range(0, inner, TILE):
        lanes = slice(j, j + TILE)
        values = jnp.concatenate([xf_ref[0, :, lanes], xb_ref[0, :, lanes]], axis=0)
        parts = []
        for h in range(j // width, (j + TILE) // width):
            gap = jnp.where(
                below,
                cols[:, h : h + 1] - rows_ref[0, 0, 0, h : h + 1, :],
                rows_ref[0, 0, 1, h : h + 1, :] - cols[:, heads + h : heads + h + 1],
            )
            decay = jnp.exp(gap)
            weights = jnp.concatenate(
                [(decay * scores_f).astype(BF16), (decay * scores_b).astype(BF16)], axis=1
            )
            parts.append(dot(weights, values))
        local_ref[0, :, lanes] += jnp.where(left, parts[0], parts[1])


def within(direct, xf, xb, b_maps, c_maps, cols, rows, enter):
    tokens, inner = direct.shape[1:]
    state = b_maps.shape[3]
    heads = rows.shape[3]
    chunks = tokens // CHUNK
    token = lambda i: (i // chunks, i % chunks, 0)
    inside = lambda i: (i // chunks, 0, i % chunks, 0)
    return pl.pallas_call(
        within_kernel,
        grid=(2 * chunks,),
        in_specs=[
            pl.BlockSpec((1, CHUNK, inner), token),
            pl.BlockSpec((1, CHUNK, inner), token),
            pl.BlockSpec((1, CHUNK, inner), token),
            pl.BlockSpec((1, 2, CHUNK, state), inside),
            pl.BlockSpec((1, 2, CHUNK, state), inside),
            pl.BlockSpec((1, 1, CHUNK, cols.shape[3]), lambda i: (i // chunks, i % chunks, 0, 0)),
            pl.BlockSpec((1, 1, 2, heads, CHUNK), lambda i: (i // chunks, i % chunks, 0, 0, 0)),
            pl.BlockSpec((1, 2, 1, state, inner), lambda i: (i // chunks, 0, i % chunks, 0, 0)),
        ],
        out_specs=pl.BlockSpec((1, CHUNK, inner), token),
        out_shape=jax.ShapeDtypeStruct((2, tokens, inner), F32),
        compiler_params=params(GRANT),
        cost_estimate=pl.CostEstimate(flops=4 << 30, transcendentals=1 << 22, bytes_accessed=16 << 20),
        name="within",
    )(direct, xf, xb, b_maps, c_maps, cols, rows, enter)


def chain_kernel(states_ref, incoming_ref):
    count = states_ref.shape[0]
    state = incoming_ref.shape[1]
    backward = lax.axis_index("ctx") >= count // 2
    carry = jnp.zeros(incoming_ref.shape[1:], F32)
    for n in range(count):
        at = jnp.where(backward, count - 1 - n, n)
        incoming_ref[at] = carry.astype(incoming_ref.dtype)
        total = jnp.sum(states_ref[at, state:, :].astype(F32), axis=0, keepdims=True)
        carry = carry * jnp.exp(total) + states_ref[at, :state, :].astype(F32)


def chain(states):
    count, rows, tile = states.shape
    return pl.pallas_call(
        chain_kernel,
        out_shape=jax.ShapeDtypeStruct((count, rows - 16, tile), BF16),
        compiler_params=pltpu.CompilerParams(vmem_limit_bytes=16 << 20),
        cost_estimate=pl.CostEstimate(flops=1 << 20, transcendentals=0, bytes_accessed=2 << 20),
        name="chain",
    )(states)


ORDERS = ((2, 6, 1), (6, 1, 2), (1, 2, 6))
GROUPS = ((0, 176), (176, 176), (352, 160))
STEPS = (2, 3, 0, 1)
PARTS = 8


def kept_blocks(order):
    kept = {0}
    for partner in order[1:]:
        kept |= {k ^ partner for k in kept}
    return kept


def slots(order):
    kept = kept_blocks(order)
    given = [r for s in STEPS for r in (s, PARTS - 1 - s)]
    return [r for r in given if r not in kept], [r for r in given if r in kept]


def normalise(row, b, local_ref, silu_ref, c_ref, cols_ref, incoming_ref, gain_ref, normed):
    size, inner = local_ref.shape[1:]
    columns = cols_ref.shape[3]
    heads = columns // COLUMNS
    width = inner // heads
    cols = cols_ref[0].reshape(size, columns)
    shape = (FLIP, FLIP)
    group = jnp.where(iota(shape, 0) // width == iota(shape, 1) // width, 1.0, 0.0).astype(BF16)
    scale_f = spread(cols, selector(4, heads, columns, inner))
    scale_b = spread(cols, selector(5, heads, columns, inner))
    for j in range(0, inner, FLIP):
        lanes = slice(j, j + FLIP)
        tiles = range(j // TILE, (j + FLIP) // TILE)
        into_f = jnp.concatenate([incoming_ref[0, 0, t] for t in tiles], axis=1)
        into_b = jnp.concatenate([incoming_ref[1, 0, t] for t in tiles], axis=1)
        y = local_ref[0, :, lanes]
        y = y + scale_f[:, lanes] * dot(c_ref[0, 0], into_f)
        y = y + scale_b[:, lanes] * dot(c_ref[0, 1], into_b)
        y = y * silu_ref[0, :, lanes]
        square = y * y
        high = square.astype(BF16)
        low = (square - high.astype(F32)).astype(BF16)
        mean = (dot(high, group) + dot(low, group)) * (1.0 / width)
        y = y * lax.rsqrt(mean + EPSILON) * gain_ref[:, lanes]
        normed[b, pl.ds(pl.multiple_of(row, size), size), lanes] = y.astype(BF16)


def multiply_out(t, part, outs, normed, straight, mirrored):
    slab = straight[0].shape[1]
    flip = reversal(FLIP)
    for n, block in enumerate((STEPS[t], PARTS - 1 - STEPS[t])):
        mine = [g for g, order in enumerate(ORDERS) if block in slots(order)[part]]
        if not mine:
            continue
        for c in range(0, slab, FLIP):
            at = slab - FLIP - c
            mirrored[:, c : c + FLIP] = dot(straight[1 - n][:, at : at + FLIP], flip).astype(BF16)
        spans = []
        for g in mine:
            if spans and spans[-1][-1] == g - 1:
                spans[-1].append(g)
            else:
                spans.append([g])
        for span in spans:
            begin = GROUPS[span[0]][0]
            at = slice(begin, sum(GROUPS[span[-1]]))
            product = dot(normed[0, at], straight[n][...]) + dot(normed[1, at], mirrored[...])
            for g in span:
                row, rows = GROUPS[g]
                slot = slots(ORDERS[g])[part].index(block) % outs[g].shape[0]
                outs[g][slot] = product[row - begin : row - begin + rows].astype(outs[g].dtype)


def send_kernel(
    place_ref, local_ref, silu_ref, c_ref, cols_ref, incoming_ref, gain_ref, wout_ref, wmir_ref, *rest
):
    outs, normed, mirrored = rest[:3], rest[3], rest[4]
    i = pl.program_id(0)
    size = local_ref.shape[1]
    halves = normed.shape[1] // size
    pre = 2 * halves

    @pl.when(i < pre)
    def _():
        normalise(
            (i % halves) * size, i // halves, local_ref, silu_ref, c_ref, cols_ref, incoming_ref,
            gain_ref, normed,
        )

    for t in range(len(STEPS)):

        @pl.when(i == pre + t)
        def _():
            multiply_out(t, 0, outs, normed, (wout_ref, wmir_ref), mirrored)


def keep_kernel(place_ref, normed_ref, wout_ref, wmir_ref, *rest):
    outs, mirrored = rest[:3], rest[3]
    for t in range(len(STEPS)):

        @pl.when(pl.program_id(0) == t)
        def _():
            multiply_out(t, 1, outs, normed_ref, (wout_ref, wmir_ref), mirrored)


def group_outs(part, dtype, slab, late):
    specs, shapes = [], []
    for order, (_, rows) in zip(ORDERS, GROUPS):
        given = slots(order)[part]
        steps = [t for t, s in enumerate(STEPS) for r in (s, PARTS - 1 - s) if r in given]
        if len(set(steps)) == len(steps):
            spec = pl.BlockSpec((1, rows, slab), lambda i, n: (late(i), 0, 0))
        else:
            spec = pl.BlockSpec(
                (2, rows, slab), lambda i, n, b=steps[0]: (jnp.clip(late(i) - b, 0, 1), 0, 0)
            )
        specs.append(spec)
        shapes.append(jax.ShapeDtypeStruct((PARTS // 2, rows, slab), dtype))
    return specs, shapes


def output(local, gate, c_maps, cols, incoming, gain, w_out):
    tokens, inner = local.shape[1:]
    state = c_maps.shape[3]
    size = 2 * CHUNK
    halves = tokens // size
    pre = 2 * halves
    slab = w_out.shape[1] // PARTS
    place = lax.axis_index("head")[None]
    held = lambda i: jnp.minimum(i, pre - 1)
    late = lambda i: jnp.maximum(i - pre, 0)
    token = lambda i, n: (held(i) // halves, held(i) % halves, 0)
    block = lambda t, n: n[0] ^ (t ^ STEPS[0])
    specs, shapes = group_outs(0, BF16, slab, late)
    *sends, normed = pl.pallas_call(
        send_kernel,
        grid_spec=pltpu.PrefetchScalarGridSpec(
            num_scalar_prefetch=1,
            grid=(pre + len(STEPS),),
            in_specs=[
                pl.BlockSpec((1, size, inner), token),
                pl.BlockSpec((1, size, inner), token),
                pl.BlockSpec((1, 2, size, state), lambda i, n: (held(i) // halves, 0, held(i) % halves, 0)),
                pl.BlockSpec(
                    (1, size // CHUNK, CHUNK, cols.shape[3]),
                    lambda i, n: (held(i) // halves, held(i) % halves, 0, 0),
                ),
                pl.BlockSpec(
                    (2, 1, inner // TILE, state, TILE), lambda i, n: (0, held(i) // halves, 0, 0, 0)
                ),
                pl.BlockSpec((1, inner), lambda i, n: (0, 0)),
                pl.BlockSpec((inner, slab), lambda i, n: (0, block(late(i), n))),
                pl.BlockSpec((inner, slab), lambda i, n: (0, PARTS - 1 - block(late(i), n))),
            ],
            out_specs=specs + [pl.BlockSpec((2, tokens, inner), lambda i, n: (0, 0, 0))],
            scratch_shapes=[pltpu.VMEM((inner, slab), BF16)],
        ),
        out_shape=shapes + [jax.ShapeDtypeStruct((2, tokens, inner), BF16)],
        compiler_params=params(OUTPUT_GRANT),
        cost_estimate=pl.CostEstimate(flops=3 << 30, transcendentals=1 << 20, bytes_accessed=14 << 20),
        name="output_send",
    )(
        place, *streamed(local, gate, c_maps, cols), incoming, gain, *twice(*streamed(w_out))
    )
    specs, shapes = group_outs(1, F32, slab, lambda i: i)
    keeps = pl.pallas_call(
        keep_kernel,
        grid_spec=pltpu.PrefetchScalarGridSpec(
            num_scalar_prefetch=1,
            grid=(len(STEPS),),
            in_specs=[
                pl.BlockSpec((2, tokens, inner), lambda i, n: (0, 0, 0)),
                pl.BlockSpec((inner, slab), lambda i, n: (0, block(i, n))),
                pl.BlockSpec((inner, slab), lambda i, n: (0, PARTS - 1 - block(i, n))),
            ],
            out_specs=specs,
            scratch_shapes=[pltpu.VMEM((inner, slab), BF16)],
        ),
        out_shape=shapes,
        compiler_params=params(OUTPUT_GRANT),
        cost_estimate=pl.CostEstimate(flops=3 << 30, transcendentals=0, bytes_accessed=10 << 20),
        name="output_keep",
    )(place, normed, *twice(*streamed(w_out)))
    return sends, keeps


def reduced(send, keep, order):
    sent, kept = slots(order)
    for n, partner in enumerate(order):
        pairs = [(i, i ^ partner) for i in range(PARTS)]
        arrived = lax.ppermute(send, "head", pairs)
        arrived_as = [r ^ partner for r in sent]

        def total(block):
            return keep[kept.index(block)] + arrived[arrived_as.index(block)].astype(F32)

        if n == len(order) - 1:
            return total(0).astype(BF16)
        following = order[n + 1]
        rest = {0}
        for other in order[n + 2 :]:
            rest |= {k ^ other for k in rest}
        new_kept = [r for r in kept if r in rest]
        new_sent = [r ^ following for r in new_kept]
        send = jnp.stack([total(r).astype(BF16) for r in new_sent])
        keep = jnp.stack([total(r) for r in new_kept])
        sent, kept = new_sent, new_kept


def shards(
    hidden,
    base_ids,
    norm_gain,
    w_gate,
    w_value,
    w_bc,
    w_step,
    conv_value,
    conv_bc,
    step_bias,
    decay_rate,
    skip_gain,
    out_gain,
    w_out,
):
    count = lax.axis_size("ctx")
    up = [(i, i + 1) for i in range(count - 1)]
    down = [(j, i) for i, j in up]
    before = lax.ppermute(hidden[-HALO:], "ctx", up)
    after = lax.ppermute(hidden[:HALO], "ctx", down)
    direct, xf, xb, b_maps, c_maps, cols, rows, enter, final = front(
        hidden, before, after, norm_gain, w_value, w_bc, w_step,
        base_ids.reshape(-1, CHUNK),
        conv_value,
        conv_bc,
        step_bias[None],
        decay_rate[None],
        skip_gain[None],
    )
    state, tile = final.shape[3:]
    sent = lax.all_to_all(final.reshape(count, state, tile), "ctx", 0, 0)
    local = within(direct, xf, xb, b_maps, c_maps, cols, rows, enter)
    sent, local = lax.optimization_barrier((sent, local))
    chained, late_gain = lax.optimization_barrier((chain(sent), norm_gain))
    incoming = lax.all_to_all(chained, "ctx", 0, 0)
    incoming = incoming.reshape(final.shape[:3] + incoming.shape[1:])
    gate = project_gate(hidden, late_gain, w_gate)
    sends, keeps = output(local, gate, c_maps, cols, incoming, out_gain[None], w_out)
    return jnp.concatenate([reduced(*group) for group in zip(sends, keeps, ORDERS)], axis=0)


def solution(mesh):
    return jax.shard_map(
        shards,
        mesh=mesh,
        in_specs=(
            P("ctx", None),
            P("ctx"),
            P(),
            P(None, "head"),
            P(None, "head"),
            P(),
            P(None, "head"),
            P(None, "head"),
            P(),
            P("head"),
            P("head"),
            P("head"),
            P("head"),
            P("head", None),
        ),
        out_specs=P("ctx", "head"),
        check_vma=False,
    )
```

```python
import functools

import jax
import jax.numpy as jnp
from jax import lax
from jax.experimental import pallas as pl
from jax.experimental.pallas import tpu as pltpu
from jax.sharding import PartitionSpec as P

EPSILON = 1e-05
HALO = 8
CHUNK = 128
TILE = 128
FLIP = 256
ROWS = 64
GRANT = 56
OUTPUT_GRANT = 28
BF16 = jnp.bfloat16
F32 = jnp.float32
NT = (((1,), (1,)), ((), ()))
TN = (((0,), (0,)), ((), ()))


def params(megabytes, dims=1):
    return pltpu.CompilerParams(
        dimension_semantics=("arbitrary",) * dims, vmem_limit_bytes=megabytes << 20
    )


def streamed(*arrays):
    return [pltpu.with_memory_space_constraint(x, pltpu.HBM) for x in arrays]


def iota(shape, dim):
    return lax.broadcasted_iota(jnp.int32, shape, dim)


def dot(a, b):
    return jnp.dot(a, b, preferred_element_type=F32)


def reversal(width):
    where = iota((width, width), 0) + iota((width, width), 1) == width - 1
    return jnp.where(where, 1.0, 0.0).astype(BF16)


def spreader(heads, width):
    shape = (heads, heads * width)
    return jnp.where(iota(shape, 1) // width == iota(shape, 0), 1.0, 0.0).astype(BF16)


def selector(group, heads, columns, inner):
    shape = (columns, inner)
    where = iota(shape, 1) // (inner // heads) + group * heads == iota(shape, 0)
    return jnp.where(where, 1.0, 0.0).astype(BF16)


def spread(columns, matrix):
    high = columns.astype(BF16)
    low = (columns - high.astype(F32)).astype(BF16)
    return dot(high, matrix) + dot(low, matrix)


def silu(x):
    half = 0.5 * x
    return half + half * jnp.tanh(half)


def scale_rows(source, begin, gain, xs, squares):
    depth = source.shape[1]
    step = min(source.shape[0], 32)
    for r in range(0, source.shape[0], step):
        x = source[r : r + step, :].astype(F32)
        xs[begin + r : begin + r + step, :] = (x * gain).astype(BF16)
        square = x * x
        partial = square[:, :TILE]
        for c in range(TILE, depth, TILE):
            partial = partial + square[:, c : c + TILE]
        squares[begin + r : begin + r + step, :] += partial


def scale_mirrored(source, begin, gain, xs):
    size, depth = source.shape
    flip = reversal(FLIP)
    step = min(size, 512)
    for i in range(depth // FLIP):
        at = depth - (i + 1) * FLIP
        lanes = slice(i * FLIP, (i + 1) * FLIP)
        for r in range(0, size, step):
            x = dot(source[r : r + step, at : at + FLIP], flip)
            xs[begin + r : begin + r + step, lanes] = (x * gain[:, lanes]).astype(BF16)


def accumulate(xs, acc, weights, splits, first=False):
    part = xs.shape[0] // splits
    depth = weights[0].shape[0]
    for i in range(splits):
        at = slice(i * part, (i + 1) * part)
        total = dot(xs[at, :depth], weights[0][...])
        for j in range(1, len(weights)):
            total = total + dot(xs[at, j * depth : (j + 1) * depth], weights[j][...])
        acc[at, :] = total if first else acc[at, :] + total


def finish_rms(squares, width):
    mean = jnp.sum(squares[...], axis=1, keepdims=True) * (1.0 / width)
    squares[...] = jnp.broadcast_to(lax.rsqrt(mean + EPSILON), squares.shape)


def scale_all(hid, gain, xs, squares, halo=None):
    tokens, depth = hid[0].shape
    rows = xs.shape[0] // 2
    for i in range(2):
        lanes = pl.ds(i * depth, depth)
        mirrored = pl.ds((1 - i) * depth, depth)
        own, other = gain[i][...], gain[1 - i][...]
        scale_rows(hid[i], 0, own, xs.at[:, lanes], squares)
        scale_mirrored(hid[i], rows, other, xs.at[:, mirrored])
        if halo:
            beside = jnp.concatenate([half[i][...].astype(F32) for half in halo], axis=0)
            scale_rows(beside, tokens, own, xs.at[:, lanes], squares)
            scale_mirrored(beside.astype(BF16), rows + tokens, other, xs.at[:, mirrored])


def placed(tokens):
    spans = [(r, r + HALO, TILE) for r in range(0, tokens, TILE)]
    return spans + [(tokens, 0, HALO), (tokens + HALO, tokens + HALO, HALO)]


def multiply_mix(scaled, halo, lanes, wv, wbc, wst, acc_v, acc_b, acc_s, first):
    tokens = scaled.shape[1]
    rows = halo.shape[1] + tokens
    for b in range(2):
        totals = [0.0, 0.0, 0.0]
        for i in range(2):
            x = jnp.concatenate([scaled[b, :, lanes[i]], halo[b, :, lanes[i]]], axis=0)
            totals[0] += dot(x, wv[i][...])
            totals[1] += dot(x, wbc[i][...])
            totals[2] += lax.dot_general(
                wst[i][...], scaled[b, :, lanes[i]], NT, preferred_element_type=F32
            )
        at = slice(b * rows, (b + 1) * rows)
        acc_v[at, :] = totals[0] if first else acc_v[at, :] + totals[0]
        acc_b[at, :] = totals[1] if first else acc_b[at, :] + totals[1]
        acc_s[b] = totals[2] if first else acc_s[b] + totals[2]


def finish_mix(mix, steps, acc_v, acc_b, acc_s, squares):
    heads, tokens = acc_s.shape[1:]
    rows = tokens + 2 * HALO
    inner, maps = acc_v.shape[1], acc_b.shape[1]
    chunks = tokens // CHUNK
    finish_rms(squares, WIDTH)
    spans = [slice(c * CHUNK, (c + 1) * CHUNK) for c in range(chunks)]
    scale = jnp.concatenate([squares[at, :heads] for at in spans], axis=1)
    for b in range(2):
        stack = [acc_s[b, :, at] for at in spans]
        stack.append(jnp.zeros((TILE - chunks * heads, CHUNK), F32))
        steps[b] = jnp.concatenate(stack, axis=0).T[:, : chunks * heads] * scale
        for r, out, size in placed(tokens):
            here = slice(b * rows + r, b * rows + r + size)
            scales = squares[r : r + size, :]
            for c in range(0, inner, TILE):
                mix[b, c // TILE, out : out + size, :] = acc_v[here, c : c + TILE] * scales
            for c in range(0, maps, TILE):
                mix[b, (inner + c) // TILE, out : out + size, :] = acc_b[here, c : c + TILE] * scales


def gate_kernel(*refs):
    hid, gain, wg = (refs[2 * i : 2 * i + 2] for i in range(3))
    gate_ref, acc_g, xs, squares = refs[6:]
    k = pl.program_id(0)
    tokens = hid[0].shape[0]

    @pl.when(k == 0)
    def _():
        for acc in (acc_g, squares):
            acc[...] = jnp.zeros_like(acc)

    scale_all(hid, gain, xs, squares)
    accumulate(xs, acc_g, wg, 2)

    @pl.when(k == pl.num_programs(0) - 1)
    def _():
        finish_rms(squares, WIDTH)
        for b in range(2):
            for r in range(0, tokens, TILE):
                scale = squares[r : r + TILE, :]
                for c in range(0, gate_ref.shape[2], TILE):
                    gate_ref[b, r : r + TILE, c : c + TILE] = silu(
                        acc_g[b * tokens + r : b * tokens + r + TILE, c : c + TILE] * scale
                    ).astype(BF16)


def convolved(source, row, taps):
    half = CONV - 1
    moved = [source[pl.ds(row + HALO + j, ROWS), :] for j in range(-half, half + 1)]
    forward = taps[0:1] * moved[0]
    backward = taps[0:1] * moved[2 * half]
    for o in range(1, CONV):
        forward = forward + taps[o : o + 1] * moved[o]
        backward = backward + taps[o : o + 1] * moved[2 * half - o]
    return silu(forward), silu(backward)


CONV = 4
DEPTH = 512
WIDTH = 4096


PAIRS = 4


def paired(block, index):
    held = lambda k: jnp.minimum(k, PAIRS - 1)
    return [
        pl.BlockSpec(block, lambda k: index(held(k))),
        pl.BlockSpec(block, lambda k: index(2 * PAIRS - 1 - held(k))),
    ]


def across(k):
    return (0, k)


def downward(k):
    return (k, 0)


def project_gate(hidden, norm_gain, w_gate):
    tokens, width = hidden.shape
    inner = w_gate.shape[1]
    return pl.pallas_call(
        gate_kernel,
        grid=(PAIRS,),
        in_specs=paired((tokens, DEPTH), across)
        + paired((1, DEPTH), across)
        + paired((DEPTH, inner), downward),
        out_specs=pl.BlockSpec((2, tokens, inner), lambda k: (0, 0, 0)),
        out_shape=jax.ShapeDtypeStruct((2, tokens, inner), BF16),
        scratch_shapes=[
            pltpu.VMEM((2 * tokens, inner), F32),
            pltpu.VMEM((2 * tokens, 2 * DEPTH), BF16),
            pltpu.VMEM((tokens, TILE), F32),
        ],
        compiler_params=params(GRANT),
        cost_estimate=pl.CostEstimate(
            flops=4 * tokens * width * (inner + FLIP),
            transcendentals=2 * tokens * inner,
            bytes_accessed=12 << 20,
        ),
        name="project_gate",
    )(*twice(*streamed(hidden), norm_gain[None], *streamed(w_gate)))


def twice(*arrays):
    return [x for x in arrays for _ in range(2)]


def thirds(x):
    high = x.astype(BF16)
    rest = x - high.astype(F32)
    middle = rest.astype(BF16)
    return high, middle, (rest - middle.astype(F32)).astype(BF16)


def exact(matrix, x):
    high, middle, low = thirds(x)
    return dot(matrix, high) + dot(matrix, middle) + dot(matrix, low)


def conv_step(
    mix, steps, base_ref, tapv_ref, tapb_ref, bias_ref, rate_ref, skip_ref,
    direct_ref, xf_ref, xb_ref, maps_ref, cmaps_ref, cols_ref, rows_ref, enter_ref, final_ref,
    dt_sc, wf_sc, wb_sc, keep_sc, vf_sc, vb_sc, carry_sc,
):
    tokens, inner = direct_ref.shape[1:]
    heads = bias_ref.shape[1]
    width = inner // heads
    state = maps_ref.shape[3]
    chunks = tokens // CHUNK
    matrix = spreader(heads, width)

    def lanes_of(x):
        return jnp.concatenate([x] * chunks, axis=1)

    raw = steps[...] + lanes_of(bias_ref[...])
    dt = jnp.maximum(raw, 0.0) + jnp.log1p(jnp.exp(-jnp.abs(raw)))
    log_decay = -lanes_of(rate_ref[...]) * dt
    square = (CHUNK, CHUNK)
    lower = jnp.where(iota(square, 0) >= iota(square, 1), 1.0, 0.0).astype(BF16)
    inclusive = exact(lower, log_decay)
    exclusive = inclusive - log_decay
    last = inclusive[CHUNK - 1 : CHUNK]
    pad = jnp.zeros((CHUNK, TILE - chunks * heads), F32)
    turned = [jnp.concatenate([x, pad], axis=1).T for x in (inclusive, exclusive)]
    for c in range(chunks):
        mine = slice(c * heads, (c + 1) * heads)
        for q, x in enumerate(turned):
            rows_ref[0, c, q] = x[mine, :]
        select = selector(c, heads, chunks * heads, inner)
        at = slice(c * CHUNK, (c + 1) * CHUNK)
        dt_sc[at] = spread(dt, select)
        wf_sc[at] = spread(jnp.exp(last - inclusive), select)
        wb_sc[at] = spread(jnp.exp(exclusive), select)
    totals = [last[:, c * heads : (c + 1) * heads] for c in range(chunks)]
    zero = jnp.zeros_like(totals[0])
    before, after = [zero], [zero]
    for c in range(chunks - 1):
        before.append(before[-1] + totals[c])
        after.append(after[-1] + totals[chunks - 1 - c])
    after = after[::-1]
    everything = before[-1] + totals[-1]
    leaving = last - exclusive
    columns = (
        inclusive,
        exclusive,
        jnp.exp(inclusive),
        jnp.exp(leaving),
        jnp.exp(inclusive + jnp.concatenate(before, axis=1)),
        jnp.exp(leaving + jnp.concatenate(after, axis=1)),
    )
    for c in range(chunks):
        mine = slice(c * heads, (c + 1) * heads)
        cols_ref[0, c] = jnp.concatenate([x[:, mine] for x in columns], axis=1)
    chunk_decay = spread(jnp.exp(jnp.concatenate(totals + [zero] * (8 - chunks), axis=0)), matrix)
    sent_totals = jnp.concatenate(
        [dot(x, matrix) for x in thirds(everything)] + [jnp.zeros((16 - 3, inner), F32)], axis=0
    ).astype(BF16)

    keep = jnp.where(base_ref[...] != 4, 1.0, 0.0)
    keep = jnp.concatenate([keep, jnp.zeros((CHUNK - chunks, CHUNK), F32)], axis=0).T
    for c in range(chunks):
        keep_sc[c * CHUNK : (c + 1) * CHUNK] = jnp.broadcast_to(keep[:, c : c + 1], square)
    skip = spread(skip_ref[...], matrix)

    def block(i, carry):
        r = pl.multiple_of(i * ROWS, ROWS)
        here = pl.ds(r, ROWS)
        kept = keep_sc[here, :]
        for c in range(0, inner, TILE):
            lanes = slice(c, c + TILE)
            forward, backward = convolved(mix.at[c // TILE], r, tapv_ref[:, lanes])
            forward = forward * kept
            backward = backward * kept
            direct_ref[0, here, lanes] = skip[:, lanes] * (forward + backward)
            dt_lanes = dt_sc[here, lanes]
            forward = forward * dt_lanes
            backward = backward * dt_lanes
            xf_ref[0, here, lanes] = forward.astype(BF16)
            xb_ref[0, here, lanes] = backward.astype(BF16)
            vf_sc[here, lanes] = (forward * wf_sc[here, lanes]).astype(BF16)
            vb_sc[here, lanes] = (backward * wb_sc[here, lanes]).astype(BF16)
        for n, maps in enumerate((maps_ref, cmaps_ref)):
            taps = tapb_ref[:, n * state : (n + 1) * state]
            forward, backward = convolved(mix.at[inner // TILE + n], r, taps)
            maps[0, 0, here, :] = forward.astype(BF16)
            maps[0, 1, here, :] = backward.astype(BF16)
        return carry

    lax.fori_loop(0, tokens // ROWS, block, 0)

    for direction, moved, order in ((0, vf_sc, range(chunks)), (1, vb_sc, range(chunks - 1, -1, -1))):
        for n, c in enumerate(order):
            at = slice(c * CHUNK, (c + 1) * CHUNK)
            gained = lax.dot_general(
                maps_ref[0, direction, at, :], moved[at, :], TN, preferred_element_type=F32
            )
            if n == 0:
                enter_ref[0, direction, c] = jnp.zeros(enter_ref.shape[3:], BF16)
                carry_sc[...] = gained
            else:
                enter_ref[0, direction, c] = carry_sc[...].astype(BF16)
                carry_sc[...] = carry_sc[...] * chunk_decay[c : c + 1, :] + gained
        for j in range(0, inner, TILE):
            final_ref[direction, 0, j // TILE, :state] = carry_sc[:, j : j + TILE].astype(BF16)
            final_ref[direction, 0, j // TILE, state:] = sent_totals[:, j : j + TILE]


COLUMNS = 6


SMALL = 8
OUTS = 9


def front_kernel(scaled_ref, square_ref, before_ref, after_ref, *rest):
    far, rest = rest[: SMALL + 2], rest[SMALL + 2 :]
    far_outs, rest = rest[:OUTS], rest[OUTS:]
    near, rest = rest[: SMALL + 2], rest[SMALL + 2 :]
    outs, rest = rest[:OUTS], rest[OUTS:]
    small_sem, weight_sem, out_sem, acc_v, acc_b, acc_s, halo, squares, mix, steps = rest[:10]
    gain, wst = near[:2]
    wv, wbc = near[SMALL:]

    fetches = [pltpu.make_async_copy(far[i], near[i], small_sem.at[i]) for i in range(SMALL)]
    blocks = [[pl.ds(j * DEPTH, DEPTH) for j in (p, 2 * PAIRS - 1 - p)] for p in range(PAIRS)]
    loads = [
        [
            pltpu.make_async_copy(
                far[SMALL + n].at[rows, :], near[SMALL + n].at[rows, :], weight_sem.at[p, h, n]
            )
            for h, rows in enumerate(blocks[p])
            for n in range(2)
        ]
        for p in range(PAIRS)
    ]
    for copy in fetches[:2] + [copy for load in loads for copy in load] + fetches[2:]:
        copy.start()
    tokens = scaled_ref.shape[1]
    squares[:tokens] = square_ref[...]
    squares[tokens:] = jnp.zeros_like(squares[tokens:])
    for copy in fetches[:2]:
        copy.wait()
    beside = jnp.concatenate([before_ref[...].astype(F32), after_ref[...].astype(F32)], axis=0)
    scale_rows(beside, 0, gain[...], halo.at[0], squares.at[pl.ds(tokens, 2 * HALO)])
    scale_mirrored(beside.astype(BF16), 0, gain[...], halo.at[1])
    for p in range(PAIRS):
        lanes = blocks[p]
        for copy in loads[p]:
            copy.wait()
        multiply_mix(
            scaled_ref,
            halo,
            lanes,
            [wv.at[at, :] for at in lanes],
            [wbc.at[at, :] for at in lanes],
            [wst.at[:, at] for at in lanes],
            acc_v, acc_b, acc_s, p == 0,
        )
    finish_mix(mix, steps, acc_v, acc_b, acc_s, squares)
    for copy in fetches[2:]:
        copy.wait()
    stores = []
    for b in range(2):
        views = [out.at[b : b + 1] for out in outs[:-1]] + [outs[-1].at[:, b : b + 1]]
        conv_step(mix.at[b], steps.at[b], *near[2:SMALL], *views, *rest[10:])
        for n, (out, far_out) in enumerate(zip(outs, far_outs)):
            at = (slice(None), b) if n == OUTS - 1 else (b,)
            stores.append(pltpu.make_async_copy(out.at[at], far_out.at[at], out_sem.at[b, n]))
            stores[-1].start()
    for copy in stores:
        copy.wait()


def scale_kernel(far_ref, far_gain_ref, scaled_ref, square_ref, hid, gain, hid_sem, gain_sem):
    blocks = [pl.ds(j * DEPTH, DEPTH) for p in range(PAIRS) for j in (p, 2 * PAIRS - 1 - p)]
    fetch = pltpu.make_async_copy(far_gain_ref, gain, gain_sem)
    fetch.start()
    loads = [
        pltpu.make_async_copy(far_ref.at[:, at], hid.at[:, at], hid_sem.at[i])
        for i, at in enumerate(blocks)
    ]
    for copy in loads:
        copy.start()
    square_ref[...] = jnp.zeros_like(square_ref)
    fetch.wait()
    for p in range(PAIRS):
        pair = blocks[2 * p : 2 * p + 2]
        for i in range(2):
            loads[2 * p + i].wait()
            scale_rows(hid.at[:, pair[i]], 0, gain[:, pair[i]], scaled_ref.at[0, :, pair[i]], square_ref)
            scale_mirrored(
                hid.at[:, pair[i]], 0, gain[:, pair[1 - i]], scaled_ref.at[1, :, pair[1 - i]]
            )


def scale(hidden, gain):
    tokens, width = hidden.shape
    outs = pl.pallas_call(
        scale_kernel,
        in_specs=[pl.BlockSpec(memory_space=pltpu.HBM)] * 2,
        out_specs=[pl.BlockSpec(memory_space=pltpu.VMEM)] * 2,
        out_shape=[pltpu.VMEM((2, tokens, width), BF16), pltpu.VMEM((tokens, TILE), F32)],
        scratch_shapes=[
            pltpu.VMEM((tokens, width), BF16),
            pltpu.VMEM((1, width), F32),
            pltpu.SemaphoreType.DMA((2 * PAIRS,)),
            pltpu.SemaphoreType.DMA,
        ],
        compiler_params=pltpu.CompilerParams(vmem_limit_bytes=20 << 20),
        cost_estimate=pl.CostEstimate(flops=2 << 30, transcendentals=0, bytes_accessed=8 << 20),
        name="scale",
    )(*streamed(hidden, gain))
    return [pltpu.with_memory_space_constraint(x, pltpu.VMEM) for x in outs]


def front(
    hidden, before, after, norm_gain, w_value, w_bc, w_step,
    base_ids, conv_value, conv_bc, step_bias, decay_rate, skip_gain,
):
    tokens, width = hidden.shape
    scaled, squares = scale(hidden, norm_gain[None])
    inner, state, heads = w_value.shape[1], w_bc.shape[1] // 2, w_step.shape[1]
    rows = tokens + 2 * HALO
    chunks = tokens // CHUNK
    far = (
        norm_gain[None], w_step.T, base_ids, conv_value, conv_bc, step_bias, decay_rate, skip_gain,
        w_value, w_bc,
    )
    outs = (
        ((2, tokens, inner), F32),
        ((2, tokens, inner), BF16),
        ((2, tokens, inner), BF16),
        ((2, 2, tokens, state), BF16),
        ((2, 2, tokens, state), BF16),
        ((2, chunks, CHUNK, COLUMNS * heads), F32),
        ((2, chunks, 2, heads, CHUNK), F32),
        ((2, 2, chunks, state, inner), BF16),
        ((2, 2, inner // TILE, state + 16, TILE), BF16),
    )
    here = pl.BlockSpec(memory_space=pltpu.VMEM)
    there = pl.BlockSpec(memory_space=pltpu.HBM)
    return pl.pallas_call(
        front_kernel,
        in_specs=[here] * 4 + [there] * len(far),
        out_specs=[there] * OUTS,
        out_shape=[pltpu.HBM(*out) for out in outs],
        scratch_shapes=[pltpu.VMEM(x.shape, x.dtype) for x in far]
        + [pltpu.VMEM(*out) for out in outs]
        + [
            pltpu.SemaphoreType.DMA((SMALL,)),
            pltpu.SemaphoreType.DMA((PAIRS, 2, 2)),
            pltpu.SemaphoreType.DMA((2, OUTS)),
            pltpu.VMEM((2 * rows, inner), F32),
            pltpu.VMEM((2 * rows, 2 * state), F32),
            pltpu.VMEM((2, heads, tokens), F32),
            pltpu.VMEM((2, 2 * HALO, width), BF16),
            pltpu.VMEM((rows, TILE), F32),
            pltpu.VMEM((2, (inner + 2 * state) // TILE, rows, TILE), F32),
            pltpu.VMEM((2, CHUNK, heads * chunks), F32),
            pltpu.VMEM((tokens, inner), F32),
            pltpu.VMEM((tokens, inner), F32),
            pltpu.VMEM((tokens, inner), F32),
            pltpu.VMEM((tokens, TILE), F32),
            pltpu.VMEM((tokens, inner), BF16),
            pltpu.VMEM((tokens, inner), BF16),
            pltpu.VMEM((state, inner), F32),
        ],
        compiler_params=pltpu.CompilerParams(vmem_limit_bytes=44 << 20),
        cost_estimate=pl.CostEstimate(
            flops=4 * rows * width * (inner + 2 * state + FLIP),
            transcendentals=1 << 22,
            bytes_accessed=24 << 20,
        ),
        name="front",
    )(scaled, squares, before, after, *streamed(*far))


def within_kernel(direct_ref, xf_ref, xb_ref, b_ref, c_ref, cols_ref, rows_ref, enter_ref, local_ref):
    heads = rows_ref.shape[3]
    inner = direct_ref.shape[2]
    width = inner // heads
    square = (CHUNK, CHUNK)
    below = iota(square, 0) >= iota(square, 1)
    above = iota(square, 0) <= iota(square, 1)
    scores_f = lax.dot_general(c_ref[0, 0], b_ref[0, 0], NT, preferred_element_type=F32)
    scores_b = lax.dot_general(c_ref[0, 1], b_ref[0, 1], NT, preferred_element_type=F32)
    scores_f = jnp.where(below, scores_f, 0.0)
    scores_b = jnp.where(above, scores_b, 0.0)
    left = iota((CHUNK, TILE), 1) < width
    cols = cols_ref[0, 0]
    across_f = dot(c_ref[0, 0], enter_ref[0, 0, 0]) * spread(
        cols, selector(2, heads, cols.shape[1], inner)
    )
    across_b = dot(c_ref[0, 1], enter_ref[0, 1, 0]) * spread(
        cols, selector(3, heads, cols.shape[1], inner)
    )
    local_ref[0] = direct_ref[0] + across_f + across_b
    for j in range(0, inner, TILE):
        lanes = slice(j, j + TILE)
        values = jnp.concatenate([xf_ref[0, :, lanes], xb_ref[0, :, lanes]], axis=0)
        parts = []
        for h in range(j // width, (j + TILE) // width):
            gap = jnp.where(
                below,
                cols[:, h : h + 1] - rows_ref[0, 0, 0, h : h + 1, :],
                rows_ref[0, 0, 1, h : h + 1, :] - cols[:, heads + h : heads + h + 1],
            )
            decay = jnp.exp(gap)
            weights = jnp.concatenate(
                [(decay * scores_f).astype(BF16), (decay * scores_b).astype(BF16)], axis=1
            )
            parts.append(dot(weights, values))
        local_ref[0, :, lanes] += jnp.where(left, parts[0], parts[1])


def within(direct, xf, xb, b_maps, c_maps, cols, rows, enter):
    tokens, inner = direct.shape[1:]
    state = b_maps.shape[3]
    heads = rows.shape[3]
    chunks = tokens // CHUNK
    token = lambda i: (i // chunks, i % chunks, 0)
    inside = lambda i: (i // chunks, 0, i % chunks, 0)
    return pl.pallas_call(
        within_kernel,
        grid=(2 * chunks,),
        in_specs=[
            pl.BlockSpec((1, CHUNK, inner), token),
            pl.BlockSpec((1, CHUNK, inner), token),
            pl.BlockSpec((1, CHUNK, inner), token),
            pl.BlockSpec((1, 2, CHUNK, state), inside),
            pl.BlockSpec((1, 2, CHUNK, state), inside),
            pl.BlockSpec((1, 1, CHUNK, cols.shape[3]), lambda i: (i // chunks, i % chunks, 0, 0)),
            pl.BlockSpec((1, 1, 2, heads, CHUNK), lambda i: (i // chunks, i % chunks, 0, 0, 0)),
            pl.BlockSpec((1, 2, 1, state, inner), lambda i: (i // chunks, 0, i % chunks, 0, 0)),
        ],
        out_specs=pl.BlockSpec((1, CHUNK, inner), token),
        out_shape=jax.ShapeDtypeStruct((2, tokens, inner), F32),
        compiler_params=params(GRANT),
        cost_estimate=pl.CostEstimate(flops=4 << 30, transcendentals=1 << 22, bytes_accessed=16 << 20),
        name="within",
    )(direct, xf, xb, b_maps, c_maps, cols, rows, enter)


def chain_kernel(states_ref, incoming_ref):
    count = states_ref.shape[0]
    state = incoming_ref.shape[1]
    backward = lax.axis_index("ctx") >= count // 2
    carry = jnp.zeros(incoming_ref.shape[1:], F32)
    for n in range(count):
        at = jnp.where(backward, count - 1 - n, n)
        incoming_ref[at] = carry.astype(incoming_ref.dtype)
        total = jnp.sum(states_ref[at, state:, :].astype(F32), axis=0, keepdims=True)
        carry = carry * jnp.exp(total) + states_ref[at, :state, :].astype(F32)


def chain(states):
    count, rows, tile = states.shape
    return pl.pallas_call(
        chain_kernel,
        out_shape=jax.ShapeDtypeStruct((count, rows - 16, tile), BF16),
        compiler_params=pltpu.CompilerParams(vmem_limit_bytes=16 << 20),
        cost_estimate=pl.CostEstimate(flops=1 << 20, transcendentals=0, bytes_accessed=2 << 20),
        name="chain",
    )(states)


ORDERS = ((2, 6, 1), (6, 1, 2), (1, 2, 6))
GROUPS = ((0, 176), (176, 176), (352, 160))
STEPS = (2, 3, 0, 1)
PARTS = 8


def kept_blocks(order):
    kept = {0}
    for partner in order[1:]:
        kept |= {k ^ partner for k in kept}
    return kept


def slots(order):
    kept = kept_blocks(order)
    given = [r for s in STEPS for r in (s, PARTS - 1 - s)]
    return [r for r in given if r not in kept], [r for r in given if r in kept]


def normalise(row, b, local_ref, silu_ref, c_ref, cols_ref, incoming_ref, gain_ref, normed):
    size, inner = local_ref.shape[1:]
    columns = cols_ref.shape[3]
    heads = columns // COLUMNS
    width = inner // heads
    cols = cols_ref[0].reshape(size, columns)
    shape = (FLIP, FLIP)
    group = jnp.where(iota(shape, 0) // width == iota(shape, 1) // width, 1.0, 0.0).astype(BF16)
    scale_f = spread(cols, selector(4, heads, columns, inner))
    scale_b = spread(cols, selector(5, heads, columns, inner))
    for j in range(0, inner, FLIP):
        lanes = slice(j, j + FLIP)
        tiles = range(j // TILE, (j + FLIP) // TILE)
        into_f = jnp.concatenate([incoming_ref[0, 0, t] for t in tiles], axis=1)
        into_b = jnp.concatenate([incoming_ref[1, 0, t] for t in tiles], axis=1)
        y = local_ref[0, :, lanes]
        y = y + scale_f[:, lanes] * dot(c_ref[0, 0], into_f)
        y = y + scale_b[:, lanes] * dot(c_ref[0, 1], into_b)
        y = y * silu_ref[0, :, lanes].astype(F32)
        square = y * y
        high = square.astype(BF16)
        low = (square - high.astype(F32)).astype(BF16)
        mean = (dot(high, group) + dot(low, group)) * (1.0 / width)
        y = y * lax.rsqrt(mean + EPSILON) * gain_ref[:, lanes]
        normed[b, pl.ds(pl.multiple_of(row, size), size), lanes] = y.astype(BF16)


def multiply_out(t, part, outs, normed, straight, mirrored):
    slab = straight[0].shape[1]
    flip = reversal(FLIP)
    for n, block in enumerate((STEPS[t], PARTS - 1 - STEPS[t])):
        mine = [g for g, order in enumerate(ORDERS) if block in slots(order)[part]]
        if not mine:
            continue
        for c in range(0, slab, FLIP):
            at = slab - FLIP - c
            mirrored[:, c : c + FLIP] = dot(straight[1 - n][:, at : at + FLIP], flip).astype(BF16)
        spans = []
        for g in mine:
            if spans and spans[-1][-1] == g - 1:
                spans[-1].append(g)
            else:
                spans.append([g])
        for span in spans:
            begin = GROUPS[span[0]][0]
            at = slice(begin, sum(GROUPS[span[-1]]))
            product = dot(normed[0, at], straight[n][...]) + dot(normed[1, at], mirrored[...])
            for g in span:
                row, rows = GROUPS[g]
                slot = slots(ORDERS[g])[part].index(block) % outs[g].shape[0]
                outs[g][slot] = product[row - begin : row - begin + rows].astype(outs[g].dtype)


def send_kernel(
    place_ref, local_ref, silu_ref, c_ref, cols_ref, incoming_ref, gain_ref, wout_ref, wmir_ref, *rest
):
    outs, normed, mirrored = rest[:3], rest[3], rest[4]
    i = pl.program_id(0)
    size = local_ref.shape[1]
    halves = normed.shape[1] // size
    pre = 2 * halves

    @pl.when(i < pre)
    def _():
        normalise(
            (i % halves) * size, i // halves, local_ref, silu_ref, c_ref, cols_ref, incoming_ref,
            gain_ref, normed,
        )

    for t in range(len(STEPS)):

        @pl.when(i == pre + t)
        def _():
            multiply_out(t, 0, outs, normed, (wout_ref, wmir_ref), mirrored)


def keep_kernel(place_ref, normed_ref, wout_ref, wmir_ref, *rest):
    outs, mirrored = rest[:3], rest[3]
    for t in range(len(STEPS)):

        @pl.when(pl.program_id(0) == t)
        def _():
            multiply_out(t, 1, outs, normed_ref, (wout_ref, wmir_ref), mirrored)


def group_outs(part, dtype, slab, late):
    specs, shapes = [], []
    for order, (_, rows) in zip(ORDERS, GROUPS):
        given = slots(order)[part]
        steps = [t for t, s in enumerate(STEPS) for r in (s, PARTS - 1 - s) if r in given]
        if len(set(steps)) == len(steps):
            spec = pl.BlockSpec((1, rows, slab), lambda i, n: (late(i), 0, 0))
        else:
            spec = pl.BlockSpec(
                (2, rows, slab), lambda i, n, b=steps[0]: (jnp.clip(late(i) - b, 0, 1), 0, 0)
            )
        specs.append(spec)
        shapes.append(jax.ShapeDtypeStruct((PARTS // 2, rows, slab), dtype))
    return specs, shapes


def output(local, gate, c_maps, cols, incoming, gain, w_out):
    tokens, inner = local.shape[1:]
    state = c_maps.shape[3]
    size = 2 * CHUNK
    halves = tokens // size
    pre = 2 * halves
    slab = w_out.shape[1] // PARTS
    place = lax.axis_index("head")[None]
    held = lambda i: jnp.minimum(i, pre - 1)
    late = lambda i: jnp.maximum(i - pre, 0)
    token = lambda i, n: (held(i) // halves, held(i) % halves, 0)
    block = lambda t, n: n[0] ^ (t ^ STEPS[0])
    specs, shapes = group_outs(0, BF16, slab, late)
    *sends, normed = pl.pallas_call(
        send_kernel,
        grid_spec=pltpu.PrefetchScalarGridSpec(
            num_scalar_prefetch=1,
            grid=(pre + len(STEPS),),
            in_specs=[
                pl.BlockSpec((1, size, inner), token),
                pl.BlockSpec((1, size, inner), token),
                pl.BlockSpec((1, 2, size, state), lambda i, n: (held(i) // halves, 0, held(i) % halves, 0)),
                pl.BlockSpec(
                    (1, size // CHUNK, CHUNK, cols.shape[3]),
                    lambda i, n: (held(i) // halves, held(i) % halves, 0, 0),
                ),
                pl.BlockSpec(
                    (2, 1, inner // TILE, state, TILE), lambda i, n: (0, held(i) // halves, 0, 0, 0)
                ),
                pl.BlockSpec((1, inner), lambda i, n: (0, 0)),
                pl.BlockSpec((inner, slab), lambda i, n: (0, block(late(i), n))),
                pl.BlockSpec((inner, slab), lambda i, n: (0, PARTS - 1 - block(late(i), n))),
            ],
            out_specs=specs + [pl.BlockSpec((2, tokens, inner), lambda i, n: (0, 0, 0))],
            scratch_shapes=[pltpu.VMEM((inner, slab), BF16)],
        ),
        out_shape=shapes + [jax.ShapeDtypeStruct((2, tokens, inner), BF16)],
        compiler_params=params(OUTPUT_GRANT),
        cost_estimate=pl.CostEstimate(flops=3 << 30, transcendentals=1 << 20, bytes_accessed=14 << 20),
        name="output_send",
    )(
        place, *streamed(local, gate, c_maps, cols), incoming, gain, *twice(*streamed(w_out))
    )
    specs, shapes = group_outs(1, F32, slab, lambda i: i)
    keeps = pl.pallas_call(
        keep_kernel,
        grid_spec=pltpu.PrefetchScalarGridSpec(
            num_scalar_prefetch=1,
            grid=(len(STEPS),),
            in_specs=[
                pl.BlockSpec((2, tokens, inner), lambda i, n: (0, 0, 0)),
                pl.BlockSpec((inner, slab), lambda i, n: (0, block(i, n))),
                pl.BlockSpec((inner, slab), lambda i, n: (0, PARTS - 1 - block(i, n))),
            ],
            out_specs=specs,
            scratch_shapes=[pltpu.VMEM((inner, slab), BF16)],
        ),
        out_shape=shapes,
        compiler_params=params(OUTPUT_GRANT),
        cost_estimate=pl.CostEstimate(flops=3 << 30, transcendentals=0, bytes_accessed=10 << 20),
        name="output_keep",
    )(place, normed, *twice(*streamed(w_out)))
    return sends, keeps


def reduced(send, keep, order):
    sent, kept = slots(order)
    for n, partner in enumerate(order):
        pairs = [(i, i ^ partner) for i in range(PARTS)]
        arrived = lax.ppermute(send, "head", pairs)
        arrived_as = [r ^ partner for r in sent]

        def total(block):
            return keep[kept.index(block)] + arrived[arrived_as.index(block)].astype(F32)

        if n == len(order) - 1:
            return total(0).astype(BF16)
        following = order[n + 1]
        rest = {0}
        for other in order[n + 2 :]:
            rest |= {k ^ other for k in rest}
        new_kept = [r for r in kept if r in rest]
        new_sent = [r ^ following for r in new_kept]
        send = jnp.stack([total(r).astype(BF16) for r in new_sent])
        keep = jnp.stack([total(r) for r in new_kept])
        sent, kept = new_sent, new_kept


def shards(
    hidden,
    base_ids,
    norm_gain,
    w_gate,
    w_value,
    w_bc,
    w_step,
    conv_value,
    conv_bc,
    step_bias,
    decay_rate,
    skip_gain,
    out_gain,
    w_out,
):
    count = lax.axis_size("ctx")
    up = [(i, i + 1) for i in range(count - 1)]
    down = [(j, i) for i, j in up]
    before = lax.ppermute(hidden[-HALO:], "ctx", up)
    after = lax.ppermute(hidden[:HALO], "ctx", down)
    direct, xf, xb, b_maps, c_maps, cols, rows, enter, final = front(
        hidden, before, after, norm_gain, w_value, w_bc, w_step,
        base_ids.reshape(-1, CHUNK),
        conv_value,
        conv_bc,
        step_bias[None],
        decay_rate[None],
        skip_gain[None],
    )
    state, tile = final.shape[3:]
    sent = lax.all_to_all(final.reshape(count, state, tile), "ctx", 0, 0)
    local = within(direct, xf, xb, b_maps, c_maps, cols, rows, enter)
    sent, local = lax.optimization_barrier((sent, local))
    chained, late_gain = lax.optimization_barrier((chain(sent), norm_gain))
    incoming = lax.all_to_all(chained, "ctx", 0, 0)
    incoming = incoming.reshape(final.shape[:3] + incoming.shape[1:])
    gate = project_gate(hidden, late_gain, w_gate)
    sends, keeps = output(local, gate, c_maps, cols, incoming, out_gain[None], w_out)
    groups = [reduced(*group) for group in zip(sends, keeps, ORDERS)]
    mixed = jnp.zeros((sum(GROUPS[-1]), groups[0].shape[1]), BF16)
    for (row, _), group in zip(GROUPS, groups):
        mixed = lax.dynamic_update_slice(mixed, group, (row, 0))
    return mixed


def solution(mesh):
    return jax.shard_map(
        shards,
        mesh=mesh,
        in_specs=(
            P("ctx", None),
            P("ctx"),
            P(),
            P(None, "head"),
            P(None, "head"),
            P(),
            P(None, "head"),
            P(None, "head"),
            P(),
            P("head"),
            P("head"),
            P("head"),
            P("head"),
            P("head", None),
        ),
        out_specs=P("ctx", "head"),
        check_vma=False,
    )
```

```python
import functools

import jax
import jax.numpy as jnp
from jax import lax
from jax.experimental import pallas as pl
from jax.experimental.pallas import tpu as pltpu
from jax.sharding import PartitionSpec as P

EPSILON = 1e-05
HALO = 8
CHUNK = 128
TILE = 128
FLIP = 256
ROWS = 64
GRANT = 56
OUTPUT_GRANT = 28
BF16 = jnp.bfloat16
F32 = jnp.float32
NT = (((1,), (1,)), ((), ()))
TN = (((0,), (0,)), ((), ()))


def params(megabytes, dims=1):
    return pltpu.CompilerParams(
        dimension_semantics=("arbitrary",) * dims, vmem_limit_bytes=megabytes << 20
    )


def streamed(*arrays):
    return [pltpu.with_memory_space_constraint(x, pltpu.HBM) for x in arrays]


def iota(shape, dim):
    return lax.broadcasted_iota(jnp.int32, shape, dim)


def dot(a, b):
    return jnp.dot(a, b, preferred_element_type=F32)


def reversal(width):
    where = iota((width, width), 0) + iota((width, width), 1) == width - 1
    return jnp.where(where, 1.0, 0.0).astype(BF16)


def spreader(heads, width):
    shape = (heads, heads * width)
    return jnp.where(iota(shape, 1) // width == iota(shape, 0), 1.0, 0.0).astype(BF16)


def selector(group, heads, columns, inner):
    shape = (columns, inner)
    where = iota(shape, 1) // (inner // heads) + group * heads == iota(shape, 0)
    return jnp.where(where, 1.0, 0.0).astype(BF16)


def spread(columns, matrix):
    high = columns.astype(BF16)
    low = (columns - high.astype(F32)).astype(BF16)
    return dot(high, matrix) + dot(low, matrix)


def silu(x):
    half = 0.5 * x
    return half + half * jnp.tanh(half)


def scale_rows(source, begin, gain, xs, squares):
    depth = source.shape[1]
    step = min(source.shape[0], 32)
    for r in range(0, source.shape[0], step):
        x = source[r : r + step, :].astype(F32)
        xs[begin + r : begin + r + step, :] = (x * gain).astype(BF16)
        square = x * x
        partial = square[:, :TILE]
        for c in range(TILE, depth, TILE):
            partial = partial + square[:, c : c + TILE]
        squares[begin + r : begin + r + step, :] += partial


def scale_mirrored(source, begin, gain, xs):
    size, depth = source.shape
    flip = reversal(FLIP)
    step = min(size, 512)
    for i in range(depth // FLIP):
        at = depth - (i + 1) * FLIP
        lanes = slice(i * FLIP, (i + 1) * FLIP)
        for r in range(0, size, step):
            x = dot(source[r : r + step, at : at + FLIP], flip)
            xs[begin + r : begin + r + step, lanes] = (x * gain[:, lanes]).astype(BF16)


def accumulate(xs, acc, weights, splits, first=False):
    part = xs.shape[0] // splits
    depth = weights[0].shape[0]
    for i in range(splits):
        at = slice(i * part, (i + 1) * part)
        total = dot(xs[at, :depth], weights[0][...])
        for j in range(1, len(weights)):
            total = total + dot(xs[at, j * depth : (j + 1) * depth], weights[j][...])
        acc[at, :] = total if first else acc[at, :] + total


def finish_rms(squares, width):
    mean = jnp.sum(squares[...], axis=1, keepdims=True) * (1.0 / width)
    squares[...] = jnp.broadcast_to(lax.rsqrt(mean + EPSILON), squares.shape)


def scale_all(hid, gain, xs, squares, halo=None):
    tokens, depth = hid[0].shape
    rows = xs.shape[0] // 2
    for i in range(2):
        lanes = pl.ds(i * depth, depth)
        mirrored = pl.ds((1 - i) * depth, depth)
        own, other = gain[i][...], gain[1 - i][...]
        scale_rows(hid[i], 0, own, xs.at[:, lanes], squares)
        scale_mirrored(hid[i], rows, other, xs.at[:, mirrored])
        if halo:
            beside = jnp.concatenate([half[i][...].astype(F32) for half in halo], axis=0)
            scale_rows(beside, tokens, own, xs.at[:, lanes], squares)
            scale_mirrored(beside.astype(BF16), rows + tokens, other, xs.at[:, mirrored])


def placed(tokens):
    spans = [(r, r + HALO, TILE) for r in range(0, tokens, TILE)]
    return spans + [(tokens, 0, HALO), (tokens + HALO, tokens + HALO, HALO)]


def multiply_mix(scaled, halo, lanes, wv, wbc, wst, acc_v, acc_b, acc_s, first):
    tokens = scaled.shape[1]
    rows = halo.shape[1] + tokens
    for b in range(2):
        totals = [0.0, 0.0, 0.0]
        for i in range(2):
            x = jnp.concatenate([scaled[b, :, lanes[i]], halo[b, :, lanes[i]]], axis=0)
            totals[0] += dot(x, wv[i][...])
            totals[1] += dot(x, wbc[i][...])
            totals[2] += lax.dot_general(
                wst[i][...], scaled[b, :, lanes[i]], NT, preferred_element_type=F32
            )
        at = slice(b * rows, (b + 1) * rows)
        acc_v[at, :] = totals[0] if first else acc_v[at, :] + totals[0]
        acc_b[at, :] = totals[1] if first else acc_b[at, :] + totals[1]
        acc_s[b] = totals[2] if first else acc_s[b] + totals[2]


def finish_mix(mix, steps, acc_v, acc_b, acc_s, squares):
    heads, tokens = acc_s.shape[1:]
    rows = tokens + 2 * HALO
    inner, maps = acc_v.shape[1], acc_b.shape[1]
    chunks = tokens // CHUNK
    finish_rms(squares, WIDTH)
    spans = [slice(c * CHUNK, (c + 1) * CHUNK) for c in range(chunks)]
    scale = jnp.concatenate([squares[at, :heads] for at in spans], axis=1)
    for b in range(2):
        stack = [acc_s[b, :, at] for at in spans]
        stack.append(jnp.zeros((TILE - chunks * heads, CHUNK), F32))
        steps[b] = jnp.concatenate(stack, axis=0).T[:, : chunks * heads] * scale
        for r, out, size in placed(tokens):
            here = slice(b * rows + r, b * rows + r + size)
            scales = squares[r : r + size, :]
            for c in range(0, inner, TILE):
                mix[b, c // TILE, out : out + size, :] = acc_v[here, c : c + TILE] * scales
            for c in range(0, maps, TILE):
                mix[b, (inner + c) // TILE, out : out + size, :] = acc_b[here, c : c + TILE] * scales


def gate_kernel(*refs):
    hid, gain, wg = (refs[2 * i : 2 * i + 2] for i in range(3))
    gate_ref, acc_g, xs, squares = refs[6:]
    k = pl.program_id(0)
    tokens = hid[0].shape[0]

    @pl.when(k == 0)
    def _():
        for acc in (acc_g, squares):
            acc[...] = jnp.zeros_like(acc)

    scale_all(hid, gain, xs, squares)
    accumulate(xs, acc_g, wg, 2)

    @pl.when(k == pl.num_programs(0) - 1)
    def _():
        finish_rms(squares, WIDTH)
        for b in range(2):
            for r in range(0, tokens, TILE):
                scale = squares[r : r + TILE, :]
                for c in range(0, gate_ref.shape[2], TILE):
                    gate_ref[b, r : r + TILE, c : c + TILE] = silu(
                        acc_g[b * tokens + r : b * tokens + r + TILE, c : c + TILE] * scale
                    )


def convolved(source, row, taps):
    half = CONV - 1
    moved = [source[pl.ds(row + HALO + j, ROWS), :] for j in range(-half, half + 1)]
    forward = taps[0:1] * moved[0]
    backward = taps[0:1] * moved[2 * half]
    for o in range(1, CONV):
        forward = forward + taps[o : o + 1] * moved[o]
        backward = backward + taps[o : o + 1] * moved[2 * half - o]
    return silu(forward), silu(backward)


CONV = 4
DEPTH = 512
WIDTH = 4096


PAIRS = 4


def paired(block, index):
    held = lambda k: jnp.minimum(k, PAIRS - 1)
    return [
        pl.BlockSpec(block, lambda k: index(held(k))),
        pl.BlockSpec(block, lambda k: index(2 * PAIRS - 1 - held(k))),
    ]


def across(k):
    return (0, k)


def downward(k):
    return (k, 0)


def project_gate(hidden, norm_gain, w_gate):
    tokens, width = hidden.shape
    inner = w_gate.shape[1]
    return pl.pallas_call(
        gate_kernel,
        grid=(PAIRS,),
        in_specs=paired((tokens, DEPTH), across)
        + paired((1, DEPTH), across)
        + paired((DEPTH, inner), downward),
        out_specs=pl.BlockSpec((2, tokens, inner), lambda k: (0, 0, 0)),
        out_shape=jax.ShapeDtypeStruct((2, tokens, inner), F32),
        scratch_shapes=[
            pltpu.VMEM((2 * tokens, inner), F32),
            pltpu.VMEM((2 * tokens, 2 * DEPTH), BF16),
            pltpu.VMEM((tokens, TILE), F32),
        ],
        compiler_params=params(GRANT),
        cost_estimate=pl.CostEstimate(
            flops=4 * tokens * width * (inner + FLIP),
            transcendentals=2 * tokens * inner,
            bytes_accessed=12 << 20,
        ),
        name="project_gate",
    )(*twice(*streamed(hidden), norm_gain[None], *streamed(w_gate)))


def twice(*arrays):
    return [x for x in arrays for _ in range(2)]


def thirds(x):
    high = x.astype(BF16)
    rest = x - high.astype(F32)
    middle = rest.astype(BF16)
    return high, middle, (rest - middle.astype(F32)).astype(BF16)


def exact(matrix, x):
    high, middle, low = thirds(x)
    return dot(matrix, high) + dot(matrix, middle) + dot(matrix, low)


def conv_step(
    mix, steps, base_ref, tapv_ref, tapb_ref, bias_ref, rate_ref, skip_ref,
    direct_ref, xf_ref, xb_ref, maps_ref, cmaps_ref, cols_ref, rows_ref, enter_ref, final_ref,
    dt_sc, wf_sc, wb_sc, keep_sc, vf_sc, vb_sc, carry_sc, flush,
):
    tokens, inner = direct_ref.shape[1:]
    heads = bias_ref.shape[1]
    width = inner // heads
    state = maps_ref.shape[3]
    chunks = tokens // CHUNK
    matrix = spreader(heads, width)

    def lanes_of(x):
        return jnp.concatenate([x] * chunks, axis=1)

    raw = steps[...] + lanes_of(bias_ref[...])
    dt = jnp.maximum(raw, 0.0) + jnp.log1p(jnp.exp(-jnp.abs(raw)))
    log_decay = -lanes_of(rate_ref[...]) * dt
    square = (CHUNK, CHUNK)
    lower = jnp.where(iota(square, 0) >= iota(square, 1), 1.0, 0.0).astype(BF16)
    inclusive = exact(lower, log_decay)
    exclusive = inclusive - log_decay
    last = inclusive[CHUNK - 1 : CHUNK]
    pad = jnp.zeros((CHUNK, TILE - chunks * heads), F32)
    turned = [jnp.concatenate([x, pad], axis=1).T for x in (inclusive, exclusive)]
    for c in range(chunks):
        mine = slice(c * heads, (c + 1) * heads)
        for q, x in enumerate(turned):
            rows_ref[0, c, q] = x[mine, :]
        select = selector(c, heads, chunks * heads, inner)
        at = slice(c * CHUNK, (c + 1) * CHUNK)
        dt_sc[at] = spread(dt, select)
        wf_sc[at] = spread(jnp.exp(last - inclusive), select)
        wb_sc[at] = spread(jnp.exp(exclusive), select)
    totals = [last[:, c * heads : (c + 1) * heads] for c in range(chunks)]
    zero = jnp.zeros_like(totals[0])
    before, after = [zero], [zero]
    for c in range(chunks - 1):
        before.append(before[-1] + totals[c])
        after.append(after[-1] + totals[chunks - 1 - c])
    after = after[::-1]
    everything = before[-1] + totals[-1]
    leaving = last - exclusive
    columns = (
        inclusive,
        exclusive,
        jnp.exp(inclusive),
        jnp.exp(leaving),
        jnp.exp(inclusive + jnp.concatenate(before, axis=1)),
        jnp.exp(leaving + jnp.concatenate(after, axis=1)),
    )
    for c in range(chunks):
        mine = slice(c * heads, (c + 1) * heads)
        cols_ref[0, c] = jnp.concatenate([x[:, mine] for x in columns], axis=1)
    chunk_decay = spread(jnp.exp(jnp.concatenate(totals + [zero] * (8 - chunks), axis=0)), matrix)
    sent_totals = jnp.concatenate(
        [dot(x, matrix) for x in thirds(everything)] + [jnp.zeros((16 - 3, inner), F32)], axis=0
    ).astype(BF16)

    keep = jnp.where(base_ref[...] != 4, 1.0, 0.0)
    keep = jnp.concatenate([keep, jnp.zeros((CHUNK - chunks, CHUNK), F32)], axis=0).T
    for c in range(chunks):
        keep_sc[c * CHUNK : (c + 1) * CHUNK] = jnp.broadcast_to(keep[:, c : c + 1], square)
    skip = spread(skip_ref[...], matrix)

    def block(i, carry):
        r = pl.multiple_of(i * ROWS, ROWS)
        here = pl.ds(r, ROWS)
        kept = keep_sc[here, :]
        for c in range(0, inner, TILE):
            lanes = slice(c, c + TILE)
            forward, backward = convolved(mix.at[c // TILE], r, tapv_ref[:, lanes])
            forward = forward * kept
            backward = backward * kept
            direct_ref[0, here, lanes] = skip[:, lanes] * (forward + backward)
            dt_lanes = dt_sc[here, lanes]
            forward = forward * dt_lanes
            backward = backward * dt_lanes
            xf_ref[0, here, lanes] = forward.astype(BF16)
            xb_ref[0, here, lanes] = backward.astype(BF16)
            vf_sc[here, lanes] = (forward * wf_sc[here, lanes]).astype(BF16)
            vb_sc[here, lanes] = (backward * wb_sc[here, lanes]).astype(BF16)
        for n, maps in enumerate((maps_ref, cmaps_ref)):
            taps = tapb_ref[:, n * state : (n + 1) * state]
            forward, backward = convolved(mix.at[inner // TILE + n], r, taps)
            maps[0, 0, here, :] = forward.astype(BF16)
            maps[0, 1, here, :] = backward.astype(BF16)
        return carry

    lax.fori_loop(0, tokens // ROWS, block, 0)
    flush()

    for direction, moved, order in ((0, vf_sc, range(chunks)), (1, vb_sc, range(chunks - 1, -1, -1))):
        for n, c in enumerate(order):
            at = slice(c * CHUNK, (c + 1) * CHUNK)
            gained = lax.dot_general(
                maps_ref[0, direction, at, :], moved[at, :], TN, preferred_element_type=F32
            )
            if n == 0:
                enter_ref[0, direction, c] = jnp.zeros(enter_ref.shape[3:], BF16)
                carry_sc[...] = gained
            else:
                enter_ref[0, direction, c] = carry_sc[...].astype(BF16)
                carry_sc[...] = carry_sc[...] * chunk_decay[c : c + 1, :] + gained
        for j in range(0, inner, TILE):
            final_ref[direction, 0, j // TILE, :state] = carry_sc[:, j : j + TILE].astype(BF16)
            final_ref[direction, 0, j // TILE, state:] = sent_totals[:, j : j + TILE]


COLUMNS = 6


SMALL = 8
OUTS = 9


def front_kernel(scaled_ref, square_ref, before_ref, after_ref, *rest):
    far, rest = rest[: SMALL + 2], rest[SMALL + 2 :]
    far_outs, rest = rest[:OUTS], rest[OUTS:]
    near, rest = rest[: SMALL + 2], rest[SMALL + 2 :]
    outs, rest = rest[:OUTS], rest[OUTS:]
    small_sem, weight_sem, out_sem, acc_v, acc_b, acc_s, halo, squares, mix, steps = rest[:10]
    gain, wst = near[:2]
    wv, wbc = near[SMALL:]

    fetches = [pltpu.make_async_copy(far[i], near[i], small_sem.at[i]) for i in range(SMALL)]
    blocks = [[pl.ds(j * DEPTH, DEPTH) for j in (p, 2 * PAIRS - 1 - p)] for p in range(PAIRS)]
    loads = [
        [
            pltpu.make_async_copy(
                far[SMALL + n].at[rows, :], near[SMALL + n].at[rows, :], weight_sem.at[p, h, n]
            )
            for h, rows in enumerate(blocks[p])
            for n in range(2)
        ]
        for p in range(PAIRS)
    ]
    for copy in fetches[:2] + [copy for load in loads for copy in load] + fetches[2:]:
        copy.start()
    tokens = scaled_ref.shape[1]
    squares[:tokens] = square_ref[...]
    squares[tokens:] = jnp.zeros_like(squares[tokens:])
    for copy in fetches[:2]:
        copy.wait()
    beside = jnp.concatenate([before_ref[...].astype(F32), after_ref[...].astype(F32)], axis=0)
    scale_rows(beside, 0, gain[...], halo.at[0], squares.at[pl.ds(tokens, 2 * HALO)])
    scale_mirrored(beside.astype(BF16), 0, gain[...], halo.at[1])
    for p in range(PAIRS):
        lanes = blocks[p]
        for copy in loads[p]:
            copy.wait()
        multiply_mix(
            scaled_ref,
            halo,
            lanes,
            [wv.at[at, :] for at in lanes],
            [wbc.at[at, :] for at in lanes],
            [wst.at[:, at] for at in lanes],
            acc_v, acc_b, acc_s, p == 0,
        )
    finish_mix(mix, steps, acc_v, acc_b, acc_s, squares)
    for copy in fetches[2:]:
        copy.wait()
    stores = []

    def store(b, which):
        for n in which:
            at = (slice(None), b) if n == OUTS - 1 else (b,)
            copy = pltpu.make_async_copy(outs[n].at[at], far_outs[n].at[at], out_sem.at[b, n])
            copy.start()
            stores.append(copy)

    for b in range(2):
        views = [out.at[b : b + 1] for out in outs[:-1]] + [outs[-1].at[:, b : b + 1]]
        conv_step(
            mix.at[b], steps.at[b], *near[2:SMALL], *views, *rest[10:],
            functools.partial(store, b, range(OUTS - 2)),
        )
        store(b, range(OUTS - 2, OUTS))
    for copy in stores:
        copy.wait()


def scale_kernel(far_ref, far_gain_ref, scaled_ref, square_ref, hid, gain, hid_sem, gain_sem):
    blocks = [pl.ds(j * DEPTH, DEPTH) for p in range(PAIRS) for j in (p, 2 * PAIRS - 1 - p)]
    fetch = pltpu.make_async_copy(far_gain_ref, gain, gain_sem)
    fetch.start()
    loads = [
        pltpu.make_async_copy(far_ref.at[:, at], hid.at[:, at], hid_sem.at[i])
        for i, at in enumerate(blocks)
    ]
    for copy in loads:
        copy.start()
    square_ref[...] = jnp.zeros_like(square_ref)
    fetch.wait()
    for p in range(PAIRS):
        pair = blocks[2 * p : 2 * p + 2]
        for i in range(2):
            loads[2 * p + i].wait()
            scale_rows(hid.at[:, pair[i]], 0, gain[:, pair[i]], scaled_ref.at[0, :, pair[i]], square_ref)
            scale_mirrored(
                hid.at[:, pair[i]], 0, gain[:, pair[1 - i]], scaled_ref.at[1, :, pair[1 - i]]
            )


def scale(hidden, gain):
    tokens, width = hidden.shape
    outs = pl.pallas_call(
        scale_kernel,
        in_specs=[pl.BlockSpec(memory_space=pltpu.HBM)] * 2,
        out_specs=[pl.BlockSpec(memory_space=pltpu.VMEM)] * 2,
        out_shape=[pltpu.VMEM((2, tokens, width), BF16), pltpu.VMEM((tokens, TILE), F32)],
        scratch_shapes=[
            pltpu.VMEM((tokens, width), BF16),
            pltpu.VMEM((1, width), F32),
            pltpu.SemaphoreType.DMA((2 * PAIRS,)),
            pltpu.SemaphoreType.DMA,
        ],
        compiler_params=pltpu.CompilerParams(vmem_limit_bytes=20 << 20),
        cost_estimate=pl.CostEstimate(flops=2 << 30, transcendentals=0, bytes_accessed=8 << 20),
        name="scale",
    )(*streamed(hidden, gain))
    return [pltpu.with_memory_space_constraint(x, pltpu.VMEM) for x in outs]


def front(
    hidden, before, after, norm_gain, w_value, w_bc, w_step,
    base_ids, conv_value, conv_bc, step_bias, decay_rate, skip_gain,
):
    tokens, width = hidden.shape
    scaled, squares = scale(hidden, norm_gain[None])
    inner, state, heads = w_value.shape[1], w_bc.shape[1] // 2, w_step.shape[1]
    rows = tokens + 2 * HALO
    chunks = tokens // CHUNK
    far = (
        norm_gain[None], w_step.T, base_ids, conv_value, conv_bc, step_bias, decay_rate, skip_gain,
        w_value, w_bc,
    )
    outs = (
        ((2, tokens, inner), F32),
        ((2, tokens, inner), BF16),
        ((2, tokens, inner), BF16),
        ((2, 2, tokens, state), BF16),
        ((2, 2, tokens, state), BF16),
        ((2, chunks, CHUNK, COLUMNS * heads), F32),
        ((2, chunks, 2, heads, CHUNK), F32),
        ((2, 2, chunks, state, inner), BF16),
        ((2, 2, inner // TILE, state + 16, TILE), BF16),
    )
    here = pl.BlockSpec(memory_space=pltpu.VMEM)
    there = pl.BlockSpec(memory_space=pltpu.HBM)
    return pl.pallas_call(
        front_kernel,
        in_specs=[here] * 4 + [there] * len(far),
        out_specs=[there] * OUTS,
        out_shape=[pltpu.HBM(*out) for out in outs],
        scratch_shapes=[pltpu.VMEM(x.shape, x.dtype) for x in far]
        + [pltpu.VMEM(*out) for out in outs]
        + [
            pltpu.SemaphoreType.DMA((SMALL,)),
            pltpu.SemaphoreType.DMA((PAIRS, 2, 2)),
            pltpu.SemaphoreType.DMA((2, OUTS)),
            pltpu.VMEM((2 * rows, inner), F32),
            pltpu.VMEM((2 * rows, 2 * state), F32),
            pltpu.VMEM((2, heads, tokens), F32),
            pltpu.VMEM((2, 2 * HALO, width), BF16),
            pltpu.VMEM((rows, TILE), F32),
            pltpu.VMEM((2, (inner + 2 * state) // TILE, rows, TILE), F32),
            pltpu.VMEM((2, CHUNK, heads * chunks), F32),
            pltpu.VMEM((tokens, inner), F32),
            pltpu.VMEM((tokens, inner), F32),
            pltpu.VMEM((tokens, inner), F32),
            pltpu.VMEM((tokens, TILE), F32),
            pltpu.VMEM((tokens, inner), BF16),
            pltpu.VMEM((tokens, inner), BF16),
            pltpu.VMEM((state, inner), F32),
        ],
        compiler_params=pltpu.CompilerParams(vmem_limit_bytes=44 << 20),
        cost_estimate=pl.CostEstimate(
            flops=4 * rows * width * (inner + 2 * state + FLIP),
            transcendentals=1 << 22,
            bytes_accessed=24 << 20,
        ),
        name="front",
    )(scaled, squares, before, after, *streamed(*far))


def within_kernel(direct_ref, xf_ref, xb_ref, b_ref, c_ref, cols_ref, rows_ref, enter_ref, local_ref):
    heads = rows_ref.shape[3]
    inner = direct_ref.shape[2]
    width = inner // heads
    square = (CHUNK, CHUNK)
    below = iota(square, 0) >= iota(square, 1)
    above = iota(square, 0) <= iota(square, 1)
    scores_f = lax.dot_general(c_ref[0, 0], b_ref[0, 0], NT, preferred_element_type=F32)
    scores_b = lax.dot_general(c_ref[0, 1], b_ref[0, 1], NT, preferred_element_type=F32)
    scores_f = jnp.where(below, scores_f, 0.0)
    scores_b = jnp.where(above, scores_b, 0.0)
    left = iota((CHUNK, TILE), 1) < width
    cols = cols_ref[0, 0]
    across_f = dot(c_ref[0, 0], enter_ref[0, 0, 0]) * spread(
        cols, selector(2, heads, cols.shape[1], inner)
    )
    across_b = dot(c_ref[0, 1], enter_ref[0, 1, 0]) * spread(
        cols, selector(3, heads, cols.shape[1], inner)
    )
    local_ref[0] = direct_ref[0] + across_f + across_b
    for j in range(0, inner, TILE):
        lanes = slice(j, j + TILE)
        values = jnp.concatenate([xf_ref[0, :, lanes], xb_ref[0, :, lanes]], axis=0)
        parts = []
        for h in range(j // width, (j + TILE) // width):
            gap = jnp.where(
                below,
                cols[:, h : h + 1] - rows_ref[0, 0, 0, h : h + 1, :],
                rows_ref[0, 0, 1, h : h + 1, :] - cols[:, heads + h : heads + h + 1],
            )
            decay = jnp.exp(gap)
            weights = jnp.concatenate(
                [(decay * scores_f).astype(BF16), (decay * scores_b).astype(BF16)], axis=1
            )
            parts.append(dot(weights, values))
        local_ref[0, :, lanes] += jnp.where(left, parts[0], parts[1])


def within(direct, xf, xb, b_maps, c_maps, cols, rows, enter):
    tokens, inner = direct.shape[1:]
    state = b_maps.shape[3]
    heads = rows.shape[3]
    chunks = tokens // CHUNK
    token = lambda i: (i // chunks, i % chunks, 0)
    inside = lambda i: (i // chunks, 0, i % chunks, 0)
    return pl.pallas_call(
        within_kernel,
        grid=(2 * chunks,),
        in_specs=[
            pl.BlockSpec((1, CHUNK, inner), token),
            pl.BlockSpec((1, CHUNK, inner), token),
            pl.BlockSpec((1, CHUNK, inner), token),
            pl.BlockSpec((1, 2, CHUNK, state), inside),
            pl.BlockSpec((1, 2, CHUNK, state), inside),
            pl.BlockSpec((1, 1, CHUNK, cols.shape[3]), lambda i: (i // chunks, i % chunks, 0, 0)),
            pl.BlockSpec((1, 1, 2, heads, CHUNK), lambda i: (i // chunks, i % chunks, 0, 0, 0)),
            pl.BlockSpec((1, 2, 1, state, inner), lambda i: (i // chunks, 0, i % chunks, 0, 0)),
        ],
        out_specs=pl.BlockSpec((1, CHUNK, inner), token),
        out_shape=jax.ShapeDtypeStruct((2, tokens, inner), F32),
        compiler_params=params(GRANT),
        cost_estimate=pl.CostEstimate(flops=4 << 30, transcendentals=1 << 22, bytes_accessed=16 << 20),
        name="within",
    )(direct, xf, xb, b_maps, c_maps, cols, rows, enter)


def chain_kernel(states_ref, incoming_ref):
    count = states_ref.shape[0]
    state = incoming_ref.shape[1]
    backward = lax.axis_index("ctx") >= count // 2
    carry = jnp.zeros(incoming_ref.shape[1:], F32)
    for n in range(count):
        at = jnp.where(backward, count - 1 - n, n)
        incoming_ref[at] = carry.astype(incoming_ref.dtype)
        total = jnp.sum(states_ref[at, state:, :].astype(F32), axis=0, keepdims=True)
        carry = carry * jnp.exp(total) + states_ref[at, :state, :].astype(F32)


def chain(states):
    count, rows, tile = states.shape
    return pl.pallas_call(
        chain_kernel,
        out_shape=jax.ShapeDtypeStruct((count, rows - 16, tile), BF16),
        compiler_params=pltpu.CompilerParams(vmem_limit_bytes=16 << 20),
        cost_estimate=pl.CostEstimate(flops=1 << 20, transcendentals=0, bytes_accessed=2 << 20),
        name="chain",
    )(states)


ORDERS = ((2, 6, 1), (6, 1, 2), (1, 2, 6))
GROUPS = ((0, 176), (176, 176), (352, 160))
STEPS = (2, 3, 0, 1)
PARTS = 8


def kept_blocks(order):
    kept = {0}
    for partner in order[1:]:
        kept |= {k ^ partner for k in kept}
    return kept


def slots(order):
    kept = kept_blocks(order)
    given = [r for s in STEPS for r in (s, PARTS - 1 - s)]
    return [r for r in given if r not in kept], [r for r in given if r in kept]


def normalise(row, b, local_ref, silu_ref, c_ref, cols_ref, incoming_ref, gain_ref, normed):
    size, inner = local_ref.shape[1:]
    columns = cols_ref.shape[3]
    heads = columns // COLUMNS
    width = inner // heads
    cols = cols_ref[0].reshape(size, columns)
    shape = (FLIP, FLIP)
    group = jnp.where(iota(shape, 0) // width == iota(shape, 1) // width, 1.0, 0.0).astype(BF16)
    scale_f = spread(cols, selector(4, heads, columns, inner))
    scale_b = spread(cols, selector(5, heads, columns, inner))
    for j in range(0, inner, FLIP):
        lanes = slice(j, j + FLIP)
        tiles = range(j // TILE, (j + FLIP) // TILE)
        into_f = jnp.concatenate([incoming_ref[0, 0, t] for t in tiles], axis=1)
        into_b = jnp.concatenate([incoming_ref[1, 0, t] for t in tiles], axis=1)
        y = local_ref[0, :, lanes]
        y = y + scale_f[:, lanes] * dot(c_ref[0, 0], into_f)
        y = y + scale_b[:, lanes] * dot(c_ref[0, 1], into_b)
        y = y * silu_ref[0, :, lanes]
        square = y * y
        high = square.astype(BF16)
        low = (square - high.astype(F32)).astype(BF16)
        mean = (dot(high, group) + dot(low, group)) * (1.0 / width)
        y = y * lax.rsqrt(mean + EPSILON) * gain_ref[:, lanes]
        normed[b, pl.ds(pl.multiple_of(row, size), size), lanes] = y.astype(BF16)


def multiply_out(t, part, outs, normed, straight, mirrored):
    slab = straight[0].shape[1]
    flip = reversal(FLIP)
    for n, block in enumerate((STEPS[t], PARTS - 1 - STEPS[t])):
        mine = [g for g, order in enumerate(ORDERS) if block in slots(order)[part]]
        if not mine:
            continue
        for c in range(0, slab, FLIP):
            at = slab - FLIP - c
            mirrored[:, c : c + FLIP] = dot(straight[1 - n][:, at : at + FLIP], flip).astype(BF16)
        spans = []
        for g in mine:
            if spans and spans[-1][-1] == g - 1:
                spans[-1].append(g)
            else:
                spans.append([g])
        for span in spans:
            begin = GROUPS[span[0]][0]
            at = slice(begin, sum(GROUPS[span[-1]]))
            product = dot(normed[0, at], straight[n][...]) + dot(normed[1, at], mirrored[...])
            for g in span:
                row, rows = GROUPS[g]
                slot = slots(ORDERS[g])[part].index(block) % outs[g].shape[0]
                outs[g][slot] = product[row - begin : row - begin + rows].astype(outs[g].dtype)


def send_kernel(
    place_ref, local_ref, silu_ref, c_ref, cols_ref, incoming_ref, gain_ref, wout_ref, wmir_ref, *rest
):
    outs, normed, mirrored = rest[:3], rest[3], rest[4]
    i = pl.program_id(0)
    size = local_ref.shape[1]
    halves = normed.shape[1] // size
    pre = 2 * halves

    @pl.when(i < pre)
    def _():
        normalise(
            (i % halves) * size, i // halves, local_ref, silu_ref, c_ref, cols_ref, incoming_ref,
            gain_ref, normed,
        )

    for t in range(len(STEPS)):

        @pl.when(i == pre + t)
        def _():
            multiply_out(t, 0, outs, normed, (wout_ref, wmir_ref), mirrored)


def keep_kernel(place_ref, normed_ref, wout_ref, wmir_ref, *rest):
    outs, mirrored = rest[:3], rest[3]
    for t in range(len(STEPS)):

        @pl.when(pl.program_id(0) == t)
        def _():
            multiply_out(t, 1, outs, normed_ref, (wout_ref, wmir_ref), mirrored)


def group_outs(part, dtype, slab, late):
    specs, shapes = [], []
    for order, (_, rows) in zip(ORDERS, GROUPS):
        given = slots(order)[part]
        steps = [t for t, s in enumerate(STEPS) for r in (s, PARTS - 1 - s) if r in given]
        if len(set(steps)) == len(steps):
            spec = pl.BlockSpec((1, rows, slab), lambda i, n: (late(i), 0, 0))
        else:
            spec = pl.BlockSpec(
                (2, rows, slab), lambda i, n, b=steps[0]: (jnp.clip(late(i) - b, 0, 1), 0, 0)
            )
        specs.append(spec)
        shapes.append(jax.ShapeDtypeStruct((PARTS // 2, rows, slab), dtype))
    return specs, shapes


def output(local, gate, c_maps, cols, incoming, gain, w_out):
    tokens, inner = local.shape[1:]
    state = c_maps.shape[3]
    size = 2 * CHUNK
    halves = tokens // size
    pre = 2 * halves
    slab = w_out.shape[1] // PARTS
    place = lax.axis_index("head")[None]
    held = lambda i: jnp.minimum(i, pre - 1)
    late = lambda i: jnp.maximum(i - pre, 0)
    token = lambda i, n: (held(i) // halves, held(i) % halves, 0)
    block = lambda t, n: n[0] ^ (t ^ STEPS[0])
    specs, shapes = group_outs(0, BF16, slab, late)
    *sends, normed = pl.pallas_call(
        send_kernel,
        grid_spec=pltpu.PrefetchScalarGridSpec(
            num_scalar_prefetch=1,
            grid=(pre + len(STEPS),),
            in_specs=[
                pl.BlockSpec((1, size, inner), token),
                pl.BlockSpec((1, size, inner), token),
                pl.BlockSpec((1, 2, size, state), lambda i, n: (held(i) // halves, 0, held(i) % halves, 0)),
                pl.BlockSpec(
                    (1, size // CHUNK, CHUNK, cols.shape[3]),
                    lambda i, n: (held(i) // halves, held(i) % halves, 0, 0),
                ),
                pl.BlockSpec(
                    (2, 1, inner // TILE, state, TILE), lambda i, n: (0, held(i) // halves, 0, 0, 0)
                ),
                pl.BlockSpec((1, inner), lambda i, n: (0, 0)),
                pl.BlockSpec((inner, slab), lambda i, n: (0, block(late(i), n))),
                pl.BlockSpec((inner, slab), lambda i, n: (0, PARTS - 1 - block(late(i), n))),
            ],
            out_specs=specs + [pl.BlockSpec((2, tokens, inner), lambda i, n: (0, 0, 0))],
            scratch_shapes=[pltpu.VMEM((inner, slab), BF16)],
        ),
        out_shape=shapes + [jax.ShapeDtypeStruct((2, tokens, inner), BF16)],
        compiler_params=params(OUTPUT_GRANT),
        cost_estimate=pl.CostEstimate(flops=3 << 30, transcendentals=1 << 20, bytes_accessed=14 << 20),
        name="output_send",
    )(
        place, *streamed(local, gate, c_maps, cols), incoming, gain, *twice(*streamed(w_out))
    )
    specs, shapes = group_outs(1, F32, slab, lambda i: i)
    keeps = pl.pallas_call(
        keep_kernel,
        grid_spec=pltpu.PrefetchScalarGridSpec(
            num_scalar_prefetch=1,
            grid=(len(STEPS),),
            in_specs=[
                pl.BlockSpec((2, tokens, inner), lambda i, n: (0, 0, 0)),
                pl.BlockSpec((inner, slab), lambda i, n: (0, block(i, n))),
                pl.BlockSpec((inner, slab), lambda i, n: (0, PARTS - 1 - block(i, n))),
            ],
            out_specs=specs,
            scratch_shapes=[pltpu.VMEM((inner, slab), BF16)],
        ),
        out_shape=shapes,
        compiler_params=params(OUTPUT_GRANT),
        cost_estimate=pl.CostEstimate(flops=3 << 30, transcendentals=0, bytes_accessed=10 << 20),
        name="output_keep",
    )(place, normed, *twice(*streamed(w_out)))
    return sends, keeps


def reduced(send, keep, order):
    sent, kept = slots(order)
    for n, partner in enumerate(order):
        pairs = [(i, i ^ partner) for i in range(PARTS)]
        arrived = lax.ppermute(send, "head", pairs)
        arrived_as = [r ^ partner for r in sent]

        def total(block):
            return keep[kept.index(block)] + arrived[arrived_as.index(block)].astype(F32)

        if n == len(order) - 1:
            return total(0).astype(BF16)
        following = order[n + 1]
        rest = {0}
        for other in order[n + 2 :]:
            rest |= {k ^ other for k in rest}
        new_kept = [r for r in kept if r in rest]
        new_sent = [r ^ following for r in new_kept]
        send = jnp.stack([total(r).astype(BF16) for r in new_sent])
        keep = jnp.stack([total(r) for r in new_kept])
        sent, kept = new_sent, new_kept


def shards(
    hidden,
    base_ids,
    norm_gain,
    w_gate,
    w_value,
    w_bc,
    w_step,
    conv_value,
    conv_bc,
    step_bias,
    decay_rate,
    skip_gain,
    out_gain,
    w_out,
):
    count = lax.axis_size("ctx")
    up = [(i, i + 1) for i in range(count - 1)]
    down = [(j, i) for i, j in up]
    before = lax.ppermute(hidden[-HALO:], "ctx", up)
    after = lax.ppermute(hidden[:HALO], "ctx", down)
    direct, xf, xb, b_maps, c_maps, cols, rows, enter, final = front(
        hidden, before, after, norm_gain, w_value, w_bc, w_step,
        base_ids.reshape(-1, CHUNK),
        conv_value,
        conv_bc,
        step_bias[None],
        decay_rate[None],
        skip_gain[None],
    )
    state, tile = final.shape[3:]
    sent = lax.all_to_all(final.reshape(count, state, tile), "ctx", 0, 0)
    local = within(direct, xf, xb, b_maps, c_maps, cols, rows, enter)
    sent, local = lax.optimization_barrier((sent, local))
    chained, late_gain = lax.optimization_barrier((chain(sent), norm_gain))
    incoming = lax.all_to_all(chained, "ctx", 0, 0)
    incoming = incoming.reshape(final.shape[:3] + incoming.shape[1:])
    gate = project_gate(hidden, late_gain, w_gate)
    sends, keeps = output(local, gate, c_maps, cols, incoming, out_gain[None], w_out)
    return jnp.concatenate([reduced(*group) for group in zip(sends, keeps, ORDERS)], axis=0)


def solution(mesh):
    return jax.shard_map(
        shards,
        mesh=mesh,
        in_specs=(
            P("ctx", None),
            P("ctx"),
            P(),
            P(None, "head"),
            P(None, "head"),
            P(),
            P(None, "head"),
            P(None, "head"),
            P(),
            P("head"),
            P("head"),
            P("head"),
            P("head"),
            P("head", None),
        ),
        out_specs=P("ctx", "head"),
        check_vma=False,
    )
```

```python
import functools

import jax
import jax.numpy as jnp
from jax import lax
from jax.experimental import pallas as pl
from jax.experimental.pallas import tpu as pltpu
from jax.sharding import PartitionSpec as P

EPSILON = 1e-05
HALO = 8
CHUNK = 128
TILE = 128
FLIP = 256
ROWS = 64
GRANT = 56
OUTPUT_GRANT = 28
BF16 = jnp.bfloat16
F32 = jnp.float32
NT = (((1,), (1,)), ((), ()))
TN = (((0,), (0,)), ((), ()))


def params(megabytes, dims=1):
    return pltpu.CompilerParams(
        dimension_semantics=("arbitrary",) * dims, vmem_limit_bytes=megabytes << 20
    )


def streamed(*arrays):
    return [pltpu.with_memory_space_constraint(x, pltpu.HBM) for x in arrays]


def iota(shape, dim):
    return lax.broadcasted_iota(jnp.int32, shape, dim)


def dot(a, b):
    return jnp.dot(a, b, preferred_element_type=F32)


def reversal(width):
    where = iota((width, width), 0) + iota((width, width), 1) == width - 1
    return jnp.where(where, 1.0, 0.0).astype(BF16)


def spreader(heads, width):
    shape = (heads, heads * width)
    return jnp.where(iota(shape, 1) // width == iota(shape, 0), 1.0, 0.0).astype(BF16)


def selector(group, heads, columns, inner):
    shape = (columns, inner)
    where = iota(shape, 1) // (inner // heads) + group * heads == iota(shape, 0)
    return jnp.where(where, 1.0, 0.0).astype(BF16)


def spread(columns, matrix):
    high = columns.astype(BF16)
    low = (columns - high.astype(F32)).astype(BF16)
    return dot(high, matrix) + dot(low, matrix)


def silu(x):
    half = 0.5 * x
    return half + half * jnp.tanh(half)


def scale_rows(source, begin, gain, xs, squares):
    depth = source.shape[1]
    step = min(source.shape[0], 32)
    for r in range(0, source.shape[0], step):
        x = source[r : r + step, :].astype(F32)
        xs[begin + r : begin + r + step, :] = (x * gain).astype(BF16)
        square = x * x
        partial = square[:, :TILE]
        for c in range(TILE, depth, TILE):
            partial = partial + square[:, c : c + TILE]
        squares[begin + r : begin + r + step, :] += partial


def scale_mirrored(source, begin, gain, xs):
    size, depth = source.shape
    flip = reversal(FLIP)
    step = min(size, 512)
    for i in range(depth // FLIP):
        at = depth - (i + 1) * FLIP
        lanes = slice(i * FLIP, (i + 1) * FLIP)
        for r in range(0, size, step):
            x = dot(source[r : r + step, at : at + FLIP], flip)
            xs[begin + r : begin + r + step, lanes] = (x * gain[:, lanes]).astype(BF16)


def accumulate(xs, acc, weights, splits, first=False):
    part = xs.shape[0] // splits
    depth = weights[0].shape[0]
    for i in range(splits):
        at = slice(i * part, (i + 1) * part)
        total = dot(xs[at, :depth], weights[0][...])
        for j in range(1, len(weights)):
            total = total + dot(xs[at, j * depth : (j + 1) * depth], weights[j][...])
        acc[at, :] = total if first else acc[at, :] + total


def finish_rms(squares, width):
    mean = jnp.sum(squares[...], axis=1, keepdims=True) * (1.0 / width)
    squares[...] = jnp.broadcast_to(lax.rsqrt(mean + EPSILON), squares.shape)


def scale_all(hid, gain, xs, squares, halo=None):
    tokens, depth = hid[0].shape
    rows = xs.shape[0] // 2
    for i in range(2):
        lanes = pl.ds(i * depth, depth)
        mirrored = pl.ds((1 - i) * depth, depth)
        own, other = gain[i][...], gain[1 - i][...]
        scale_rows(hid[i], 0, own, xs.at[:, lanes], squares)
        scale_mirrored(hid[i], rows, other, xs.at[:, mirrored])
        if halo:
            beside = jnp.concatenate([half[i][...].astype(F32) for half in halo], axis=0)
            scale_rows(beside, tokens, own, xs.at[:, lanes], squares)
            scale_mirrored(beside.astype(BF16), rows + tokens, other, xs.at[:, mirrored])


def placed(tokens):
    spans = [(r, r + HALO, TILE) for r in range(0, tokens, TILE)]
    return spans + [(tokens, 0, HALO), (tokens + HALO, tokens + HALO, HALO)]


def multiply_mix(scaled, halo, lanes, wv, wbc, wst, acc_v, acc_b, acc_s, first):
    tokens = scaled.shape[1]
    rows = halo.shape[1] + tokens
    for b in range(2):
        totals = [0.0, 0.0, 0.0]
        for i in range(2):
            x = jnp.concatenate([scaled[b, :, lanes[i]], halo[b, :, lanes[i]]], axis=0)
            totals[0] += dot(x, wv[i][...])
            totals[1] += dot(x, wbc[i][...])
            totals[2] += lax.dot_general(
                wst[i][...], scaled[b, :, lanes[i]], NT, preferred_element_type=F32
            )
        at = slice(b * rows, (b + 1) * rows)
        acc_v[at, :] = totals[0] if first else acc_v[at, :] + totals[0]
        acc_b[at, :] = totals[1] if first else acc_b[at, :] + totals[1]
        acc_s[b] = totals[2] if first else acc_s[b] + totals[2]


def finish_mix(mix, steps, acc_v, acc_b, acc_s, squares):
    heads, tokens = acc_s.shape[1:]
    rows = tokens + 2 * HALO
    inner, maps = acc_v.shape[1], acc_b.shape[1]
    chunks = tokens // CHUNK
    finish_rms(squares, WIDTH)
    spans = [slice(c * CHUNK, (c + 1) * CHUNK) for c in range(chunks)]
    scale = jnp.concatenate([squares[at, :heads] for at in spans], axis=1)
    for b in range(2):
        stack = [acc_s[b, :, at] for at in spans]
        stack.append(jnp.zeros((TILE - chunks * heads, CHUNK), F32))
        steps[b] = jnp.concatenate(stack, axis=0).T[:, : chunks * heads] * scale
        for r, out, size in placed(tokens):
            here = slice(b * rows + r, b * rows + r + size)
            scales = squares[r : r + size, :]
            for c in range(0, inner, TILE):
                mix[b, c // TILE, out : out + size, :] = acc_v[here, c : c + TILE] * scales
            for c in range(0, maps, TILE):
                mix[b, (inner + c) // TILE, out : out + size, :] = acc_b[here, c : c + TILE] * scales


def gate_kernel(*refs):
    hid, gain, wg = (refs[2 * i : 2 * i + 2] for i in range(3))
    gate_ref, acc_g, xs, squares = refs[6:]
    k = pl.program_id(0)
    tokens = hid[0].shape[0]

    @pl.when(k == 0)
    def _():
        for acc in (acc_g, squares):
            acc[...] = jnp.zeros_like(acc)

    scale_all(hid, gain, xs, squares)
    accumulate(xs, acc_g, wg, 2)

    @pl.when(k == pl.num_programs(0) - 1)
    def _():
        finish_rms(squares, WIDTH)
        for b in range(2):
            for r in range(0, tokens, TILE):
                scale = squares[r : r + TILE, :]
                for c in range(0, gate_ref.shape[2], TILE):
                    gate_ref[b, r : r + TILE, c : c + TILE] = silu(
                        acc_g[b * tokens + r : b * tokens + r + TILE, c : c + TILE] * scale
                    )


def convolved(source, row, taps):
    half = CONV - 1
    moved = [source[pl.ds(row + HALO + j, ROWS), :] for j in range(-half, half + 1)]
    forward = taps[0:1] * moved[0]
    backward = taps[0:1] * moved[2 * half]
    for o in range(1, CONV):
        forward = forward + taps[o : o + 1] * moved[o]
        backward = backward + taps[o : o + 1] * moved[2 * half - o]
    return silu(forward), silu(backward)


CONV = 4
DEPTH = 512
WIDTH = 4096


PAIRS = 4


def paired(block, index):
    held = lambda k: jnp.minimum(k, PAIRS - 1)
    return [
        pl.BlockSpec(block, lambda k: index(held(k))),
        pl.BlockSpec(block, lambda k: index(2 * PAIRS - 1 - held(k))),
    ]


def across(k):
    return (0, k)


def downward(k):
    return (k, 0)


def project_gate(hidden, norm_gain, w_gate):
    tokens, width = hidden.shape
    inner = w_gate.shape[1]
    return pl.pallas_call(
        gate_kernel,
        grid=(PAIRS,),
        in_specs=paired((tokens, DEPTH), across)
        + paired((1, DEPTH), across)
        + paired((DEPTH, inner), downward),
        out_specs=pl.BlockSpec((2, tokens, inner), lambda k: (0, 0, 0)),
        out_shape=jax.ShapeDtypeStruct((2, tokens, inner), F32),
        scratch_shapes=[
            pltpu.VMEM((2 * tokens, inner), F32),
            pltpu.VMEM((2 * tokens, 2 * DEPTH), BF16),
            pltpu.VMEM((tokens, TILE), F32),
        ],
        compiler_params=params(GRANT),
        cost_estimate=pl.CostEstimate(
            flops=4 * tokens * width * (inner + FLIP),
            transcendentals=2 * tokens * inner,
            bytes_accessed=12 << 20,
        ),
        name="project_gate",
    )(*twice(*streamed(hidden), norm_gain[None], *streamed(w_gate)))


def twice(*arrays):
    return [x for x in arrays for _ in range(2)]


def thirds(x):
    high = x.astype(BF16)
    rest = x - high.astype(F32)
    middle = rest.astype(BF16)
    return high, middle, (rest - middle.astype(F32)).astype(BF16)


def exact(matrix, x):
    high, middle, low = thirds(x)
    return dot(matrix, high) + dot(matrix, middle) + dot(matrix, low)


def conv_step(
    mix, steps, base_ref, tapv_ref, tapb_ref, bias_ref, rate_ref, skip_ref,
    direct_ref, xf_ref, xb_ref, maps_ref, cmaps_ref, cols_ref, rows_ref, enter_ref, final_ref,
    dt_sc, wf_sc, wb_sc, keep_sc, vf_sc, vb_sc, carry_sc, flush,
):
    tokens, inner = direct_ref.shape[1:]
    heads = bias_ref.shape[1]
    width = inner // heads
    state = maps_ref.shape[3]
    chunks = tokens // CHUNK
    matrix = spreader(heads, width)

    def lanes_of(x):
        return jnp.concatenate([x] * chunks, axis=1)

    raw = steps[...] + lanes_of(bias_ref[...])
    dt = jnp.maximum(raw, 0.0) + jnp.log1p(jnp.exp(-jnp.abs(raw)))
    log_decay = -lanes_of(rate_ref[...]) * dt
    square = (CHUNK, CHUNK)
    lower = jnp.where(iota(square, 0) >= iota(square, 1), 1.0, 0.0).astype(BF16)
    inclusive = exact(lower, log_decay)
    exclusive = inclusive - log_decay
    last = inclusive[CHUNK - 1 : CHUNK]
    pad = jnp.zeros((CHUNK, TILE - chunks * heads), F32)
    turned = [jnp.concatenate([x, pad], axis=1).T for x in (inclusive, exclusive)]
    for c in range(chunks):
        mine = slice(c * heads, (c + 1) * heads)
        for q, x in enumerate(turned):
            rows_ref[0, c, q] = x[mine, :]
        select = selector(c, heads, chunks * heads, inner)
        at = slice(c * CHUNK, (c + 1) * CHUNK)
        dt_sc[at] = spread(dt, select)
        wf_sc[at] = spread(jnp.exp(last - inclusive), select)
        wb_sc[at] = spread(jnp.exp(exclusive), select)
    totals = [last[:, c * heads : (c + 1) * heads] for c in range(chunks)]
    zero = jnp.zeros_like(totals[0])
    before, after = [zero], [zero]
    for c in range(chunks - 1):
        before.append(before[-1] + totals[c])
        after.append(after[-1] + totals[chunks - 1 - c])
    after = after[::-1]
    everything = before[-1] + totals[-1]
    leaving = last - exclusive
    columns = (
        inclusive,
        exclusive,
        jnp.exp(inclusive),
        jnp.exp(leaving),
        jnp.exp(inclusive + jnp.concatenate(before, axis=1)),
        jnp.exp(leaving + jnp.concatenate(after, axis=1)),
    )
    for c in range(chunks):
        mine = slice(c * heads, (c + 1) * heads)
        cols_ref[0, c] = jnp.concatenate([x[:, mine] for x in columns], axis=1)
    chunk_decay = spread(jnp.exp(jnp.concatenate(totals + [zero] * (8 - chunks), axis=0)), matrix)
    sent_totals = jnp.concatenate(
        [dot(x, matrix) for x in thirds(everything)] + [jnp.zeros((16 - 3, inner), F32)], axis=0
    ).astype(BF16)

    keep = jnp.where(base_ref[...] != 4, 1.0, 0.0)
    keep = jnp.concatenate([keep, jnp.zeros((CHUNK - chunks, CHUNK), F32)], axis=0).T
    for c in range(chunks):
        keep_sc[c * CHUNK : (c + 1) * CHUNK] = jnp.broadcast_to(keep[:, c : c + 1], square)
    skip = spread(skip_ref[...], matrix)

    def block(i, carry):
        r = pl.multiple_of(i * ROWS, ROWS)
        here = pl.ds(r, ROWS)
        kept = keep_sc[here, :]
        for c in range(0, inner, TILE):
            lanes = slice(c, c + TILE)
            forward, backward = convolved(mix.at[c // TILE], r, tapv_ref[:, lanes])
            forward = forward * kept
            backward = backward * kept
            direct_ref[0, here, lanes] = skip[:, lanes] * (forward + backward)
            dt_lanes = dt_sc[here, lanes]
            forward = forward * dt_lanes
            backward = backward * dt_lanes
            xf_ref[0, here, lanes] = forward.astype(BF16)
            xb_ref[0, here, lanes] = backward.astype(BF16)
            vf_sc[here, lanes] = (forward * wf_sc[here, lanes]).astype(BF16)
            vb_sc[here, lanes] = (backward * wb_sc[here, lanes]).astype(BF16)
        for n, maps in enumerate((maps_ref, cmaps_ref)):
            taps = tapb_ref[:, n * state : (n + 1) * state]
            forward, backward = convolved(mix.at[inner // TILE + n], r, taps)
            maps[0, 0, here, :] = forward.astype(BF16)
            maps[0, 1, here, :] = backward.astype(BF16)
        return carry

    lax.fori_loop(0, tokens // ROWS, block, 0)
    flush()

    for direction, moved, order in ((0, vf_sc, range(chunks)), (1, vb_sc, range(chunks - 1, -1, -1))):
        for n, c in enumerate(order):
            at = slice(c * CHUNK, (c + 1) * CHUNK)
            gained = lax.dot_general(
                maps_ref[0, direction, at, :], moved[at, :], TN, preferred_element_type=F32
            )
            if n == 0:
                enter_ref[0, direction, c] = jnp.zeros(enter_ref.shape[3:], BF16)
                carry_sc[...] = gained
            else:
                enter_ref[0, direction, c] = carry_sc[...].astype(BF16)
                carry_sc[...] = carry_sc[...] * chunk_decay[c : c + 1, :] + gained
        for j in range(0, inner, TILE):
            final_ref[direction, 0, j // TILE, :state] = carry_sc[:, j : j + TILE].astype(BF16)
            final_ref[direction, 0, j // TILE, state:] = sent_totals[:, j : j + TILE]


COLUMNS = 6


SMALL = 8
OUTS = 9


def front_kernel(scaled_ref, square_ref, before_ref, after_ref, *rest):
    far, rest = rest[: SMALL + 2], rest[SMALL + 2 :]
    far_outs, rest = rest[:OUTS], rest[OUTS:]
    near, rest = rest[: SMALL + 2], rest[SMALL + 2 :]
    outs, rest = rest[:OUTS], rest[OUTS:]
    small_sem, weight_sem, out_sem, acc_v, acc_b, acc_s, halo, squares, mix, steps = rest[:10]
    gain, wst = near[:2]
    wv, wbc = near[SMALL:]

    fetches = [pltpu.make_async_copy(far[i], near[i], small_sem.at[i]) for i in range(SMALL)]
    blocks = [[pl.ds(j * DEPTH, DEPTH) for j in (p, 2 * PAIRS - 1 - p)] for p in range(PAIRS)]
    loads = [
        [
            pltpu.make_async_copy(
                far[SMALL + n].at[rows, :], near[SMALL + n].at[rows, :], weight_sem.at[p, h, n]
            )
            for h, rows in enumerate(blocks[p])
            for n in range(2)
        ]
        for p in range(PAIRS)
    ]
    for copy in fetches[:2] + [copy for load in loads for copy in load] + fetches[2:]:
        copy.start()
    tokens = scaled_ref.shape[1]
    squares[:tokens] = square_ref[...]
    squares[tokens:] = jnp.zeros_like(squares[tokens:])
    for copy in fetches[:2]:
        copy.wait()
    beside = jnp.concatenate([before_ref[...].astype(F32), after_ref[...].astype(F32)], axis=0)
    scale_rows(beside, 0, gain[...], halo.at[0], squares.at[pl.ds(tokens, 2 * HALO)])
    scale_mirrored(beside.astype(BF16), 0, gain[...], halo.at[1])
    for p in range(PAIRS):
        lanes = blocks[p]
        for copy in loads[p]:
            copy.wait()
        multiply_mix(
            scaled_ref,
            halo,
            lanes,
            [wv.at[at, :] for at in lanes],
            [wbc.at[at, :] for at in lanes],
            [wst.at[:, at] for at in lanes],
            acc_v, acc_b, acc_s, p == 0,
        )
    finish_mix(mix, steps, acc_v, acc_b, acc_s, squares)
    for copy in fetches[2:]:
        copy.wait()
    stores = []

    def store(b, which):
        for n in which:
            at = (slice(None), b) if n == OUTS - 1 else (b,)
            copy = pltpu.make_async_copy(outs[n].at[at], far_outs[n].at[at], out_sem.at[b, n])
            copy.start()
            stores.append(copy)

    for b in range(2):
        views = [out.at[b : b + 1] for out in outs[:-1]] + [outs[-1].at[:, b : b + 1]]
        conv_step(
            mix.at[b], steps.at[b], *near[2:SMALL], *views, *rest[10:],
            functools.partial(store, b, range(OUTS - 2)),
        )
        store(b, range(OUTS - 2, OUTS))
    for copy in stores:
        copy.wait()


def scale_kernel(far_ref, far_gain_ref, scaled_ref, square_ref, hid, gain, hid_sem, gain_sem):
    blocks = [pl.ds(j * DEPTH, DEPTH) for p in range(PAIRS) for j in (p, 2 * PAIRS - 1 - p)]
    fetch = pltpu.make_async_copy(far_gain_ref, gain, gain_sem)
    fetch.start()
    loads = [
        pltpu.make_async_copy(far_ref.at[:, at], hid.at[:, at], hid_sem.at[i])
        for i, at in enumerate(blocks)
    ]
    for copy in loads:
        copy.start()
    square_ref[...] = jnp.zeros_like(square_ref)
    fetch.wait()
    for p in range(PAIRS):
        pair = blocks[2 * p : 2 * p + 2]
        for i in range(2):
            loads[2 * p + i].wait()
            scale_rows(hid.at[:, pair[i]], 0, gain[:, pair[i]], scaled_ref.at[0, :, pair[i]], square_ref)
            scale_mirrored(
                hid.at[:, pair[i]], 0, gain[:, pair[1 - i]], scaled_ref.at[1, :, pair[1 - i]]
            )


def scale(hidden, gain):
    tokens, width = hidden.shape
    outs = pl.pallas_call(
        scale_kernel,
        in_specs=[pl.BlockSpec(memory_space=pltpu.HBM)] * 2,
        out_specs=[pl.BlockSpec(memory_space=pltpu.VMEM)] * 2,
        out_shape=[pltpu.VMEM((2, tokens, width), BF16), pltpu.VMEM((tokens, TILE), F32)],
        scratch_shapes=[
            pltpu.VMEM((tokens, width), BF16),
            pltpu.VMEM((1, width), F32),
            pltpu.SemaphoreType.DMA((2 * PAIRS,)),
            pltpu.SemaphoreType.DMA,
        ],
        compiler_params=pltpu.CompilerParams(vmem_limit_bytes=20 << 20),
        cost_estimate=pl.CostEstimate(flops=2 << 30, transcendentals=0, bytes_accessed=8 << 20),
        name="scale",
    )(*streamed(hidden, gain))
    return [pltpu.with_memory_space_constraint(x, pltpu.VMEM) for x in outs]


def front(
    hidden, before, after, norm_gain, w_value, w_bc, w_step,
    base_ids, conv_value, conv_bc, step_bias, decay_rate, skip_gain,
):
    tokens, width = hidden.shape
    scaled, squares = scale(hidden, norm_gain[None])
    inner, state, heads = w_value.shape[1], w_bc.shape[1] // 2, w_step.shape[1]
    rows = tokens + 2 * HALO
    chunks = tokens // CHUNK
    far = (
        norm_gain[None], w_step.T, base_ids, conv_value, conv_bc, step_bias, decay_rate, skip_gain,
        w_value, w_bc,
    )
    outs = (
        ((2, tokens, inner), F32),
        ((2, tokens, inner), BF16),
        ((2, tokens, inner), BF16),
        ((2, 2, tokens, state), BF16),
        ((2, 2, tokens, state), BF16),
        ((2, chunks, CHUNK, COLUMNS * heads), F32),
        ((2, chunks, 2, heads, CHUNK), F32),
        ((2, 2, chunks, state, inner), BF16),
        ((2, 2, inner // TILE, state + 16, TILE), BF16),
    )
    here = pl.BlockSpec(memory_space=pltpu.VMEM)
    there = pl.BlockSpec(memory_space=pltpu.HBM)
    return pl.pallas_call(
        front_kernel,
        in_specs=[here] * 4 + [there] * len(far),
        out_specs=[there] * OUTS,
        out_shape=[pltpu.HBM(*out) for out in outs],
        scratch_shapes=[pltpu.VMEM(x.shape, x.dtype) for x in far]
        + [pltpu.VMEM(*out) for out in outs]
        + [
            pltpu.SemaphoreType.DMA((SMALL,)),
            pltpu.SemaphoreType.DMA((PAIRS, 2, 2)),
            pltpu.SemaphoreType.DMA((2, OUTS)),
            pltpu.VMEM((2 * rows, inner), F32),
            pltpu.VMEM((2 * rows, 2 * state), F32),
            pltpu.VMEM((2, heads, tokens), F32),
            pltpu.VMEM((2, 2 * HALO, width), BF16),
            pltpu.VMEM((rows, TILE), F32),
            pltpu.VMEM((2, (inner + 2 * state) // TILE, rows, TILE), F32),
            pltpu.VMEM((2, CHUNK, heads * chunks), F32),
            pltpu.VMEM((tokens, inner), F32),
            pltpu.VMEM((tokens, inner), F32),
            pltpu.VMEM((tokens, inner), F32),
            pltpu.VMEM((tokens, TILE), F32),
            pltpu.VMEM((tokens, inner), BF16),
            pltpu.VMEM((tokens, inner), BF16),
            pltpu.VMEM((state, inner), F32),
        ],
        compiler_params=pltpu.CompilerParams(vmem_limit_bytes=44 << 20),
        cost_estimate=pl.CostEstimate(
            flops=4 * rows * width * (inner + 2 * state + FLIP),
            transcendentals=1 << 22,
            bytes_accessed=24 << 20,
        ),
        name="front",
    )(scaled, squares, before, after, *streamed(*far))


def within_kernel(direct_ref, xf_ref, xb_ref, b_ref, c_ref, cols_ref, rows_ref, enter_ref, local_ref):
    heads = rows_ref.shape[3]
    inner = direct_ref.shape[2]
    width = inner // heads
    square = (CHUNK, CHUNK)
    below = iota(square, 0) >= iota(square, 1)
    above = iota(square, 0) <= iota(square, 1)
    scores_f = lax.dot_general(c_ref[0, 0], b_ref[0, 0], NT, preferred_element_type=F32)
    scores_b = lax.dot_general(c_ref[0, 1], b_ref[0, 1], NT, preferred_element_type=F32)
    scores_f = jnp.where(below, scores_f, 0.0)
    scores_b = jnp.where(above, scores_b, 0.0)
    left = iota((CHUNK, TILE), 1) < width
    cols = cols_ref[0, 0]
    across_f = dot(c_ref[0, 0], enter_ref[0, 0, 0]) * spread(
        cols, selector(2, heads, cols.shape[1], inner)
    )
    across_b = dot(c_ref[0, 1], enter_ref[0, 1, 0]) * spread(
        cols, selector(3, heads, cols.shape[1], inner)
    )
    local_ref[0] = direct_ref[0] + across_f + across_b
    for j in range(0, inner, TILE):
        lanes = slice(j, j + TILE)
        values = jnp.concatenate([xf_ref[0, :, lanes], xb_ref[0, :, lanes]], axis=0)
        parts = []
        for h in range(j // width, (j + TILE) // width):
            gap = jnp.where(
                below,
                cols[:, h : h + 1] - rows_ref[0, 0, 0, h : h + 1, :],
                rows_ref[0, 0, 1, h : h + 1, :] - cols[:, heads + h : heads + h + 1],
            )
            decay = jnp.exp(gap)
            weights = jnp.concatenate(
                [(decay * scores_f).astype(BF16), (decay * scores_b).astype(BF16)], axis=1
            )
            parts.append(dot(weights, values))
        local_ref[0, :, lanes] += jnp.where(left, parts[0], parts[1])


def within(direct, xf, xb, b_maps, c_maps, cols, rows, enter):
    tokens, inner = direct.shape[1:]
    state = b_maps.shape[3]
    heads = rows.shape[3]
    chunks = tokens // CHUNK
    token = lambda i: (i // chunks, i % chunks, 0)
    inside = lambda i: (i // chunks, 0, i % chunks, 0)
    return pl.pallas_call(
        within_kernel,
        grid=(2 * chunks,),
        in_specs=[
            pl.BlockSpec((1, CHUNK, inner), token),
            pl.BlockSpec((1, CHUNK, inner), token),
            pl.BlockSpec((1, CHUNK, inner), token),
            pl.BlockSpec((1, 2, CHUNK, state), inside),
            pl.BlockSpec((1, 2, CHUNK, state), inside),
            pl.BlockSpec((1, 1, CHUNK, cols.shape[3]), lambda i: (i // chunks, i % chunks, 0, 0)),
            pl.BlockSpec((1, 1, 2, heads, CHUNK), lambda i: (i // chunks, i % chunks, 0, 0, 0)),
            pl.BlockSpec((1, 2, 1, state, inner), lambda i: (i // chunks, 0, i % chunks, 0, 0)),
        ],
        out_specs=pl.BlockSpec((1, CHUNK, inner), token),
        out_shape=jax.ShapeDtypeStruct((2, tokens, inner), F32),
        compiler_params=params(GRANT),
        cost_estimate=pl.CostEstimate(flops=4 << 30, transcendentals=1 << 22, bytes_accessed=16 << 20),
        name="within",
    )(direct, xf, xb, b_maps, c_maps, cols, rows, enter)


def chain_kernel(states_ref, incoming_ref):
    count = states_ref.shape[0]
    state = incoming_ref.shape[1]
    backward = lax.axis_index("ctx") >= count // 2
    carry = jnp.zeros(incoming_ref.shape[1:], F32)
    for n in range(count):
        at = jnp.where(backward, count - 1 - n, n)
        incoming_ref[at] = carry.astype(incoming_ref.dtype)
        total = jnp.sum(states_ref[at, state:, :].astype(F32), axis=0, keepdims=True)
        carry = carry * jnp.exp(total) + states_ref[at, :state, :].astype(F32)


def chain(states):
    count, rows, tile = states.shape
    return pl.pallas_call(
        chain_kernel,
        out_shape=jax.ShapeDtypeStruct((count, rows - 16, tile), BF16),
        compiler_params=pltpu.CompilerParams(vmem_limit_bytes=16 << 20),
        cost_estimate=pl.CostEstimate(flops=1 << 20, transcendentals=0, bytes_accessed=2 << 20),
        name="chain",
    )(states)


ORDERS = ((2, 6, 1), (6, 1, 2), (1, 2, 6))
GROUPS = ((0, 176), (176, 176), (352, 160))
STEPS = (2, 3, 0, 1)
PARTS = 8


def kept_blocks(order):
    kept = {0}
    for partner in order[1:]:
        kept |= {k ^ partner for k in kept}
    return kept


def slots(order):
    kept = kept_blocks(order)
    given = [r for s in STEPS for r in (s, PARTS - 1 - s)]
    return [r for r in given if r not in kept], [r for r in given if r in kept]


def normalise(row, b, local_ref, silu_ref, c_ref, cols_ref, incoming_ref, gain_ref, normed):
    size, inner = local_ref.shape[1:]
    columns = cols_ref.shape[3]
    heads = columns // COLUMNS
    width = inner // heads
    cols = cols_ref[0].reshape(size, columns)
    shape = (FLIP, FLIP)
    group = jnp.where(iota(shape, 0) // width == iota(shape, 1) // width, 1.0, 0.0).astype(BF16)
    scale_f = spread(cols, selector(4, heads, columns, inner))
    scale_b = spread(cols, selector(5, heads, columns, inner))
    for j in range(0, inner, FLIP):
        lanes = slice(j, j + FLIP)
        tiles = range(j // TILE, (j + FLIP) // TILE)
        into_f = jnp.concatenate([incoming_ref[0, 0, t] for t in tiles], axis=1)
        into_b = jnp.concatenate([incoming_ref[1, 0, t] for t in tiles], axis=1)
        y = local_ref[0, :, lanes]
        y = y + scale_f[:, lanes] * dot(c_ref[0, 0], into_f)
        y = y + scale_b[:, lanes] * dot(c_ref[0, 1], into_b)
        y = y * silu_ref[0, :, lanes]
        square = y * y
        high = square.astype(BF16)
        low = (square - high.astype(F32)).astype(BF16)
        mean = (dot(high, group) + dot(low, group)) * (1.0 / width)
        y = y * lax.rsqrt(mean + EPSILON) * gain_ref[:, lanes]
        normed[b, pl.ds(pl.multiple_of(row, size), size), lanes] = y.astype(BF16)


def multiply_out(t, part, outs, normed, straight, mirrored):
    slab = straight[0].shape[1]
    flip = reversal(FLIP)
    for n, block in enumerate((STEPS[t], PARTS - 1 - STEPS[t])):
        mine = [g for g, order in enumerate(ORDERS) if block in slots(order)[part]]
        if not mine:
            continue
        for c in range(0, slab, FLIP):
            at = slab - FLIP - c
            mirrored[:, c : c + FLIP] = dot(straight[1 - n][:, at : at + FLIP], flip).astype(BF16)
        spans = []
        for g in mine:
            if spans and spans[-1][-1] == g - 1:
                spans[-1].append(g)
            else:
                spans.append([g])
        for span in spans:
            begin = GROUPS[span[0]][0]
            at = slice(begin, sum(GROUPS[span[-1]]))
            product = dot(normed[0, at], straight[n][...]) + dot(normed[1, at], mirrored[...])
            for g in span:
                row, rows = GROUPS[g]
                slot = slots(ORDERS[g])[part].index(block) % outs[g].shape[0]
                outs[g][slot] = product[row - begin : row - begin + rows].astype(outs[g].dtype)


def send_kernel(
    place_ref, local_ref, silu_ref, c_ref, cols_ref, incoming_ref, gain_ref, wout_ref, wmir_ref, *rest
):
    outs, normed, mirrored = rest[:3], rest[3], rest[4]
    i = pl.program_id(0)
    size = local_ref.shape[1]
    halves = normed.shape[1] // size
    pre = 2 * halves

    @pl.when(i < pre)
    def _():
        normalise(
            (i % halves) * size, i // halves, local_ref, silu_ref, c_ref, cols_ref, incoming_ref,
            gain_ref, normed,
        )

    for t in range(len(STEPS)):

        @pl.when(i == pre + t)
        def _():
            multiply_out(t, 0, outs, normed, (wout_ref, wmir_ref), mirrored)


def keep_kernel(place_ref, normed_ref, wout_ref, wmir_ref, *rest):
    outs, mirrored = rest[:3], rest[3]
    for t in range(len(STEPS)):

        @pl.when(pl.program_id(0) == t)
        def _():
            multiply_out(t, 1, outs, normed_ref, (wout_ref, wmir_ref), mirrored)


def group_outs(part, dtype, slab, late):
    specs, shapes = [], []
    for order, (_, rows) in zip(ORDERS, GROUPS):
        given = slots(order)[part]
        steps = [t for t, s in enumerate(STEPS) for r in (s, PARTS - 1 - s) if r in given]
        if len(set(steps)) == len(steps):
            spec = pl.BlockSpec((1, rows, slab), lambda i, n: (late(i), 0, 0))
        else:
            spec = pl.BlockSpec(
                (2, rows, slab), lambda i, n, b=steps[0]: (jnp.clip(late(i) - b, 0, 1), 0, 0)
            )
        specs.append(spec)
        shapes.append(jax.ShapeDtypeStruct((PARTS // 2, rows, slab), dtype))
    return specs, shapes


def output(local, gate, c_maps, cols, incoming, gain, w_out):
    tokens, inner = local.shape[1:]
    state = c_maps.shape[3]
    size = 4 * CHUNK
    halves = tokens // size
    pre = 2 * halves
    slab = w_out.shape[1] // PARTS
    place = lax.axis_index("head")[None]
    held = lambda i: jnp.minimum(i, pre - 1)
    late = lambda i: jnp.maximum(i - pre, 0)
    token = lambda i, n: (held(i) // halves, held(i) % halves, 0)
    block = lambda t, n: n[0] ^ (t ^ STEPS[0])
    specs, shapes = group_outs(0, BF16, slab, late)
    *sends, normed = pl.pallas_call(
        send_kernel,
        grid_spec=pltpu.PrefetchScalarGridSpec(
            num_scalar_prefetch=1,
            grid=(pre + len(STEPS),),
            in_specs=[
                pl.BlockSpec((1, size, inner), token),
                pl.BlockSpec((1, size, inner), token),
                pl.BlockSpec((1, 2, size, state), lambda i, n: (held(i) // halves, 0, held(i) % halves, 0)),
                pl.BlockSpec(
                    (1, size // CHUNK, CHUNK, cols.shape[3]),
                    lambda i, n: (held(i) // halves, held(i) % halves, 0, 0),
                ),
                pl.BlockSpec(
                    (2, 1, inner // TILE, state, TILE), lambda i, n: (0, held(i) // halves, 0, 0, 0)
                ),
                pl.BlockSpec((1, inner), lambda i, n: (0, 0)),
                pl.BlockSpec((inner, slab), lambda i, n: (0, block(late(i), n))),
                pl.BlockSpec((inner, slab), lambda i, n: (0, PARTS - 1 - block(late(i), n))),
            ],
            out_specs=specs + [pl.BlockSpec((2, tokens, inner), lambda i, n: (0, 0, 0))],
            scratch_shapes=[pltpu.VMEM((inner, slab), BF16)],
        ),
        out_shape=shapes + [jax.ShapeDtypeStruct((2, tokens, inner), BF16)],
        compiler_params=params(OUTPUT_GRANT),
        cost_estimate=pl.CostEstimate(flops=3 << 30, transcendentals=1 << 20, bytes_accessed=14 << 20),
        name="output_send",
    )(
        place, *streamed(local, gate, c_maps, cols), incoming, gain, *twice(*streamed(w_out))
    )
    specs, shapes = group_outs(1, F32, slab, lambda i: i)
    keeps = pl.pallas_call(
        keep_kernel,
        grid_spec=pltpu.PrefetchScalarGridSpec(
            num_scalar_prefetch=1,
            grid=(len(STEPS),),
            in_specs=[
                pl.BlockSpec((2, tokens, inner), lambda i, n: (0, 0, 0)),
                pl.BlockSpec((inner, slab), lambda i, n: (0, block(i, n))),
                pl.BlockSpec((inner, slab), lambda i, n: (0, PARTS - 1 - block(i, n))),
            ],
            out_specs=specs,
            scratch_shapes=[pltpu.VMEM((inner, slab), BF16)],
        ),
        out_shape=shapes,
        compiler_params=params(OUTPUT_GRANT),
        cost_estimate=pl.CostEstimate(flops=3 << 30, transcendentals=0, bytes_accessed=10 << 20),
        name="output_keep",
    )(place, normed, *twice(*streamed(w_out)))
    return sends, keeps


def reduced(send, keep, order):
    sent, kept = slots(order)
    for n, partner in enumerate(order):
        pairs = [(i, i ^ partner) for i in range(PARTS)]
        arrived = lax.ppermute(send, "head", pairs)
        arrived_as = [r ^ partner for r in sent]

        def total(block):
            return keep[kept.index(block)] + arrived[arrived_as.index(block)].astype(F32)

        if n == len(order) - 1:
            return total(0).astype(BF16)
        following = order[n + 1]
        rest = {0}
        for other in order[n + 2 :]:
            rest |= {k ^ other for k in rest}
        new_kept = [r for r in kept if r in rest]
        new_sent = [r ^ following for r in new_kept]
        send = jnp.stack([total(r).astype(BF16) for r in new_sent])
        keep = jnp.stack([total(r) for r in new_kept])
        sent, kept = new_sent, new_kept


def shards(
    hidden,
    base_ids,
    norm_gain,
    w_gate,
    w_value,
    w_bc,
    w_step,
    conv_value,
    conv_bc,
    step_bias,
    decay_rate,
    skip_gain,
    out_gain,
    w_out,
):
    count = lax.axis_size("ctx")
    up = [(i, i + 1) for i in range(count - 1)]
    down = [(j, i) for i, j in up]
    before = lax.ppermute(hidden[-HALO:], "ctx", up)
    after = lax.ppermute(hidden[:HALO], "ctx", down)
    direct, xf, xb, b_maps, c_maps, cols, rows, enter, final = front(
        hidden, before, after, norm_gain, w_value, w_bc, w_step,
        base_ids.reshape(-1, CHUNK),
        conv_value,
        conv_bc,
        step_bias[None],
        decay_rate[None],
        skip_gain[None],
    )
    state, tile = final.shape[3:]
    sent = lax.all_to_all(final.reshape(count, state, tile), "ctx", 0, 0)
    local = within(direct, xf, xb, b_maps, c_maps, cols, rows, enter)
    sent, local = lax.optimization_barrier((sent, local))
    chained, late_gain = lax.optimization_barrier((chain(sent), norm_gain))
    incoming = lax.all_to_all(chained, "ctx", 0, 0)
    incoming = incoming.reshape(final.shape[:3] + incoming.shape[1:])
    gate = project_gate(hidden, late_gain, w_gate)
    sends, keeps = output(local, gate, c_maps, cols, incoming, out_gain[None], w_out)
    return jnp.concatenate([reduced(*group) for group in zip(sends, keeps, ORDERS)], axis=0)


def solution(mesh):
    return jax.shard_map(
        shards,
        mesh=mesh,
        in_specs=(
            P("ctx", None),
            P("ctx"),
            P(),
            P(None, "head"),
            P(None, "head"),
            P(),
            P(None, "head"),
            P(None, "head"),
            P(),
            P("head"),
            P("head"),
            P("head"),
            P("head"),
            P("head", None),
        ),
        out_specs=P("ctx", "head"),
        check_vma=False,
    )
```
